512 devices in a mesh: row: 16 (over z), col: 32 (over y, x, core).
Axes of the slice: x: 4, y: 4, z: 16, core: 2. Of those that a mesh axis runs over, the one named last changes fastest.
Arguments:
- new_keys: bfloat16 [1024, 28672], P('col', 'row'), may hold values from -6 to 6
- precision: bfloat16 [28672, 28672], P('row', 'col'), may hold values from -0.03125 to 0.03125
- stored_keys: bfloat16 [32, 256, 28672], P('row', None, 'col'), may hold values from -0.03125 to 0.03125
- pair_batch: int32 [16, 24], replicated, may hold values from 0 to 31, as said below
- pair_count: int32 [16], replicated, may hold values from 8 to 24, as said below
- batch_length: int32 [32], replicated, may hold values from 64 to 256
- batch_slot: int32 [32], replicated, may hold values from 0 to 31, each once
Outputs:
- whitened: bfloat16 [1024, 28672], P('row', 'col')
- intersections: float32 [16, 24, 64, 256], P('row', None, 'col')
The draws below stay inside these ranges and needn't reach their ends.
Inputs may be any that keep to these rules, and one draw needn't show every extreme that they name: `pair_batch`: the ids in one block's row are distinct; ids at places at or beyond the block's count are ignored. `pair_count`: some block lists exactly 24 batches. `batch_slot`: every store slot belongs to exactly one batch.
All inputs are finite; a program needn't handle non-finite values.
Results may differ from the reference program's by a relative error of at most 0.0029.
Values may be sent and summed in bfloat16 or wider, within the bound.
A program may use at most 64 MiB of HBM per device.

```python
import jax
import jax.numpy as jnp
from jax import lax

ORDER = 28672
KB = 64
BK = 256
NBLK = 16
NK = 1024
NB = 32
MAXP = 24
MINP = 8


def draw_pair_batch(key, part):
    scores = jax.random.randint(key, (NBLK, NB), 0, 1 << 20) * NB + jnp.arange(NB, dtype=jnp.int32)[None, :]
    order = jnp.argsort(scores, axis=1, stable=True)
    return order[:, :MAXP].astype(jnp.int32)


def draw_pair_count(key, part):
    counts = jax.random.randint(key, (NBLK,), MINP, MAXP + 1)
    chosen = jax.random.randint(jax.random.fold_in(key, 7), (), 0, NBLK)
    return counts.at[chosen].set(MAXP).astype(jnp.int32)


def with_ends(entries, key, low, top_value):
    shape = entries.shape
    index_at = [jax.random.randint(jax.random.fold_in(key, axis), (), 0, shape[axis]) for axis in range(len(shape))]
    entries = entries.at[tuple(index_at)].set(low)
    longest = shape.index(max(shape))
    index_at[longest] = (index_at[longest] + 1) % shape[longest]
    return entries.at[tuple(index_at)].set(top_value)


def strengthened(entries, stream_key, source, target, blocks, factor):
    owner, partner = [(jnp.arange(entries.shape[axis_at]) // (entries.shape[axis_at] // blocks)).reshape([-1 if axis == axis_at else 1 for axis in range(entries.ndim)]) for axis_at in (source, target)]
    chosen = jax.random.permutation(stream_key, blocks)[partner]
    strong = (owner == chosen) | (owner == (partner + blocks // 2) % blocks)
    return jnp.where(strong, factor * entries, entries)


def steps_of(stream_key, shape, split, smallest, largest):
    def one(position, blocks):
        heights = jax.random.uniform(jax.random.fold_in(jax.random.fold_in(stream_key, 6), position), (blocks,), jnp.float32, smallest / len(split), largest / len(split))
        return jnp.repeat(jnp.exp(heights), shape[position] // blocks).reshape((-1,) + (1,) * (len(shape) - position - 1))

    level = one(*split[0])
    for cut in split[1:]:
        level = level * one(*cut)
    return level


def normal_values(stream_key, dims, scale, limit, cuts=(), held_as=jnp.bfloat16):
    drawn = jax.random.normal(stream_key, dims, jnp.float32) * scale
    if len(cuts) > 0:
        drawn = steps_of(stream_key, dims, cuts, -0.22, 0.18) * drawn
    return jnp.clip(drawn, min=-limit, max=limit).astype(held_as)


def noise_with(own_key, shape, deviation, bound, cuts, heavy, held_as=jnp.bfloat16):
    array = deviation * jax.random.normal(own_key, shape, jnp.float32)
    if cuts:
        array = array * steps_of(own_key, shape, cuts, -0.22, 0.18)
    return jnp.clip(strengthened(array, jax.random.fold_in(own_key, 3), *heavy), -bound, bound).astype(held_as)


def setup_inputs(seed: int = 0) -> dict:
    seeds = jax.random.split(jax.random.key(seed), 8)
    return {
        "new_keys": noise_with(seeds[0], (NK, ORDER), 1.0, 6.0, ((0, 32), (1, 16)), (1, 0, 32, 2.75)),
        "precision": normal_values(seeds[1], (ORDER, ORDER), ORDER ** -0.5, 0.03125, ((0, 16), (1, 32))),
        "stored_keys": normal_values(seeds[2], (NB, BK, ORDER), ORDER ** -0.5, 0.03125, ((0, 16), (2, 32))),
        "pair_batch": draw_pair_batch(jax.random.fold_in(seeds[7], 71), 0),
        "pair_count": draw_pair_count(jax.random.fold_in(seeds[7], 71), 0),
        "batch_length": with_ends(jax.random.randint(seeds[5], (NB,), BK // 4, BK + 1), jax.random.fold_in(seeds[5], 1), BK // 4, BK).astype(jnp.int32),
        "batch_slot": jax.random.permutation(seeds[6], NB).astype(jnp.int32),
    }


def reference(new_keys, precision, stored_keys, pair_batch, pair_count, batch_length, batch_slot):
    whitened = jnp.dot(new_keys, precision, preferred_element_type=jnp.float32).astype(jnp.bfloat16)
    key_slots = jnp.arange(BK, dtype=jnp.int32)

    def one_block(block):
        rows = lax.dynamic_slice_in_dim(whitened, (block * KB).astype(jnp.int32), KB, 0)

        def one_pair(place):
            batch = pair_batch[block, place]
            slot = batch_slot[batch]
            stored = lax.dynamic_index_in_dim(stored_keys, slot, 0, keepdims=False)
            raw = jnp.dot(rows, stored.T, preferred_element_type=jnp.float32)
            keep = (place < pair_count[block]) & (key_slots < batch_length[batch])
            return jnp.where(keep[None, :], raw, jnp.zeros_like(raw))

        return lax.map(one_pair, jnp.arange(MAXP, dtype=jnp.int32))

    intersections = lax.map(one_block, jnp.arange(NBLK, dtype=jnp.int32))
    return whitened, intersections
```

```python
import jax
import jax.numpy as jnp
from jax import lax
from jax.sharding import PartitionSpec as P


def shards(new_keys, precision, stored_keys, pair_batch, pair_count, batch_length, batch_slot):
    row_count = lax.axis_size("row")
    col_count = lax.axis_size("col")
    row_index = lax.axis_index("row")
    total_keys = new_keys.shape[0] * col_count
    block_keys = total_keys // row_count
    part_keys = block_keys // col_count
    local_batches, batch_keys, width = stored_keys.shape
    partial_value = jnp.dot(
        lax.all_gather(new_keys, "col", axis=0, tiled=True),
        precision,
        preferred_element_type=jnp.float32,
    )
    summed = lax.psum_scatter(partial_value, "row", scatter_dimension=0, tiled=True)
    whitened = summed.astype(jnp.bfloat16)
    every_row = lax.all_gather(whitened, "row", axis=0, tiled=True)
    rows = every_row.reshape(row_count, col_count, part_keys, width)
    terms = jnp.einsum("bcid,sjd->csbij", rows, stored_keys, preferred_element_type=jnp.float32)
    mine = lax.psum_scatter(terms, "col", scatter_dimension=0, tiled=True)[0]
    routed = lax.all_to_all(mine, "row", split_axis=1, concat_axis=0, tiled=True)
    table = routed[:, 0]
    listed = pair_batch[row_index]
    slots = batch_slot[listed]
    lengths = batch_length[listed]
    count = pair_count[row_index]
    picked = jnp.take(table, slots, axis=0)
    places = jnp.arange(slots.shape[0], dtype=jnp.int32)
    columns = jnp.arange(batch_keys, dtype=jnp.int32)
    keep = (places < count)[:, None, None] & (columns[None, None, :] < lengths[:, None, None])
    shares = jnp.where(keep, picked, jnp.zeros_like(picked))
    return (whitened, shares[None])


def solution(mesh):
    placed = (P("col", "row"), P("row", "col"), P("row", None, "col"), P(), P(), P(), P())
    return jax.shard_map(
        shards,
        mesh=mesh,
        in_specs=placed,
        out_specs=(P("row", "col"), P("row", None, "col", None)),
        check_vma=False,
    )
```

```python
import functools

import jax
import jax.numpy as jnp
from jax import lax
from jax.experimental import pallas as pl
from jax.experimental.pallas import tpu as pltpu
from jax.sharding import PartitionSpec as P


def _exchange_kernel(axis, other, n, gather, x_ref, out_ref, send_sems, recv_sems):
    me = lax.axis_index(axis)
    mine = lax.axis_index(other)

    def at(peer):
        return (peer, mine) if axis == "row" else (mine, peer)

    barrier = pltpu.get_barrier_semaphore()
    for d in range(1, n):
        peer = lax.rem(me + d, n)
        pl.semaphore_signal(barrier, inc=1, device_id=at(peer), device_id_type=pl.DeviceIdType.MESH)
    pl.semaphore_wait(barrier, n - 1)
    copies = []
    for d in range(1, n):
        peer = lax.rem(me + d, n)
        src = x_ref if gather else x_ref.at[peer]
        copy = pltpu.make_async_remote_copy(
            src_ref=src, dst_ref=out_ref.at[me], send_sem=send_sems.at[d], recv_sem=recv_sems.at[d],
            device_id=at(peer), device_id_type=pl.DeviceIdType.MESH)
        copy.start()
        copies.append(copy)
    if gather:
        out_ref[me] = x_ref[...]
    else:
        out_ref[me] = x_ref[me]
    for d in range(1, n):
        copies[d - 1].wait_send()
        source = lax.rem(me + n - d, n)
        src = x_ref if gather else x_ref.at[source]
        incoming = pltpu.make_async_remote_copy(
            src_ref=src, dst_ref=out_ref.at[source], send_sem=send_sems.at[d], recv_sem=recv_sems.at[d],
            device_id=at(source), device_id_type=pl.DeviceIdType.MESH)
        incoming.wait_recv()


def exchange(x, axis, other, n, gather, collective_id):
    block = x.shape if gather else x.shape[1:]
    return pl.pallas_call(
        functools.partial(_exchange_kernel, axis, other, n, gather),
        out_shape=jax.ShapeDtypeStruct((n,) + tuple(block), x.dtype),
        in_specs=[pl.BlockSpec(memory_space=pltpu.VMEM)],
        out_specs=pl.BlockSpec(memory_space=pltpu.VMEM),
        scratch_shapes=[pltpu.SemaphoreType.DMA((n,)), pltpu.SemaphoreType.DMA((n,))],
        compiler_params=pltpu.CompilerParams(collective_id=collective_id, has_side_effects=True),
    )(x)


def shards(new_keys, precision, stored_keys, pair_batch, pair_count, batch_length, batch_slot):
    row_count = lax.axis_size("row")
    col_count = lax.axis_size("col")
    row_index = lax.axis_index("row")
    total_keys = new_keys.shape[0] * col_count
    block_keys = total_keys // row_count
    part_keys = block_keys // col_count
    local_batches, batch_keys, width = stored_keys.shape
    gathered = exchange(new_keys, "col", "row", col_count, True, 0)
    partial_value = jnp.dot(
        gathered.reshape(total_keys, new_keys.shape[1]),
        precision,
        preferred_element_type=jnp.float32,
    )
    summed = lax.psum_scatter(partial_value, "row", scatter_dimension=0, tiled=True)
    whitened = summed.astype(jnp.bfloat16)
    every_row = lax.all_gather(whitened, "row", axis=0, tiled=True)
    rows = every_row.reshape(row_count, col_count, part_keys, width)
    terms = jnp.einsum("bcid,sjd->csbij", rows, stored_keys, preferred_element_type=jnp.float32)
    terms = terms.reshape(col_count, local_batches * row_count * part_keys, batch_keys)
    mine = exchange(terms, "col", "row", col_count, False, 1).sum(0)
    mine = mine.reshape(local_batches, row_count, part_keys, batch_keys).transpose(1, 0, 2, 3)
    mine = mine.reshape(row_count, local_batches * part_keys, batch_keys)
    routed = exchange(mine, "row", "col", row_count, False, 2)
    table = routed.reshape(row_count * local_batches, part_keys, batch_keys)
    listed = pair_batch[row_index]
    slots = batch_slot[listed]
    lengths = batch_length[listed]
    count = pair_count[row_index]
    picked = jnp.take(table, slots, axis=0)
    places = jnp.arange(slots.shape[0], dtype=jnp.int32)
    columns = jnp.arange(batch_keys, dtype=jnp.int32)
    keep = (places < count)[:, None, None] & (columns[None, None, :] < lengths[:, None, None])
    shares = jnp.where(keep, picked, jnp.zeros_like(picked))
    return (whitened, shares[None])


def solution(mesh):
    placed = (P("col", "row"), P("row", "col"), P("row", None, "col"), P(), P(), P(), P())
    return jax.shard_map(
        shards,
        mesh=mesh,
        in_specs=placed,
        out_specs=(P("row", "col"), P("row", None, "col", None)),
        check_vma=False,
    )
```

```python
import functools

import jax
import jax.numpy as jnp
from jax import lax
from jax.experimental import pallas as pl
from jax.experimental.pallas import tpu as pltpu
from jax.sharding import PartitionSpec as P


def _exchange_kernel(axis, other, n, gather, x_ref, out_ref, send_sems, recv_sems):
    me = lax.axis_index(axis)
    mine = lax.axis_index(other)

    def at(peer):
        return (peer, mine) if axis == "row" else (mine, peer)

    barrier = pltpu.get_barrier_semaphore()
    for d in range(1, n):
        peer = lax.rem(me + d, n)
        pl.semaphore_signal(barrier, inc=1, device_id=at(peer), device_id_type=pl.DeviceIdType.MESH)
    pl.semaphore_wait(barrier, n - 1)
    copies = []
    for d in range(1, n):
        peer = lax.rem(me + d, n)
        src = x_ref if gather else x_ref.at[peer]
        copy = pltpu.make_async_remote_copy(
            src_ref=src, dst_ref=out_ref.at[me], send_sem=send_sems.at[d], recv_sem=recv_sems.at[d],
            device_id=at(peer), device_id_type=pl.DeviceIdType.MESH)
        copy.start()
        copies.append(copy)
    if gather:
        out_ref[me] = x_ref[...]
    else:
        out_ref[me] = x_ref[me]
    for d in range(1, n):
        copies[d - 1].wait_send()
        source = lax.rem(me + n - d, n)
        src = x_ref if gather else x_ref.at[source]
        incoming = pltpu.make_async_remote_copy(
            src_ref=src, dst_ref=out_ref.at[source], send_sem=send_sems.at[d], recv_sem=recv_sems.at[d],
            device_id=at(source), device_id_type=pl.DeviceIdType.MESH)
        incoming.wait_recv()


def exchange(x, axis, other, n, gather, collective_id):
    block = x.shape if gather else x.shape[1:]
    return pl.pallas_call(
        functools.partial(_exchange_kernel, axis, other, n, gather),
        out_shape=jax.ShapeDtypeStruct((n,) + tuple(block), x.dtype),
        in_specs=[pl.BlockSpec(memory_space=pltpu.VMEM)],
        out_specs=pl.BlockSpec(memory_space=pltpu.VMEM),
        scratch_shapes=[pltpu.SemaphoreType.DMA((n,)), pltpu.SemaphoreType.DMA((n,))],
        compiler_params=pltpu.CompilerParams(collective_id=collective_id, has_side_effects=True),
    )(x)


def _ring_kernel(n, partial_ref, out_ref, recv_r, recv_l, acc_r, acc_l, rs_send, rs_recv, ag_send, ag_recv):
    me = lax.axis_index("row")
    mine = lax.axis_index("col")
    right = lax.rem(me + 1, n)
    left = lax.rem(me + n - 1, n)
    steps_r = n // 2
    steps_l = n - 1 - steps_r
    barrier = pltpu.get_barrier_semaphore()
    for peer in (left, right):
        pl.semaphore_signal(barrier, inc=1, device_id=(peer, mine), device_id_type=pl.DeviceIdType.MESH)
    pl.semaphore_wait(barrier, 2)

    def send(src, dst, sems, k, peer):
        copy = pltpu.make_async_remote_copy(
            src_ref=src, dst_ref=dst, send_sem=sems.at[k], recv_sem=sems.at[k + n],
            device_id=(peer, mine), device_id_type=pl.DeviceIdType.MESH)
        copy.start()
        return copy

    sent = []
    for s in range(steps_r):
        d_r = lax.rem(me + steps_r - s, n)
        if s == 0:
            src = partial_ref.at[d_r]
        else:
            sent_r[s - 1].wait_recv()
            acc_r[s - 1] = recv_r[s - 1] + partial_ref[d_r]
            src = acc_r.at[s - 1]
        c = send(src, recv_r.at[s], rs_send, s, right)
        sent.append(c)
        sent_r = sent_r + [c] if s else [c]
        if s < steps_l:
            d_l = lax.rem(me + n - steps_l + s, n)
            if s == 0:
                src = partial_ref.at[d_l]
            else:
                sent_l[s - 1].wait_recv()
                acc_l[s - 1] = recv_l[s - 1] + partial_ref[d_l]
                src = acc_l.at[s - 1]
            c = send(src, recv_l.at[s], rs_send, n // 2 + s, left)
            sent.append(c)
            sent_l = sent_l + [c] if s else [c]
    sent_r[-1].wait_recv()
    sent_l[-1].wait_recv()
    total = partial_ref[me] + recv_r[steps_r - 1] + recv_l[steps_l - 1]
    out_ref[me] = total.astype(out_ref.dtype)

    for t in range(steps_r):
        b_r = lax.rem(me + n - t, n)
        if t:
            got_r[t - 1].wait_recv()
        c = send(out_ref.at[b_r], out_ref.at[b_r], ag_send, t, right)
        sent.append(c)
        got_r = got_r + [c] if t else [c]
        if t < steps_l:
            b_l = lax.rem(me + t, n)
            if t:
                got_l[t - 1].wait_recv()
            c = send(out_ref.at[b_l], out_ref.at[b_l], ag_send, n // 2 + t, left)
            sent.append(c)
            got_l = got_l + [c] if t else [c]
    got_r[-1].wait_recv()
    got_l[-1].wait_recv()
    for c in sent:
        c.wait_send()


def row_ring(partial, n, collective_id):
    blocks, rows, width = partial.shape
    steps_r = n // 2
    steps_l = n - 1 - steps_r
    return pl.pallas_call(
        functools.partial(_ring_kernel, n),
        out_shape=jax.ShapeDtypeStruct((blocks, rows, width), jnp.bfloat16),
        in_specs=[pl.BlockSpec(memory_space=pltpu.VMEM)],
        out_specs=pl.BlockSpec(memory_space=pltpu.VMEM),
        scratch_shapes=[
            pltpu.VMEM((steps_r, rows, width), jnp.float32),
            pltpu.VMEM((steps_l, rows, width), jnp.float32),
            pltpu.VMEM((steps_r - 1, rows, width), jnp.float32),
            pltpu.VMEM((steps_l - 1, rows, width), jnp.float32),
            pltpu.SemaphoreType.DMA((2 * n,)),
            pltpu.SemaphoreType.DMA((2 * n,)),
            pltpu.SemaphoreType.DMA((2 * n,)),
            pltpu.SemaphoreType.DMA((2 * n,)),
        ],
        compiler_params=pltpu.CompilerParams(collective_id=collective_id, has_side_effects=True),
    )(partial)


def shards(new_keys, precision, stored_keys, pair_batch, pair_count, batch_length, batch_slot):
    row_count = lax.axis_size("row")
    col_count = lax.axis_size("col")
    row_index = lax.axis_index("row")
    total_keys = new_keys.shape[0] * col_count
    block_keys = total_keys // row_count
    part_keys = block_keys // col_count
    local_batches, batch_keys, width = stored_keys.shape
    gathered = exchange(new_keys, "col", "row", col_count, True, 0)
    partial_value = jnp.dot(
        gathered.reshape(total_keys, new_keys.shape[1]),
        precision,
        preferred_element_type=jnp.float32,
    )
    every_row = row_ring(partial_value.reshape(row_count, block_keys, -1), row_count, 3)
    whitened = every_row[row_index]
    rows = every_row.reshape(row_count, col_count, part_keys, width)
    terms = jnp.einsum("bcid,sjd->csbij", rows, stored_keys, preferred_element_type=jnp.float32)
    terms = terms.reshape(col_count, local_batches * row_count * part_keys, batch_keys)
    mine = exchange(terms, "col", "row", col_count, False, 1).sum(0)
    mine = mine.reshape(local_batches, row_count, part_keys, batch_keys).transpose(1, 0, 2, 3)
    mine = mine.reshape(row_count, local_batches * part_keys, batch_keys)
    routed = exchange(mine, "row", "col", row_count, False, 2)
    table = routed.reshape(row_count * local_batches, part_keys, batch_keys)
    listed = pair_batch[row_index]
    slots = batch_slot[listed]
    lengths = batch_length[listed]
    count = pair_count[row_index]
    picked = jnp.take(table, slots, axis=0)
    places = jnp.arange(slots.shape[0], dtype=jnp.int32)
    columns = jnp.arange(batch_keys, dtype=jnp.int32)
    keep = (places < count)[:, None, None] & (columns[None, None, :] < lengths[:, None, None])
    shares = jnp.where(keep, picked, jnp.zeros_like(picked))
    return (whitened, shares[None])


def solution(mesh):
    placed = (P("col", "row"), P("row", "col"), P("row", None, "col"), P(), P(), P(), P())
    return jax.shard_map(
        shards,
        mesh=mesh,
        in_specs=placed,
        out_specs=(P("row", "col"), P("row", None, "col", None)),
        check_vma=False,
    )
```

```python
import functools

import jax
import jax.numpy as jnp
from jax import lax
from jax.experimental import pallas as pl
from jax.experimental.pallas import tpu as pltpu
from jax.sharding import PartitionSpec as P


def _exchange_kernel(axis, other, n, gather, x_ref, out_ref, send_sems, recv_sems):
    me = lax.axis_index(axis)
    mine = lax.axis_index(other)

    def at(peer):
        return (peer, mine) if axis == "row" else (mine, peer)

    barrier = pltpu.get_barrier_semaphore()
    for d in range(1, n):
        peer = lax.rem(me + d, n)
        pl.semaphore_signal(barrier, inc=1, device_id=at(peer), device_id_type=pl.DeviceIdType.MESH)
    pl.semaphore_wait(barrier, n - 1)
    copies = []
    for d in range(1, n):
        peer = lax.rem(me + d, n)
        src = x_ref if gather else x_ref.at[peer]
        copy = pltpu.make_async_remote_copy(
            src_ref=src, dst_ref=out_ref.at[me], send_sem=send_sems.at[d], recv_sem=recv_sems.at[d],
            device_id=at(peer), device_id_type=pl.DeviceIdType.MESH)
        copy.start()
        copies.append(copy)
    if gather:
        out_ref[me] = x_ref[...]
    else:
        out_ref[me] = x_ref[me]
    for d in range(1, n):
        copies[d - 1].wait_send()
        source = lax.rem(me + n - d, n)
        src = x_ref if gather else x_ref.at[source]
        incoming = pltpu.make_async_remote_copy(
            src_ref=src, dst_ref=out_ref.at[source], send_sem=send_sems.at[d], recv_sem=recv_sems.at[d],
            device_id=at(source), device_id_type=pl.DeviceIdType.MESH)
        incoming.wait_recv()


def exchange(x, axis, other, n, gather, collective_id):
    block = x.shape if gather else x.shape[1:]
    return pl.pallas_call(
        functools.partial(_exchange_kernel, axis, other, n, gather),
        out_shape=jax.ShapeDtypeStruct((n,) + tuple(block), x.dtype),
        in_specs=[pl.BlockSpec(memory_space=pltpu.VMEM)],
        out_specs=pl.BlockSpec(memory_space=pltpu.VMEM),
        scratch_shapes=[pltpu.SemaphoreType.DMA((n,)), pltpu.SemaphoreType.DMA((n,))],
        compiler_params=pltpu.CompilerParams(collective_id=collective_id, has_side_effects=True),
    )(x)


def _gather_kernel(n, x_ref, out_ref, send_sems, forward_sems, recv_sems):
    me = lax.axis_index("col")
    mine = lax.axis_index("row")
    core = lax.rem(me, 2)
    chip = me // 2
    chips = n // 2
    sibling = chip * 2 + 1 - core
    peers = [lax.rem(chip + d, chips) * 2 + core for d in range(1, chips)]
    barrier = pltpu.get_barrier_semaphore()
    for peer in peers + [sibling]:
        pl.semaphore_signal(barrier, inc=1, device_id=(mine, peer), device_id_type=pl.DeviceIdType.MESH)
    pl.semaphore_wait(barrier, chips)

    def copy(src, slot, sem, peer):
        return pltpu.make_async_remote_copy(
            src_ref=src, dst_ref=out_ref.at[slot], send_sem=sem, recv_sem=recv_sems.at[slot],
            device_id=(mine, peer), device_id_type=pl.DeviceIdType.MESH)

    sent = []
    for d, peer in enumerate(peers + [sibling]):
        c = copy(x_ref, me, send_sems.at[d], peer)
        c.start()
        sent.append(c)
    out_ref[me] = x_ref[...]
    for d, peer in enumerate(peers):
        copy(x_ref, peer, send_sems.at[d], peer).wait_recv()
        c = copy(out_ref.at[peer], peer, forward_sems.at[d], sibling)
        c.start()
        sent.append(c)
    copy(x_ref, sibling, send_sems.at[0], sibling).wait_recv()
    for d in range(1, chips):
        far = lax.rem(chip + d, chips) * 2 + 1 - core
        copy(x_ref, far, send_sems.at[0], sibling).wait_recv()
    for c in sent:
        c.wait_send()


def col_gather(x, n, collective_id):
    return pl.pallas_call(
        functools.partial(_gather_kernel, n),
        out_shape=jax.ShapeDtypeStruct((n,) + x.shape, x.dtype),
        in_specs=[pl.BlockSpec(memory_space=pltpu.VMEM)],
        out_specs=pl.BlockSpec(memory_space=pltpu.VMEM),
        scratch_shapes=[
            pltpu.SemaphoreType.DMA((n,)),
            pltpu.SemaphoreType.DMA((n,)),
            pltpu.SemaphoreType.DMA((n,)),
        ],
        compiler_params=pltpu.CompilerParams(collective_id=collective_id, has_side_effects=True),
    )(x)


def _ring_kernel(n, partial_ref, out_ref, recv_r, recv_l, acc_r, acc_l, rs_send, rs_recv, ag_send, ag_recv):
    me = lax.axis_index("row")
    mine = lax.axis_index("col")
    right = lax.rem(me + 1, n)
    left = lax.rem(me + n - 1, n)
    steps_r = n // 2
    steps_l = n - 1 - steps_r
    barrier = pltpu.get_barrier_semaphore()
    for peer in (left, right):
        pl.semaphore_signal(barrier, inc=1, device_id=(peer, mine), device_id_type=pl.DeviceIdType.MESH)
    pl.semaphore_wait(barrier, 2)

    def send(src, dst, sems, k, peer):
        copy = pltpu.make_async_remote_copy(
            src_ref=src, dst_ref=dst, send_sem=sems.at[k], recv_sem=sems.at[k + n],
            device_id=(peer, mine), device_id_type=pl.DeviceIdType.MESH)
        copy.start()
        return copy

    sent = []
    for s in range(steps_r):
        d_r = lax.rem(me + steps_r - s, n)
        if s == 0:
            src = partial_ref.at[d_r]
        else:
            sent_r[s - 1].wait_recv()
            acc_r[s - 1] = recv_r[s - 1] + partial_ref[d_r]
            src = acc_r.at[s - 1]
        c = send(src, recv_r.at[s], rs_send, s, right)
        sent.append(c)
        sent_r = sent_r + [c] if s else [c]
        if s < steps_l:
            d_l = lax.rem(me + n - steps_l + s, n)
            if s == 0:
                src = partial_ref.at[d_l]
            else:
                sent_l[s - 1].wait_recv()
                acc_l[s - 1] = recv_l[s - 1] + partial_ref[d_l]
                src = acc_l.at[s - 1]
            c = send(src, recv_l.at[s], rs_send, n // 2 + s, left)
            sent.append(c)
            sent_l = sent_l + [c] if s else [c]
    sent_r[-1].wait_recv()
    sent_l[-1].wait_recv()
    total = partial_ref[me] + recv_r[steps_r - 1] + recv_l[steps_l - 1]
    out_ref[me] = total.astype(out_ref.dtype)

    for t in range(steps_r):
        b_r = lax.rem(me + n - t, n)
        if t:
            got_r[t - 1].wait_recv()
        c = send(out_ref.at[b_r], out_ref.at[b_r], ag_send, t, right)
        sent.append(c)
        got_r = got_r + [c] if t else [c]
        if t < steps_l:
            b_l = lax.rem(me + t, n)
            if t:
                got_l[t - 1].wait_recv()
            c = send(out_ref.at[b_l], out_ref.at[b_l], ag_send, n // 2 + t, left)
            sent.append(c)
            got_l = got_l + [c] if t else [c]
    got_r[-1].wait_recv()
    got_l[-1].wait_recv()
    for c in sent:
        c.wait_send()


def row_ring(partial, n, collective_id):
    blocks, rows, width = partial.shape
    steps_r = n // 2
    steps_l = n - 1 - steps_r
    return pl.pallas_call(
        functools.partial(_ring_kernel, n),
        out_shape=jax.ShapeDtypeStruct((blocks, rows, width), jnp.bfloat16),
        in_specs=[pl.BlockSpec(memory_space=pltpu.VMEM)],
        out_specs=pl.BlockSpec(memory_space=pltpu.VMEM),
        scratch_shapes=[
            pltpu.VMEM((steps_r, rows, width), jnp.float32),
            pltpu.VMEM((steps_l, rows, width), jnp.float32),
            pltpu.VMEM((steps_r - 1, rows, width), jnp.float32),
            pltpu.VMEM((steps_l - 1, rows, width), jnp.float32),
            pltpu.SemaphoreType.DMA((2 * n,)),
            pltpu.SemaphoreType.DMA((2 * n,)),
            pltpu.SemaphoreType.DMA((2 * n,)),
            pltpu.SemaphoreType.DMA((2 * n,)),
        ],
        compiler_params=pltpu.CompilerParams(collective_id=collective_id, has_side_effects=True),
    )(partial)


def shards(new_keys, precision, stored_keys, pair_batch, pair_count, batch_length, batch_slot):
    row_count = lax.axis_size("row")
    col_count = lax.axis_size("col")
    row_index = lax.axis_index("row")
    total_keys = new_keys.shape[0] * col_count
    block_keys = total_keys // row_count
    part_keys = block_keys // col_count
    local_batches, batch_keys, width = stored_keys.shape
    gathered = col_gather(new_keys, col_count, 0)
    partial_value = jnp.dot(
        gathered.reshape(total_keys, new_keys.shape[1]),
        precision,
        preferred_element_type=jnp.float32,
    )
    every_row = row_ring(partial_value.reshape(row_count, block_keys, -1), row_count, 3)
    whitened = every_row[row_index]
    rows = every_row.reshape(row_count, col_count, part_keys, width)
    terms = jnp.einsum("bcid,sjd->csbij", rows, stored_keys, preferred_element_type=jnp.float32)
    terms = terms.reshape(col_count, local_batches * row_count * part_keys, batch_keys)
    mine = exchange(terms, "col", "row", col_count, False, 1).sum(0)
    mine = mine.reshape(local_batches, row_count, part_keys, batch_keys).transpose(1, 0, 2, 3)
    mine = mine.reshape(row_count, local_batches * part_keys, batch_keys)
    routed = exchange(mine, "row", "col", row_count, False, 2)
    table = routed.reshape(row_count * local_batches, part_keys, batch_keys)
    listed = pair_batch[row_index]
    slots = batch_slot[listed]
    lengths = batch_length[listed]
    count = pair_count[row_index]
    picked = jnp.take(table, slots, axis=0)
    places = jnp.arange(slots.shape[0], dtype=jnp.int32)
    columns = jnp.arange(batch_keys, dtype=jnp.int32)
    keep = (places < count)[:, None, None] & (columns[None, None, :] < lengths[:, None, None])
    shares = jnp.where(keep, picked, jnp.zeros_like(picked))
    return (whitened, shares[None])


def solution(mesh):
    placed = (P("col", "row"), P("row", "col"), P("row", None, "col"), P(), P(), P(), P())
    return jax.shard_map(
        shards,
        mesh=mesh,
        in_specs=placed,
        out_specs=(P("row", "col"), P("row", None, "col", None)),
        check_vma=False,
    )
```

```python
import functools

import jax
import jax.numpy as jnp
from jax import lax
from jax.experimental import pallas as pl
from jax.experimental.pallas import tpu as pltpu
from jax.sharding import PartitionSpec as P


def _exchange_kernel(axis, other, n, gather, x_ref, out_ref, send_sems, recv_sems):
    me = lax.axis_index(axis)
    mine = lax.axis_index(other)

    def at(peer):
        return (peer, mine) if axis == "row" else (mine, peer)

    barrier = pltpu.get_barrier_semaphore()
    for d in range(1, n):
        peer = lax.rem(me + d, n)
        pl.semaphore_signal(barrier, inc=1, device_id=at(peer), device_id_type=pl.DeviceIdType.MESH)
    pl.semaphore_wait(barrier, n - 1)
    copies = []
    for d in range(1, n):
        peer = lax.rem(me + d, n)
        src = x_ref if gather else x_ref.at[peer]
        copy = pltpu.make_async_remote_copy(
            src_ref=src, dst_ref=out_ref.at[me], send_sem=send_sems.at[d], recv_sem=recv_sems.at[d],
            device_id=at(peer), device_id_type=pl.DeviceIdType.MESH)
        copy.start()
        copies.append(copy)
    if gather:
        out_ref[me] = x_ref[...]
    else:
        out_ref[me] = x_ref[me]
    for d in range(1, n):
        copies[d - 1].wait_send()
        source = lax.rem(me + n - d, n)
        src = x_ref if gather else x_ref.at[source]
        incoming = pltpu.make_async_remote_copy(
            src_ref=src, dst_ref=out_ref.at[source], send_sem=send_sems.at[d], recv_sem=recv_sems.at[d],
            device_id=at(source), device_id_type=pl.DeviceIdType.MESH)
        incoming.wait_recv()


def exchange(x, axis, other, n, gather, collective_id):
    block = x.shape if gather else x.shape[1:]
    return pl.pallas_call(
        functools.partial(_exchange_kernel, axis, other, n, gather),
        out_shape=jax.ShapeDtypeStruct((n,) + tuple(block), x.dtype),
        in_specs=[pl.BlockSpec(memory_space=pltpu.VMEM)],
        out_specs=pl.BlockSpec(memory_space=pltpu.VMEM),
        scratch_shapes=[pltpu.SemaphoreType.DMA((n,)), pltpu.SemaphoreType.DMA((n,))],
        compiler_params=pltpu.CompilerParams(collective_id=collective_id, has_side_effects=True),
    )(x)


def _gather_kernel(n, x_ref, out_ref, send_sems, forward_sems, recv_sems):
    me = lax.axis_index("col")
    mine = lax.axis_index("row")
    core = lax.rem(me, 2)
    chip = me // 2
    chips = n // 2
    sibling = chip * 2 + 1 - core
    peers = [lax.rem(chip + d, chips) * 2 + core for d in range(1, chips)]
    barrier = pltpu.get_barrier_semaphore()
    for peer in peers + [sibling]:
        pl.semaphore_signal(barrier, inc=1, device_id=(mine, peer), device_id_type=pl.DeviceIdType.MESH)
    pl.semaphore_wait(barrier, chips)

    def copy(src, slot, sem, peer):
        return pltpu.make_async_remote_copy(
            src_ref=src, dst_ref=out_ref.at[slot], send_sem=sem, recv_sem=recv_sems.at[slot],
            device_id=(mine, peer), device_id_type=pl.DeviceIdType.MESH)

    sent = []
    for d, peer in enumerate(peers + [sibling]):
        c = copy(x_ref, me, send_sems.at[d], peer)
        c.start()
        sent.append(c)
    out_ref[me] = x_ref[...]
    for d, peer in enumerate(peers):
        copy(x_ref, peer, send_sems.at[d], peer).wait_recv()
        c = copy(out_ref.at[peer], peer, forward_sems.at[d], sibling)
        c.start()
        sent.append(c)
    copy(x_ref, sibling, send_sems.at[0], sibling).wait_recv()
    for d in range(1, chips):
        far = lax.rem(chip + d, chips) * 2 + 1 - core
        copy(x_ref, far, send_sems.at[0], sibling).wait_recv()
    for c in sent:
        c.wait_send()


def col_gather(x, n, collective_id):
    return pl.pallas_call(
        functools.partial(_gather_kernel, n),
        out_shape=jax.ShapeDtypeStruct((n,) + x.shape, x.dtype),
        in_specs=[pl.BlockSpec(memory_space=pltpu.VMEM)],
        out_specs=pl.BlockSpec(memory_space=pltpu.VMEM),
        scratch_shapes=[
            pltpu.SemaphoreType.DMA((n,)),
            pltpu.SemaphoreType.DMA((n,)),
            pltpu.SemaphoreType.DMA((n,)),
        ],
        compiler_params=pltpu.CompilerParams(collective_id=collective_id, has_side_effects=True),
    )(x)


def _scatter_kernel(n, x_ref, out_ref, half, recv, acc, send_sems, recv_sems):
    me = lax.axis_index("col")
    mine = lax.axis_index("row")
    core = lax.rem(me, 2)
    chip = me // 2
    chips = n // 2
    sibling = chip * 2 + 1 - core
    peers = [lax.rem(chip + d, chips) * 2 + core for d in range(1, chips)]
    barrier = pltpu.get_barrier_semaphore()
    for peer in peers + [sibling]:
        pl.semaphore_signal(barrier, inc=1, device_id=(mine, peer), device_id_type=pl.DeviceIdType.MESH)
    pl.semaphore_wait(barrier, chips)

    swap = pltpu.make_async_remote_copy(
        src_ref=x_ref.at[:, 1 - core], dst_ref=half, send_sem=send_sems.at[0], recv_sem=recv_sems.at[0],
        device_id=(mine, sibling), device_id_type=pl.DeviceIdType.MESH)
    swap.start()
    swap.wait_recv()
    acc[...] = x_ref[:, core] + half[...]
    sent = [swap]
    for d in range(1, chips):
        target = lax.rem(chip + d, chips)
        c = pltpu.make_async_remote_copy(
            src_ref=acc.at[target], dst_ref=recv.at[chip], send_sem=send_sems.at[d], recv_sem=recv_sems.at[d],
            device_id=(mine, target * 2 + core), device_id_type=pl.DeviceIdType.MESH)
        c.start()
        sent.append(c)
    total = acc[chip]
    for d in range(1, chips):
        source = lax.rem(chip + chips - d, chips)
        pltpu.make_async_remote_copy(
            src_ref=acc.at[source], dst_ref=recv.at[source], send_sem=send_sems.at[d], recv_sem=recv_sems.at[d],
            device_id=(mine, source * 2 + core), device_id_type=pl.DeviceIdType.MESH).wait_recv()
        total = total + recv[source]
    out_ref[...] = total
    for c in sent:
        c.wait_send()


def col_scatter(x, n, collective_id):
    chips = n // 2
    block = x.shape[1:]
    return pl.pallas_call(
        functools.partial(_scatter_kernel, n),
        out_shape=jax.ShapeDtypeStruct(block, x.dtype),
        in_specs=[pl.BlockSpec(memory_space=pltpu.VMEM)],
        out_specs=pl.BlockSpec(memory_space=pltpu.VMEM),
        scratch_shapes=[
            pltpu.VMEM((chips,) + block, x.dtype),
            pltpu.VMEM((chips,) + block, x.dtype),
            pltpu.VMEM((chips,) + block, x.dtype),
            pltpu.SemaphoreType.DMA((chips,)),
            pltpu.SemaphoreType.DMA((chips,)),
        ],
        compiler_params=pltpu.CompilerParams(collective_id=collective_id, has_side_effects=True),
    )(x.reshape((chips, 2) + block))


def _ring_kernel(n, partial_ref, out_ref, recv_r, recv_l, acc_r, acc_l, rs_send, rs_recv, ag_send, ag_recv):
    me = lax.axis_index("row")
    mine = lax.axis_index("col")
    right = lax.rem(me + 1, n)
    left = lax.rem(me + n - 1, n)
    steps_r = n // 2
    steps_l = n - 1 - steps_r
    barrier = pltpu.get_barrier_semaphore()
    for peer in (left, right):
        pl.semaphore_signal(barrier, inc=1, device_id=(peer, mine), device_id_type=pl.DeviceIdType.MESH)
    pl.semaphore_wait(barrier, 2)

    def send(src, dst, sems, k, peer):
        copy = pltpu.make_async_remote_copy(
            src_ref=src, dst_ref=dst, send_sem=sems.at[k], recv_sem=sems.at[k + n],
            device_id=(peer, mine), device_id_type=pl.DeviceIdType.MESH)
        copy.start()
        return copy

    sent = []
    for s in range(steps_r):
        d_r = lax.rem(me + steps_r - s, n)
        if s == 0:
            src = partial_ref.at[d_r]
        else:
            sent_r[s - 1].wait_recv()
            acc_r[s - 1] = recv_r[s - 1] + partial_ref[d_r]
            src = acc_r.at[s - 1]
        c = send(src, recv_r.at[s], rs_send, s, right)
        sent.append(c)
        sent_r = sent_r + [c] if s else [c]
        if s < steps_l:
            d_l = lax.rem(me + n - steps_l + s, n)
            if s == 0:
                src = partial_ref.at[d_l]
            else:
                sent_l[s - 1].wait_recv()
                acc_l[s - 1] = recv_l[s - 1] + partial_ref[d_l]
                src = acc_l.at[s - 1]
            c = send(src, recv_l.at[s], rs_send, n // 2 + s, left)
            sent.append(c)
            sent_l = sent_l + [c] if s else [c]
    sent_r[-1].wait_recv()
    sent_l[-1].wait_recv()
    total = partial_ref[me] + recv_r[steps_r - 1] + recv_l[steps_l - 1]
    out_ref[me] = total.astype(out_ref.dtype)

    for t in range(steps_r):
        b_r = lax.rem(me + n - t, n)
        if t:
            got_r[t - 1].wait_recv()
        c = send(out_ref.at[b_r], out_ref.at[b_r], ag_send, t, right)
        sent.append(c)
        got_r = got_r + [c] if t else [c]
        if t < steps_l:
            b_l = lax.rem(me + t, n)
            if t:
                got_l[t - 1].wait_recv()
            c = send(out_ref.at[b_l], out_ref.at[b_l], ag_send, n // 2 + t, left)
            sent.append(c)
            got_l = got_l + [c] if t else [c]
    got_r[-1].wait_recv()
    got_l[-1].wait_recv()
    for c in sent:
        c.wait_send()


def row_ring(partial, n, collective_id):
    blocks, rows, width = partial.shape
    steps_r = n // 2
    steps_l = n - 1 - steps_r
    return pl.pallas_call(
        functools.partial(_ring_kernel, n),
        out_shape=jax.ShapeDtypeStruct((blocks, rows, width), jnp.bfloat16),
        in_specs=[pl.BlockSpec(memory_space=pltpu.VMEM)],
        out_specs=pl.BlockSpec(memory_space=pltpu.VMEM),
        scratch_shapes=[
            pltpu.VMEM((steps_r, rows, width), jnp.float32),
            pltpu.VMEM((steps_l, rows, width), jnp.float32),
            pltpu.VMEM((steps_r - 1, rows, width), jnp.float32),
            pltpu.VMEM((steps_l - 1, rows, width), jnp.float32),
            pltpu.SemaphoreType.DMA((2 * n,)),
            pltpu.SemaphoreType.DMA((2 * n,)),
            pltpu.SemaphoreType.DMA((2 * n,)),
            pltpu.SemaphoreType.DMA((2 * n,)),
        ],
        compiler_params=pltpu.CompilerParams(collective_id=collective_id, has_side_effects=True),
    )(partial)


def shards(new_keys, precision, stored_keys, pair_batch, pair_count, batch_length, batch_slot):
    row_count = lax.axis_size("row")
    col_count = lax.axis_size("col")
    row_index = lax.axis_index("row")
    total_keys = new_keys.shape[0] * col_count
    block_keys = total_keys // row_count
    part_keys = block_keys // col_count
    local_batches, batch_keys, width = stored_keys.shape
    gathered = col_gather(new_keys, col_count, 0)
    partial_value = jnp.dot(
        gathered.reshape(total_keys, new_keys.shape[1]),
        precision,
        preferred_element_type=jnp.float32,
    )
    every_row = row_ring(partial_value.reshape(row_count, block_keys, -1), row_count, 3)
    whitened = every_row[row_index]
    rows = every_row.reshape(row_count, col_count, part_keys, width)
    terms = jnp.einsum("bcid,sjd->csbij", rows, stored_keys, preferred_element_type=jnp.float32)
    terms = terms.reshape(col_count, local_batches * row_count * part_keys, batch_keys)
    mine = col_scatter(terms, col_count, 1)
    mine = mine.reshape(local_batches, row_count, part_keys, batch_keys).transpose(1, 0, 2, 3)
    mine = mine.reshape(row_count, local_batches * part_keys, batch_keys)
    routed = exchange(mine, "row", "col", row_count, False, 2)
    table = routed.reshape(row_count * local_batches, part_keys, batch_keys)
    listed = pair_batch[row_index]
    slots = batch_slot[listed]
    lengths = batch_length[listed]
    count = pair_count[row_index]
    picked = jnp.take(table, slots, axis=0)
    places = jnp.arange(slots.shape[0], dtype=jnp.int32)
    columns = jnp.arange(batch_keys, dtype=jnp.int32)
    keep = (places < count)[:, None, None] & (columns[None, None, :] < lengths[:, None, None])
    shares = jnp.where(keep, picked, jnp.zeros_like(picked))
    return (whitened, shares[None])


def solution(mesh):
    placed = (P("col", "row"), P("row", "col"), P("row", None, "col"), P(), P(), P(), P())
    return jax.shard_map(
        shards,
        mesh=mesh,
        in_specs=placed,
        out_specs=(P("row", "col"), P("row", None, "col", None)),
        check_vma=False,
    )
```

```python
import functools

import jax
import jax.numpy as jnp
from jax import lax
from jax.experimental import pallas as pl
from jax.experimental.pallas import tpu as pltpu
from jax.sharding import PartitionSpec as P


def _exchange_kernel(axis, other, n, gather, x_ref, out_ref, send_sems, recv_sems):
    me = lax.axis_index(axis)
    mine = lax.axis_index(other)

    def at(peer):
        return (peer, mine) if axis == "row" else (mine, peer)

    barrier = pltpu.get_barrier_semaphore()
    for d in range(1, n):
        peer = lax.rem(me + d, n)
        pl.semaphore_signal(barrier, inc=1, device_id=at(peer), device_id_type=pl.DeviceIdType.MESH)
    pl.semaphore_wait(barrier, n - 1)
    copies = []
    for d in range(1, n):
        peer = lax.rem(me + d, n)
        src = x_ref if gather else x_ref.at[peer]
        copy = pltpu.make_async_remote_copy(
            src_ref=src, dst_ref=out_ref.at[me], send_sem=send_sems.at[d], recv_sem=recv_sems.at[d],
            device_id=at(peer), device_id_type=pl.DeviceIdType.MESH)
        copy.start()
        copies.append(copy)
    if gather:
        out_ref[me] = x_ref[...]
    else:
        out_ref[me] = x_ref[me]
    for d in range(1, n):
        copies[d - 1].wait_send()
        source = lax.rem(me + n - d, n)
        src = x_ref if gather else x_ref.at[source]
        incoming = pltpu.make_async_remote_copy(
            src_ref=src, dst_ref=out_ref.at[source], send_sem=send_sems.at[d], recv_sem=recv_sems.at[d],
            device_id=at(source), device_id_type=pl.DeviceIdType.MESH)
        incoming.wait_recv()


def exchange(x, axis, other, n, gather, collective_id):
    block = x.shape if gather else x.shape[1:]
    return pl.pallas_call(
        functools.partial(_exchange_kernel, axis, other, n, gather),
        out_shape=jax.ShapeDtypeStruct((n,) + tuple(block), x.dtype),
        in_specs=[pl.BlockSpec(memory_space=pltpu.VMEM)],
        out_specs=pl.BlockSpec(memory_space=pltpu.VMEM),
        scratch_shapes=[pltpu.SemaphoreType.DMA((n,)), pltpu.SemaphoreType.DMA((n,))],
        compiler_params=pltpu.CompilerParams(collective_id=collective_id, has_side_effects=True),
    )(x)


def _gather_kernel(n, x_ref, out_ref, send_sems, forward_sems, recv_sems):
    me = lax.axis_index("col")
    mine = lax.axis_index("row")
    core = lax.rem(me, 2)
    chip = me // 2
    chips = n // 2
    sibling = chip * 2 + 1 - core
    peers = [lax.rem(chip + d, chips) * 2 + core for d in range(1, chips)]
    barrier = pltpu.get_barrier_semaphore()
    for peer in peers + [sibling]:
        pl.semaphore_signal(barrier, inc=1, device_id=(mine, peer), device_id_type=pl.DeviceIdType.MESH)
    pl.semaphore_wait(barrier, chips)

    def copy(src, slot, sem, peer):
        return pltpu.make_async_remote_copy(
            src_ref=src, dst_ref=out_ref.at[slot], send_sem=sem, recv_sem=recv_sems.at[slot],
            device_id=(mine, peer), device_id_type=pl.DeviceIdType.MESH)

    sent = []
    for d, peer in enumerate(peers + [sibling]):
        c = copy(x_ref, me, send_sems.at[d], peer)
        c.start()
        sent.append(c)
    out_ref[me] = x_ref[...]
    for d, peer in enumerate(peers):
        copy(x_ref, peer, send_sems.at[d], peer).wait_recv()
        c = copy(out_ref.at[peer], peer, forward_sems.at[d], sibling)
        c.start()
        sent.append(c)
    copy(x_ref, sibling, send_sems.at[0], sibling).wait_recv()
    for d in range(1, chips):
        far = lax.rem(chip + d, chips) * 2 + 1 - core
        copy(x_ref, far, send_sems.at[0], sibling).wait_recv()
    for c in sent:
        c.wait_send()


def col_gather(x, n, collective_id):
    return pl.pallas_call(
        functools.partial(_gather_kernel, n),
        out_shape=jax.ShapeDtypeStruct((n,) + x.shape, x.dtype),
        in_specs=[pl.BlockSpec(memory_space=pltpu.VMEM)],
        out_specs=pl.BlockSpec(memory_space=pltpu.VMEM),
        scratch_shapes=[
            pltpu.SemaphoreType.DMA((n,)),
            pltpu.SemaphoreType.DMA((n,)),
            pltpu.SemaphoreType.DMA((n,)),
        ],
        compiler_params=pltpu.CompilerParams(collective_id=collective_id, has_side_effects=True),
    )(x)


def _scatter_kernel(n, x_ref, out_ref, half, recv, acc, send_sems, recv_sems):
    me = lax.axis_index("col")
    mine = lax.axis_index("row")
    core = lax.rem(me, 2)
    chip = me // 2
    chips = n // 2
    sibling = chip * 2 + 1 - core
    peers = [lax.rem(chip + d, chips) * 2 + core for d in range(1, chips)]
    barrier = pltpu.get_barrier_semaphore()
    for peer in peers + [sibling]:
        pl.semaphore_signal(barrier, inc=1, device_id=(mine, peer), device_id_type=pl.DeviceIdType.MESH)
    pl.semaphore_wait(barrier, chips)

    swap = pltpu.make_async_remote_copy(
        src_ref=x_ref.at[:, 1 - core], dst_ref=half, send_sem=send_sems.at[0], recv_sem=recv_sems.at[0],
        device_id=(mine, sibling), device_id_type=pl.DeviceIdType.MESH)
    swap.start()
    swap.wait_recv()
    acc[...] = x_ref[:, core] + half[...]
    sent = [swap]
    for d in range(1, chips):
        target = lax.rem(chip + d, chips)
        c = pltpu.make_async_remote_copy(
            src_ref=acc.at[target], dst_ref=recv.at[chip], send_sem=send_sems.at[d], recv_sem=recv_sems.at[d],
            device_id=(mine, target * 2 + core), device_id_type=pl.DeviceIdType.MESH)
        c.start()
        sent.append(c)
    total = acc[chip]
    for d in range(1, chips):
        source = lax.rem(chip + chips - d, chips)
        pltpu.make_async_remote_copy(
            src_ref=acc.at[source], dst_ref=recv.at[source], send_sem=send_sems.at[d], recv_sem=recv_sems.at[d],
            device_id=(mine, source * 2 + core), device_id_type=pl.DeviceIdType.MESH).wait_recv()
        total = total + recv[source]
    out_ref[...] = total
    for c in sent:
        c.wait_send()


def col_scatter(x, n, collective_id):
    chips = n // 2
    block = x.shape[1:]
    return pl.pallas_call(
        functools.partial(_scatter_kernel, n),
        out_shape=jax.ShapeDtypeStruct(block, x.dtype),
        in_specs=[pl.BlockSpec(memory_space=pltpu.VMEM)],
        out_specs=pl.BlockSpec(memory_space=pltpu.VMEM),
        scratch_shapes=[
            pltpu.VMEM((chips,) + block, x.dtype),
            pltpu.VMEM((chips,) + block, x.dtype),
            pltpu.VMEM((chips,) + block, x.dtype),
            pltpu.SemaphoreType.DMA((chips,)),
            pltpu.SemaphoreType.DMA((chips,)),
        ],
        compiler_params=pltpu.CompilerParams(collective_id=collective_id, has_side_effects=True),
    )(x.reshape((chips, 2) + block))


def _ring_kernel(n, chunks, partial_ref, out_ref, recv_r, recv_l, acc_r, acc_l, rs_sems, ag_sems):
    me = lax.axis_index("row")
    mine = lax.axis_index("col")
    right = lax.rem(me + 1, n)
    left = lax.rem(me + n - 1, n)
    steps_r = n // 2
    steps_l = n - 1 - steps_r
    size = partial_ref.shape[1] // chunks
    half = n * chunks
    barrier = pltpu.get_barrier_semaphore()
    for peer in (left, right):
        pl.semaphore_signal(barrier, inc=1, device_id=(peer, mine), device_id_type=pl.DeviceIdType.MESH)
    pl.semaphore_wait(barrier, 2)

    def send(src, dst, sems, k, peer):
        copy = pltpu.make_async_remote_copy(
            src_ref=src, dst_ref=dst, send_sem=sems.at[k], recv_sem=sems.at[k + 2 * half],
            device_id=(peer, mine), device_id_type=pl.DeviceIdType.MESH)
        copy.start()
        return copy

    sent = []
    got_r = {}
    got_l = {}
    for s in range(steps_r):
        for h in range(chunks):
            rows = pl.ds(h * size, size)
            d_r = lax.rem(me + steps_r - s, n)
            if s == 0:
                src = partial_ref.at[d_r, rows]
            else:
                got_r[s - 1, h].wait_recv()
                acc_r[s - 1, rows] = recv_r[s - 1, rows] + partial_ref[d_r, rows]
                src = acc_r.at[s - 1, rows]
            got_r[s, h] = send(src, recv_r.at[s, rows], rs_sems, s * chunks + h, right)
            sent.append(got_r[s, h])
            if s < steps_l:
                d_l = lax.rem(me + n - steps_l + s, n)
                if s == 0:
                    src = partial_ref.at[d_l, rows]
                else:
                    got_l[s - 1, h].wait_recv()
                    acc_l[s - 1, rows] = recv_l[s - 1, rows] + partial_ref[d_l, rows]
                    src = acc_l.at[s - 1, rows]
                got_l[s, h] = send(src, recv_l.at[s, rows], rs_sems, half + s * chunks + h, left)
                sent.append(got_l[s, h])
    for h in range(chunks):
        rows = pl.ds(h * size, size)
        got_r[steps_r - 1, h].wait_recv()
        got_l[steps_l - 1, h].wait_recv()
        total = partial_ref[me, rows] + recv_r[steps_r - 1, rows] + recv_l[steps_l - 1, rows]
        out_ref[me, rows] = total.astype(out_ref.dtype)

    ag_r = {}
    ag_l = {}
    for t in range(steps_r):
        for h in range(chunks):
            rows = pl.ds(h * size, size)
            b_r = lax.rem(me + n - t, n)
            if t:
                ag_r[t - 1, h].wait_recv()
            ag_r[t, h] = send(out_ref.at[b_r, rows], out_ref.at[b_r, rows], ag_sems, t * chunks + h, right)
            sent.append(ag_r[t, h])
            if t < steps_l:
                b_l = lax.rem(me + t, n)
                if t:
                    ag_l[t - 1, h].wait_recv()
                ag_l[t, h] = send(out_ref.at[b_l, rows], out_ref.at[b_l, rows], ag_sems, half + t * chunks + h, left)
                sent.append(ag_l[t, h])
    for h in range(chunks):
        ag_r[steps_r - 1, h].wait_recv()
        ag_l[steps_l - 1, h].wait_recv()
    for c in sent:
        c.wait_send()


def row_ring(partial, n, collective_id, chunks=2):
    blocks, rows, width = partial.shape
    steps_r = n // 2
    steps_l = n - 1 - steps_r
    return pl.pallas_call(
        functools.partial(_ring_kernel, n, chunks),
        out_shape=jax.ShapeDtypeStruct((blocks, rows, width), jnp.bfloat16),
        in_specs=[pl.BlockSpec(memory_space=pltpu.VMEM)],
        out_specs=pl.BlockSpec(memory_space=pltpu.VMEM),
        scratch_shapes=[
            pltpu.VMEM((steps_r, rows, width), jnp.float32),
            pltpu.VMEM((steps_l, rows, width), jnp.float32),
            pltpu.VMEM((steps_r - 1, rows, width), jnp.float32),
            pltpu.VMEM((steps_l - 1, rows, width), jnp.float32),
            pltpu.SemaphoreType.DMA((4 * n * chunks,)),
            pltpu.SemaphoreType.DMA((4 * n * chunks,)),
        ],
        compiler_params=pltpu.CompilerParams(collective_id=collective_id, has_side_effects=True),
    )(partial)


def shards(new_keys, precision, stored_keys, pair_batch, pair_count, batch_length, batch_slot):
    row_count = lax.axis_size("row")
    col_count = lax.axis_size("col")
    row_index = lax.axis_index("row")
    total_keys = new_keys.shape[0] * col_count
    block_keys = total_keys // row_count
    part_keys = block_keys // col_count
    local_batches, batch_keys, width = stored_keys.shape
    gathered = col_gather(new_keys, col_count, 0)
    partial_value = jnp.dot(
        gathered.reshape(total_keys, new_keys.shape[1]),
        precision,
        preferred_element_type=jnp.float32,
    )
    every_row = row_ring(partial_value.reshape(row_count, block_keys, -1), row_count, 3)
    whitened = every_row[row_index]
    rows = every_row.reshape(row_count, col_count, part_keys, width)
    terms = jnp.einsum("bcid,sjd->csbij", rows, stored_keys, preferred_element_type=jnp.float32)
    terms = terms.reshape(col_count, local_batches * row_count * part_keys, batch_keys)
    mine = col_scatter(terms, col_count, 1)
    mine = mine.reshape(local_batches, row_count, part_keys, batch_keys).transpose(1, 0, 2, 3)
    mine = mine.reshape(row_count, local_batches * part_keys, batch_keys)
    routed = exchange(mine, "row", "col", row_count, False, 2)
    table = routed.reshape(row_count * local_batches, part_keys, batch_keys)
    listed = pair_batch[row_index]
    slots = batch_slot[listed]
    lengths = batch_length[listed]
    count = pair_count[row_index]
    picked = jnp.take(table, slots, axis=0)
    places = jnp.arange(slots.shape[0], dtype=jnp.int32)
    columns = jnp.arange(batch_keys, dtype=jnp.int32)
    keep = (places < count)[:, None, None] & (columns[None, None, :] < lengths[:, None, None])
    shares = jnp.where(keep, picked, jnp.zeros_like(picked))
    return (whitened, shares[None])


def solution(mesh):
    placed = (P("col", "row"), P("row", "col"), P("row", None, "col"), P(), P(), P(), P())
    return jax.shard_map(
        shards,
        mesh=mesh,
        in_specs=placed,
        out_specs=(P("row", "col"), P("row", None, "col", None)),
        check_vma=False,
    )
```

```python
import functools

import jax
import jax.numpy as jnp
from jax import lax
from jax.experimental import pallas as pl
from jax.experimental.pallas import tpu as pltpu
from jax.sharding import PartitionSpec as P


def _exchange_kernel(axis, other, n, gather, x_ref, out_ref, send_sems, recv_sems):
    me = lax.axis_index(axis)
    mine = lax.axis_index(other)

    def at(peer):
        return (peer, mine) if axis == "row" else (mine, peer)

    barrier = pltpu.get_barrier_semaphore()
    for d in range(1, n):
        peer = lax.rem(me + d, n)
        pl.semaphore_signal(barrier, inc=1, device_id=at(peer), device_id_type=pl.DeviceIdType.MESH)
    pl.semaphore_wait(barrier, n - 1)
    copies = []
    for d in range(1, n):
        peer = lax.rem(me + d, n)
        src = x_ref if gather else x_ref.at[peer]
        copy = pltpu.make_async_remote_copy(
            src_ref=src, dst_ref=out_ref.at[me], send_sem=send_sems.at[d], recv_sem=recv_sems.at[d],
            device_id=at(peer), device_id_type=pl.DeviceIdType.MESH)
        copy.start()
        copies.append(copy)
    if gather:
        out_ref[me] = x_ref[...]
    else:
        out_ref[me] = x_ref[me]
    for d in range(1, n):
        copies[d - 1].wait_send()
        source = lax.rem(me + n - d, n)
        src = x_ref if gather else x_ref.at[source]
        incoming = pltpu.make_async_remote_copy(
            src_ref=src, dst_ref=out_ref.at[source], send_sem=send_sems.at[d], recv_sem=recv_sems.at[d],
            device_id=at(source), device_id_type=pl.DeviceIdType.MESH)
        incoming.wait_recv()


def exchange(x, axis, other, n, gather, collective_id):
    block = x.shape if gather else x.shape[1:]
    return pl.pallas_call(
        functools.partial(_exchange_kernel, axis, other, n, gather),
        out_shape=jax.ShapeDtypeStruct((n,) + tuple(block), x.dtype),
        in_specs=[pl.BlockSpec(memory_space=pltpu.VMEM)],
        out_specs=pl.BlockSpec(memory_space=pltpu.VMEM),
        scratch_shapes=[pltpu.SemaphoreType.DMA((n,)), pltpu.SemaphoreType.DMA((n,))],
        compiler_params=pltpu.CompilerParams(collective_id=collective_id, has_side_effects=True),
    )(x)


def _gather_kernel(n, x_ref, out_ref, send_sems, forward_sems, recv_sems):
    me = lax.axis_index("col")
    mine = lax.axis_index("row")
    core = lax.rem(me, 2)
    chip = me // 2
    chips = n // 2
    sibling = chip * 2 + 1 - core
    peers = [lax.rem(chip + d, chips) * 2 + core for d in range(1, chips)]
    barrier = pltpu.get_barrier_semaphore()
    for peer in peers + [sibling]:
        pl.semaphore_signal(barrier, inc=1, device_id=(mine, peer), device_id_type=pl.DeviceIdType.MESH)
    pl.semaphore_wait(barrier, chips)

    def copy(src, slot, sem, peer):
        return pltpu.make_async_remote_copy(
            src_ref=src, dst_ref=out_ref.at[slot], send_sem=sem, recv_sem=recv_sems.at[slot],
            device_id=(mine, peer), device_id_type=pl.DeviceIdType.MESH)

    sent = []
    for d, peer in enumerate(peers + [sibling]):
        c = copy(x_ref, me, send_sems.at[d], peer)
        c.start()
        sent.append(c)
    out_ref[me] = x_ref[...]
    for d, peer in enumerate(peers):
        copy(x_ref, peer, send_sems.at[d], peer).wait_recv()
        c = copy(out_ref.at[peer], peer, forward_sems.at[d], sibling)
        c.start()
        sent.append(c)
    copy(x_ref, sibling, send_sems.at[0], sibling).wait_recv()
    for d in range(1, chips):
        far = lax.rem(chip + d, chips) * 2 + 1 - core
        copy(x_ref, far, send_sems.at[0], sibling).wait_recv()
    for c in sent:
        c.wait_send()


def col_gather(x, n, collective_id):
    return pl.pallas_call(
        functools.partial(_gather_kernel, n),
        out_shape=jax.ShapeDtypeStruct((n,) + x.shape, x.dtype),
        in_specs=[pl.BlockSpec(memory_space=pltpu.VMEM)],
        out_specs=pl.BlockSpec(memory_space=pltpu.VMEM),
        scratch_shapes=[
            pltpu.SemaphoreType.DMA((n,)),
            pltpu.SemaphoreType.DMA((n,)),
            pltpu.SemaphoreType.DMA((n,)),
        ],
        compiler_params=pltpu.CompilerParams(collective_id=collective_id, has_side_effects=True),
    )(x)


def _scatter_kernel(n, x_ref, out_ref, half, recv, acc, send_sems, recv_sems):
    me = lax.axis_index("col")
    mine = lax.axis_index("row")
    core = lax.rem(me, 2)
    chip = me // 2
    chips = n // 2
    sibling = chip * 2 + 1 - core
    peers = [lax.rem(chip + d, chips) * 2 + core for d in range(1, chips)]
    barrier = pltpu.get_barrier_semaphore()
    for peer in peers + [sibling]:
        pl.semaphore_signal(barrier, inc=1, device_id=(mine, peer), device_id_type=pl.DeviceIdType.MESH)
    pl.semaphore_wait(barrier, chips)

    swap = pltpu.make_async_remote_copy(
        src_ref=x_ref.at[:, 1 - core], dst_ref=half, send_sem=send_sems.at[0], recv_sem=recv_sems.at[0],
        device_id=(mine, sibling), device_id_type=pl.DeviceIdType.MESH)
    swap.start()
    swap.wait_recv()
    acc[...] = x_ref[:, core] + half[...]
    sent = [swap]
    for d in range(1, chips):
        target = lax.rem(chip + d, chips)
        c = pltpu.make_async_remote_copy(
            src_ref=acc.at[target], dst_ref=recv.at[chip], send_sem=send_sems.at[d], recv_sem=recv_sems.at[d],
            device_id=(mine, target * 2 + core), device_id_type=pl.DeviceIdType.MESH)
        c.start()
        sent.append(c)
    total = acc[chip]
    for d in range(1, chips):
        source = lax.rem(chip + chips - d, chips)
        pltpu.make_async_remote_copy(
            src_ref=acc.at[source], dst_ref=recv.at[source], send_sem=send_sems.at[d], recv_sem=recv_sems.at[d],
            device_id=(mine, source * 2 + core), device_id_type=pl.DeviceIdType.MESH).wait_recv()
        total = total + recv[source]
    out_ref[...] = total
    for c in sent:
        c.wait_send()


def col_scatter(x, n, collective_id):
    chips = n // 2
    block = x.shape[1:]
    return pl.pallas_call(
        functools.partial(_scatter_kernel, n),
        out_shape=jax.ShapeDtypeStruct(block, x.dtype),
        in_specs=[pl.BlockSpec(memory_space=pltpu.VMEM)],
        out_specs=pl.BlockSpec(memory_space=pltpu.VMEM),
        scratch_shapes=[
            pltpu.VMEM((chips,) + block, x.dtype),
            pltpu.VMEM((chips,) + block, x.dtype),
            pltpu.VMEM((chips,) + block, x.dtype),
            pltpu.SemaphoreType.DMA((chips,)),
            pltpu.SemaphoreType.DMA((chips,)),
        ],
        compiler_params=pltpu.CompilerParams(collective_id=collective_id, has_side_effects=True),
    )(x.reshape((chips, 2) + block))


def _ring_kernel(n, chunks, partial_ref, out_ref, recv_r, recv_l, acc_r, acc_l, rs_sems, ag_sems):
    me = lax.axis_index("row")
    mine = lax.axis_index("col")
    right = lax.rem(me + 1, n)
    left = lax.rem(me + n - 1, n)
    steps_r = n // 2
    steps_l = n - 1 - steps_r
    size = partial_ref.shape[1] // chunks
    half = n * chunks
    barrier = pltpu.get_barrier_semaphore()
    for peer in (left, right):
        pl.semaphore_signal(barrier, inc=1, device_id=(peer, mine), device_id_type=pl.DeviceIdType.MESH)
    pl.semaphore_wait(barrier, 2)

    def send(src, dst, sems, k, peer):
        copy = pltpu.make_async_remote_copy(
            src_ref=src, dst_ref=dst, send_sem=sems.at[k], recv_sem=sems.at[k + 2 * half],
            device_id=(peer, mine), device_id_type=pl.DeviceIdType.MESH)
        copy.start()
        return copy

    sent = []
    got_r = {}
    got_l = {}
    for s in range(steps_r):
        for h in range(chunks):
            rows = pl.ds(h * size, size)
            d_r = lax.rem(me + steps_r - s, n)
            if s == 0:
                src = partial_ref.at[d_r, rows]
            else:
                got_r[s - 1, h].wait_recv()
                acc_r[s - 1, rows] = recv_r[s - 1, rows] + partial_ref[d_r, rows]
                src = acc_r.at[s - 1, rows]
            got_r[s, h] = send(src, recv_r.at[s, rows], rs_sems, s * chunks + h, right)
            sent.append(got_r[s, h])
            if s < steps_l:
                d_l = lax.rem(me + n - steps_l + s, n)
                if s == 0:
                    src = partial_ref.at[d_l, rows]
                else:
                    got_l[s - 1, h].wait_recv()
                    acc_l[s - 1, rows] = recv_l[s - 1, rows] + partial_ref[d_l, rows]
                    src = acc_l.at[s - 1, rows]
                got_l[s, h] = send(src, recv_l.at[s, rows], rs_sems, half + s * chunks + h, left)
                sent.append(got_l[s, h])
    for h in range(chunks):
        rows = pl.ds(h * size, size)
        got_r[steps_r - 1, h].wait_recv()
        got_l[steps_l - 1, h].wait_recv()
        total = partial_ref[me, rows] + recv_r[steps_r - 1, rows] + recv_l[steps_l - 1, rows]
        out_ref[me, rows] = total.astype(out_ref.dtype)

    ag_r = {}
    ag_l = {}
    for t in range(steps_r):
        for h in range(chunks):
            rows = pl.ds(h * size, size)
            b_r = lax.rem(me + n - t, n)
            if t:
                ag_r[t - 1, h].wait_recv()
            ag_r[t, h] = send(out_ref.at[b_r, rows], out_ref.at[b_r, rows], ag_sems, t * chunks + h, right)
            sent.append(ag_r[t, h])
            if t < steps_l:
                b_l = lax.rem(me + t, n)
                if t:
                    ag_l[t - 1, h].wait_recv()
                ag_l[t, h] = send(out_ref.at[b_l, rows], out_ref.at[b_l, rows], ag_sems, half + t * chunks + h, left)
                sent.append(ag_l[t, h])
    for h in range(chunks):
        ag_r[steps_r - 1, h].wait_recv()
        ag_l[steps_l - 1, h].wait_recv()
    for c in sent:
        c.wait_send()


def row_ring(partial, n, collective_id, chunks=4):
    blocks, rows, width = partial.shape
    steps_r = n // 2
    steps_l = n - 1 - steps_r
    return pl.pallas_call(
        functools.partial(_ring_kernel, n, chunks),
        out_shape=jax.ShapeDtypeStruct((blocks, rows, width), jnp.bfloat16),
        in_specs=[pl.BlockSpec(memory_space=pltpu.VMEM)],
        out_specs=pl.BlockSpec(memory_space=pltpu.VMEM),
        scratch_shapes=[
            pltpu.VMEM((steps_r, rows, width), jnp.float32),
            pltpu.VMEM((steps_l, rows, width), jnp.float32),
            pltpu.VMEM((steps_r - 1, rows, width), jnp.float32),
            pltpu.VMEM((steps_l - 1, rows, width), jnp.float32),
            pltpu.SemaphoreType.DMA((4 * n * chunks,)),
            pltpu.SemaphoreType.DMA((4 * n * chunks,)),
        ],
        compiler_params=pltpu.CompilerParams(collective_id=collective_id, has_side_effects=True),
    )(partial)


def shards(new_keys, precision, stored_keys, pair_batch, pair_count, batch_length, batch_slot):
    row_count = lax.axis_size("row")
    col_count = lax.axis_size("col")
    row_index = lax.axis_index("row")
    total_keys = new_keys.shape[0] * col_count
    block_keys = total_keys // row_count
    part_keys = block_keys // col_count
    local_batches, batch_keys, width = stored_keys.shape
    gathered = col_gather(new_keys, col_count, 0)
    partial_value = jnp.dot(
        gathered.reshape(total_keys, new_keys.shape[1]),
        precision,
        preferred_element_type=jnp.float32,
    )
    every_row = row_ring(partial_value.reshape(row_count, block_keys, -1), row_count, 3)
    whitened = every_row[row_index]
    rows = every_row.reshape(row_count, col_count, part_keys, width)
    terms = jnp.einsum("bcid,sjd->csbij", rows, stored_keys, preferred_element_type=jnp.float32)
    terms = terms.reshape(col_count, local_batches * row_count * part_keys, batch_keys)
    mine = col_scatter(terms, col_count, 1)
    mine = mine.reshape(local_batches, row_count, part_keys, batch_keys).transpose(1, 0, 2, 3)
    mine = mine.reshape(row_count, local_batches * part_keys, batch_keys)
    routed = exchange(mine, "row", "col", row_count, False, 2)
    table = routed.reshape(row_count * local_batches, part_keys, batch_keys)
    listed = pair_batch[row_index]
    slots = batch_slot[listed]
    lengths = batch_length[listed]
    count = pair_count[row_index]
    picked = jnp.take(table, slots, axis=0)
    places = jnp.arange(slots.shape[0], dtype=jnp.int32)
    columns = jnp.arange(batch_keys, dtype=jnp.int32)
    keep = (places < count)[:, None, None] & (columns[None, None, :] < lengths[:, None, None])
    shares = jnp.where(keep, picked, jnp.zeros_like(picked))
    return (whitened, shares[None])


def solution(mesh):
    placed = (P("col", "row"), P("row", "col"), P("row", None, "col"), P(), P(), P(), P())
    return jax.shard_map(
        shards,
        mesh=mesh,
        in_specs=placed,
        out_specs=(P("row", "col"), P("row", None, "col", None)),
        check_vma=False,
    )
```

```python
import functools

import jax
import jax.numpy as jnp
from jax import lax
from jax.experimental import pallas as pl
from jax.experimental.pallas import tpu as pltpu
from jax.sharding import PartitionSpec as P


def _exchange_kernel(axis, other, n, gather, x_ref, out_ref, send_sems, recv_sems):
    me = lax.axis_index(axis)
    mine = lax.axis_index(other)

    def at(peer):
        return (peer, mine) if axis == "row" else (mine, peer)

    barrier = pltpu.get_barrier_semaphore()
    for d in range(1, n):
        peer = lax.rem(me + d, n)
        pl.semaphore_signal(barrier, inc=1, device_id=at(peer), device_id_type=pl.DeviceIdType.MESH)
    pl.semaphore_wait(barrier, n - 1)
    copies = []
    for d in range(1, n):
        peer = lax.rem(me + d, n)
        src = x_ref if gather else x_ref.at[peer]
        copy = pltpu.make_async_remote_copy(
            src_ref=src, dst_ref=out_ref.at[me], send_sem=send_sems.at[d], recv_sem=recv_sems.at[d],
            device_id=at(peer), device_id_type=pl.DeviceIdType.MESH)
        copy.start()
        copies.append(copy)
    if gather:
        out_ref[me] = x_ref[...]
    else:
        out_ref[me] = x_ref[me]
    for d in range(1, n):
        copies[d - 1].wait_send()
        source = lax.rem(me + n - d, n)
        src = x_ref if gather else x_ref.at[source]
        incoming = pltpu.make_async_remote_copy(
            src_ref=src, dst_ref=out_ref.at[source], send_sem=send_sems.at[d], recv_sem=recv_sems.at[d],
            device_id=at(source), device_id_type=pl.DeviceIdType.MESH)
        incoming.wait_recv()


def exchange(x, axis, other, n, gather, collective_id):
    block = x.shape if gather else x.shape[1:]
    return pl.pallas_call(
        functools.partial(_exchange_kernel, axis, other, n, gather),
        out_shape=jax.ShapeDtypeStruct((n,) + tuple(block), x.dtype),
        in_specs=[pl.BlockSpec(memory_space=pltpu.VMEM)],
        out_specs=pl.BlockSpec(memory_space=pltpu.VMEM),
        scratch_shapes=[pltpu.SemaphoreType.DMA((n,)), pltpu.SemaphoreType.DMA((n,))],
        compiler_params=pltpu.CompilerParams(collective_id=collective_id, has_side_effects=True),
    )(x)


def _gather_kernel(n, x_ref, out_ref, send_sems, forward_sems, recv_sems):
    me = lax.axis_index("col")
    mine = lax.axis_index("row")
    core = lax.rem(me, 2)
    chip = me // 2
    chips = n // 2
    sibling = chip * 2 + 1 - core
    peers = [lax.rem(chip + d, chips) * 2 + core for d in range(1, chips)]
    barrier = pltpu.get_barrier_semaphore()
    for peer in peers + [sibling]:
        pl.semaphore_signal(barrier, inc=1, device_id=(mine, peer), device_id_type=pl.DeviceIdType.MESH)
    pl.semaphore_wait(barrier, chips)

    def copy(src, slot, sem, peer):
        return pltpu.make_async_remote_copy(
            src_ref=src, dst_ref=out_ref.at[slot], send_sem=sem, recv_sem=recv_sems.at[slot],
            device_id=(mine, peer), device_id_type=pl.DeviceIdType.MESH)

    sent = []
    for d, peer in enumerate(peers + [sibling]):
        c = copy(x_ref, me, send_sems.at[d], peer)
        c.start()
        sent.append(c)
    out_ref[me] = x_ref[...]
    for d, peer in enumerate(peers):
        copy(x_ref, peer, send_sems.at[d], peer).wait_recv()
        c = copy(out_ref.at[peer], peer, forward_sems.at[d], sibling)
        c.start()
        sent.append(c)
    copy(x_ref, sibling, send_sems.at[0], sibling).wait_recv()
    for d in range(1, chips):
        far = lax.rem(chip + d, chips) * 2 + 1 - core
        copy(x_ref, far, send_sems.at[0], sibling).wait_recv()
    for c in sent:
        c.wait_send()


def col_gather(x, n, collective_id):
    return pl.pallas_call(
        functools.partial(_gather_kernel, n),
        out_shape=jax.ShapeDtypeStruct((n,) + x.shape, x.dtype),
        in_specs=[pl.BlockSpec(memory_space=pltpu.VMEM)],
        out_specs=pl.BlockSpec(memory_space=pltpu.VMEM),
        scratch_shapes=[
            pltpu.SemaphoreType.DMA((n,)),
            pltpu.SemaphoreType.DMA((n,)),
            pltpu.SemaphoreType.DMA((n,)),
        ],
        compiler_params=pltpu.CompilerParams(collective_id=collective_id, has_side_effects=True),
    )(x)


def _scatter_kernel(n, x_ref, out_ref, half, recv, acc, send_sems, recv_sems):
    me = lax.axis_index("col")
    mine = lax.axis_index("row")
    core = lax.rem(me, 2)
    chip = me // 2
    chips = n // 2
    sibling = chip * 2 + 1 - core
    peers = [lax.rem(chip + d, chips) * 2 + core for d in range(1, chips)]
    barrier = pltpu.get_barrier_semaphore()
    for peer in peers + [sibling]:
        pl.semaphore_signal(barrier, inc=1, device_id=(mine, peer), device_id_type=pl.DeviceIdType.MESH)
    pl.semaphore_wait(barrier, chips)

    swap = pltpu.make_async_remote_copy(
        src_ref=x_ref.at[:, 1 - core], dst_ref=half, send_sem=send_sems.at[0], recv_sem=recv_sems.at[0],
        device_id=(mine, sibling), device_id_type=pl.DeviceIdType.MESH)
    swap.start()
    swap.wait_recv()
    acc[...] = x_ref[:, core] + half[...]
    sent = [swap]
    for d in range(1, chips):
        target = lax.rem(chip + d, chips)
        c = pltpu.make_async_remote_copy(
            src_ref=acc.at[target], dst_ref=recv.at[chip], send_sem=send_sems.at[d], recv_sem=recv_sems.at[d],
            device_id=(mine, target * 2 + core), device_id_type=pl.DeviceIdType.MESH)
        c.start()
        sent.append(c)
    total = acc[chip]
    for d in range(1, chips):
        source = lax.rem(chip + chips - d, chips)
        pltpu.make_async_remote_copy(
            src_ref=acc.at[source], dst_ref=recv.at[source], send_sem=send_sems.at[d], recv_sem=recv_sems.at[d],
            device_id=(mine, source * 2 + core), device_id_type=pl.DeviceIdType.MESH).wait_recv()
        total = total + recv[source]
    out_ref[...] = total
    for c in sent:
        c.wait_send()


def col_scatter(x, n, collective_id):
    chips = n // 2
    block = x.shape[1:]
    return pl.pallas_call(
        functools.partial(_scatter_kernel, n),
        out_shape=jax.ShapeDtypeStruct(block, x.dtype),
        in_specs=[pl.BlockSpec(memory_space=pltpu.VMEM)],
        out_specs=pl.BlockSpec(memory_space=pltpu.VMEM),
        scratch_shapes=[
            pltpu.VMEM((chips,) + block, x.dtype),
            pltpu.VMEM((chips,) + block, x.dtype),
            pltpu.VMEM((chips,) + block, x.dtype),
            pltpu.SemaphoreType.DMA((chips,)),
            pltpu.SemaphoreType.DMA((chips,)),
        ],
        compiler_params=pltpu.CompilerParams(collective_id=collective_id, has_side_effects=True),
    )(x.reshape((chips, 2) + block))


def _route_kernel(x_ref, out_ref, send_buf, send_sems, recv_sems):
    row = lax.axis_index("row")
    col = lax.axis_index("col")
    pairs = x_ref.shape[0] // 2
    rows = lax.axis_size("row")
    block = col // 2
    half = lax.rem(col, 2)
    base = pairs * half
    source_col = 2 * row + col // pairs
    mirrored = (row == block) & (col // pairs == half)

    barrier = pltpu.get_barrier_semaphore()
    for k in range(pairs):
        target = base + k

        @pl.when((block != row) | (target != col))
        def _():
            pl.semaphore_signal(barrier, inc=1, device_id=(block, target), device_id_type=pl.DeviceIdType.MESH)
    for r in range(rows):

        @pl.when((r != row) | (source_col != col))
        def _():
            pl.semaphore_signal(barrier, inc=1, device_id=(r, source_col), device_id_type=pl.DeviceIdType.MESH)

    @pl.when(mirrored)
    def _():
        pl.semaphore_wait(barrier, pairs + rows - 2)

    @pl.when(jnp.logical_not(mirrored))
    def _():
        pl.semaphore_wait(barrier, pairs + rows)

    for k in range(pairs):
        send_buf[k] = x_ref[2 * k:2 * k + 2, :]

    def copy(k, r, device):
        return pltpu.make_async_remote_copy(
            src_ref=send_buf.at[k], dst_ref=out_ref.at[r], send_sem=send_sems.at[k], recv_sem=recv_sems.at[r],
            device_id=device, device_id_type=pl.DeviceIdType.MESH)

    for k in range(pairs):
        target = base + k

        @pl.when((block != row) | (target != col))
        def _():
            copy(k, row, (block, target)).start()

        @pl.when((block == row) & (target == col))
        def _():
            out_ref[row] = send_buf[k]
    for r in range(rows):

        @pl.when((r != row) | (source_col != col))
        def _():
            copy(0, r, (r, source_col)).wait_recv()
    for k in range(pairs):
        target = base + k

        @pl.when((block != row) | (target != col))
        def _():
            copy(k, row, (block, target)).wait_send()


def route(x, rows, collective_id):
    pairs = x.shape[0] // 2
    return pl.pallas_call(
        _route_kernel,
        out_shape=jax.ShapeDtypeStruct((rows, 2, x.shape[1]), x.dtype),
        in_specs=[pl.BlockSpec(memory_space=pltpu.VMEM)],
        out_specs=pl.BlockSpec(memory_space=pltpu.VMEM),
        scratch_shapes=[
            pltpu.VMEM((pairs, 2, x.shape[1]), x.dtype),
            pltpu.SemaphoreType.DMA((pairs,)),
            pltpu.SemaphoreType.DMA((rows,)),
        ],
        compiler_params=pltpu.CompilerParams(collective_id=collective_id, has_side_effects=True),
    )(x)


def _ring_kernel(n, chunks, partial_ref, out_ref, recv_r, recv_l, acc_r, acc_l, rs_sems, ag_sems):
    me = lax.axis_index("row")
    mine = lax.axis_index("col")
    right = lax.rem(me + 1, n)
    left = lax.rem(me + n - 1, n)
    steps_r = n // 2
    steps_l = n - 1 - steps_r
    size = partial_ref.shape[1] // chunks
    half = n * chunks
    barrier = pltpu.get_barrier_semaphore()
    for peer in (left, right):
        pl.semaphore_signal(barrier, inc=1, device_id=(peer, mine), device_id_type=pl.DeviceIdType.MESH)
    pl.semaphore_wait(barrier, 2)

    def send(src, dst, sems, k, peer):
        copy = pltpu.make_async_remote_copy(
            src_ref=src, dst_ref=dst, send_sem=sems.at[k], recv_sem=sems.at[k + 2 * half],
            device_id=(peer, mine), device_id_type=pl.DeviceIdType.MESH)
        copy.start()
        return copy

    sent = []
    got_r = {}
    got_l = {}
    for s in range(steps_r):
        for h in range(chunks):
            rows = pl.ds(h * size, size)
            d_r = lax.rem(me + steps_r - s, n)
            if s == 0:
                src = partial_ref.at[d_r, rows]
            else:
                got_r[s - 1, h].wait_recv()
                acc_r[s - 1, rows] = recv_r[s - 1, rows] + partial_ref[d_r, rows]
                src = acc_r.at[s - 1, rows]
            got_r[s, h] = send(src, recv_r.at[s, rows], rs_sems, s * chunks + h, right)
            sent.append(got_r[s, h])
            if s < steps_l:
                d_l = lax.rem(me + n - steps_l + s, n)
                if s == 0:
                    src = partial_ref.at[d_l, rows]
                else:
                    got_l[s - 1, h].wait_recv()
                    acc_l[s - 1, rows] = recv_l[s - 1, rows] + partial_ref[d_l, rows]
                    src = acc_l.at[s - 1, rows]
                got_l[s, h] = send(src, recv_l.at[s, rows], rs_sems, half + s * chunks + h, left)
                sent.append(got_l[s, h])
    for h in range(chunks):
        rows = pl.ds(h * size, size)
        got_r[steps_r - 1, h].wait_recv()
        got_l[steps_l - 1, h].wait_recv()
        total = partial_ref[me, rows] + recv_r[steps_r - 1, rows] + recv_l[steps_l - 1, rows]
        out_ref[me, rows] = total.astype(out_ref.dtype)

    ag_r = {}
    ag_l = {}
    for t in range(steps_r):
        for h in range(chunks):
            rows = pl.ds(h * size, size)
            b_r = lax.rem(me + n - t, n)
            if t:
                ag_r[t - 1, h].wait_recv()
            ag_r[t, h] = send(out_ref.at[b_r, rows], out_ref.at[b_r, rows], ag_sems, t * chunks + h, right)
            sent.append(ag_r[t, h])
            if t < steps_l:
                b_l = lax.rem(me + t, n)
                if t:
                    ag_l[t - 1, h].wait_recv()
                ag_l[t, h] = send(out_ref.at[b_l, rows], out_ref.at[b_l, rows], ag_sems, half + t * chunks + h, left)
                sent.append(ag_l[t, h])
    for h in range(chunks):
        ag_r[steps_r - 1, h].wait_recv()
        ag_l[steps_l - 1, h].wait_recv()
    for c in sent:
        c.wait_send()


def row_ring(partial, n, collective_id, chunks=2):
    blocks, rows, width = partial.shape
    steps_r = n // 2
    steps_l = n - 1 - steps_r
    return pl.pallas_call(
        functools.partial(_ring_kernel, n, chunks),
        out_shape=jax.ShapeDtypeStruct((blocks, rows, width), jnp.bfloat16),
        in_specs=[pl.BlockSpec(memory_space=pltpu.VMEM)],
        out_specs=pl.BlockSpec(memory_space=pltpu.VMEM),
        scratch_shapes=[
            pltpu.VMEM((steps_r, rows, width), jnp.float32),
            pltpu.VMEM((steps_l, rows, width), jnp.float32),
            pltpu.VMEM((steps_r - 1, rows, width), jnp.float32),
            pltpu.VMEM((steps_l - 1, rows, width), jnp.float32),
            pltpu.SemaphoreType.DMA((4 * n * chunks,)),
            pltpu.SemaphoreType.DMA((4 * n * chunks,)),
        ],
        compiler_params=pltpu.CompilerParams(collective_id=collective_id, has_side_effects=True),
    )(partial)


def shards(new_keys, precision, stored_keys, pair_batch, pair_count, batch_length, batch_slot):
    row_count = lax.axis_size("row")
    col_count = lax.axis_size("col")
    row_index = lax.axis_index("row")
    total_keys = new_keys.shape[0] * col_count
    block_keys = total_keys // row_count
    part_keys = block_keys // col_count
    local_batches, batch_keys, width = stored_keys.shape
    gathered = col_gather(new_keys, col_count, 0)
    partial_value = jnp.dot(
        gathered.reshape(total_keys, new_keys.shape[1]),
        precision,
        preferred_element_type=jnp.float32,
    )
    every_row = row_ring(partial_value.reshape(row_count, block_keys, -1), row_count, 3)
    whitened = every_row[row_index]
    terms = jnp.einsum("brd,sjd->brsj", every_row.reshape(row_count, block_keys, width), stored_keys,
                       preferred_element_type=jnp.float32)
    terms = terms.reshape(col_count, block_keys // 2, local_batches * batch_keys)
    mine = col_scatter(terms, col_count, 1)
    routed = route(mine, row_count, 2)
    table = routed.reshape(row_count, part_keys, local_batches, batch_keys).transpose(0, 2, 1, 3)
    table = table.reshape(row_count * local_batches, part_keys, batch_keys)
    listed = pair_batch[row_index]
    slots = batch_slot[listed]
    lengths = batch_length[listed]
    count = pair_count[row_index]
    picked = jnp.take(table, slots, axis=0)
    places = jnp.arange(slots.shape[0], dtype=jnp.int32)
    columns = jnp.arange(batch_keys, dtype=jnp.int32)
    keep = (places < count)[:, None, None] & (columns[None, None, :] < lengths[:, None, None])
    shares = jnp.where(keep, picked, jnp.zeros_like(picked))
    return (whitened, shares[None])


def solution(mesh):
    placed = (P("col", "row"), P("row", "col"), P("row", None, "col"), P(), P(), P(), P())
    return jax.shard_map(
        shards,
        mesh=mesh,
        in_specs=placed,
        out_specs=(P("row", "col"), P("row", None, "col", None)),
        check_vma=False,
    )
```

```python
import functools

import jax
import jax.numpy as jnp
from jax import lax
from jax.experimental import pallas as pl
from jax.experimental.pallas import tpu as pltpu
from jax.sharding import PartitionSpec as P


def _exchange_kernel(axis, other, n, gather, x_ref, out_ref, send_sems, recv_sems):
    me = lax.axis_index(axis)
    mine = lax.axis_index(other)

    def at(peer):
        return (peer, mine) if axis == "row" else (mine, peer)

    barrier = pltpu.get_barrier_semaphore()
    for d in range(1, n):
        peer = lax.rem(me + d, n)
        pl.semaphore_signal(barrier, inc=1, device_id=at(peer), device_id_type=pl.DeviceIdType.MESH)
    pl.semaphore_wait(barrier, n - 1)
    copies = []
    for d in range(1, n):
        peer = lax.rem(me + d, n)
        src = x_ref if gather else x_ref.at[peer]
        copy = pltpu.make_async_remote_copy(
            src_ref=src, dst_ref=out_ref.at[me], send_sem=send_sems.at[d], recv_sem=recv_sems.at[d],
            device_id=at(peer), device_id_type=pl.DeviceIdType.MESH)
        copy.start()
        copies.append(copy)
    if gather:
        out_ref[me] = x_ref[...]
    else:
        out_ref[me] = x_ref[me]
    for d in range(1, n):
        copies[d - 1].wait_send()
        source = lax.rem(me + n - d, n)
        src = x_ref if gather else x_ref.at[source]
        incoming = pltpu.make_async_remote_copy(
            src_ref=src, dst_ref=out_ref.at[source], send_sem=send_sems.at[d], recv_sem=recv_sems.at[d],
            device_id=at(source), device_id_type=pl.DeviceIdType.MESH)
        incoming.wait_recv()


def exchange(x, axis, other, n, gather, collective_id):
    block = x.shape if gather else x.shape[1:]
    return pl.pallas_call(
        functools.partial(_exchange_kernel, axis, other, n, gather),
        out_shape=jax.ShapeDtypeStruct((n,) + tuple(block), x.dtype),
        in_specs=[pl.BlockSpec(memory_space=pltpu.VMEM)],
        out_specs=pl.BlockSpec(memory_space=pltpu.VMEM),
        scratch_shapes=[pltpu.SemaphoreType.DMA((n,)), pltpu.SemaphoreType.DMA((n,))],
        compiler_params=pltpu.CompilerParams(collective_id=collective_id, has_side_effects=True),
    )(x)


def _gather_kernel(n, x_ref, out_ref, send_sems, forward_sems, recv_sems):
    me = lax.axis_index("col")
    mine = lax.axis_index("row")
    core = lax.rem(me, 2)
    chip = me // 2
    chips = n // 2
    sibling = chip * 2 + 1 - core
    peers = [lax.rem(chip + d, chips) * 2 + core for d in range(1, chips)]
    barrier = pltpu.get_barrier_semaphore()
    for peer in peers + [sibling]:
        pl.semaphore_signal(barrier, inc=1, device_id=(mine, peer), device_id_type=pl.DeviceIdType.MESH)
    pl.semaphore_wait(barrier, chips)

    def copy(src, slot, sem, peer):
        return pltpu.make_async_remote_copy(
            src_ref=src, dst_ref=out_ref.at[slot], send_sem=sem, recv_sem=recv_sems.at[slot],
            device_id=(mine, peer), device_id_type=pl.DeviceIdType.MESH)

    sent = []
    for d, peer in enumerate(peers + [sibling]):
        c = copy(x_ref, me, send_sems.at[d], peer)
        c.start()
        sent.append(c)
    out_ref[me] = x_ref[...]
    for d, peer in enumerate(peers):
        copy(x_ref, peer, send_sems.at[d], peer).wait_recv()
        c = copy(out_ref.at[peer], peer, forward_sems.at[d], sibling)
        c.start()
        sent.append(c)
    copy(x_ref, sibling, send_sems.at[0], sibling).wait_recv()
    for d in range(1, chips):
        far = lax.rem(chip + d, chips) * 2 + 1 - core
        copy(x_ref, far, send_sems.at[0], sibling).wait_recv()
    for c in sent:
        c.wait_send()


def col_gather(x, n, collective_id):
    return pl.pallas_call(
        functools.partial(_gather_kernel, n),
        out_shape=jax.ShapeDtypeStruct((n,) + x.shape, x.dtype),
        in_specs=[pl.BlockSpec(memory_space=pltpu.VMEM)],
        out_specs=pl.BlockSpec(memory_space=pltpu.VMEM),
        scratch_shapes=[
            pltpu.SemaphoreType.DMA((n,)),
            pltpu.SemaphoreType.DMA((n,)),
            pltpu.SemaphoreType.DMA((n,)),
        ],
        compiler_params=pltpu.CompilerParams(collective_id=collective_id, has_side_effects=True),
    )(x)


def _scatter_kernel(n, x_ref, out_ref, half, recv, acc, send_sems, recv_sems):
    me = lax.axis_index("col")
    mine = lax.axis_index("row")
    core = lax.rem(me, 2)
    chip = me // 2
    chips = n // 2
    sibling = chip * 2 + 1 - core
    peers = [lax.rem(chip + d, chips) * 2 + core for d in range(1, chips)]
    barrier = pltpu.get_barrier_semaphore()
    for peer in peers + [sibling]:
        pl.semaphore_signal(barrier, inc=1, device_id=(mine, peer), device_id_type=pl.DeviceIdType.MESH)
    pl.semaphore_wait(barrier, chips)

    swap = pltpu.make_async_remote_copy(
        src_ref=x_ref.at[:, 1 - core], dst_ref=half, send_sem=send_sems.at[0], recv_sem=recv_sems.at[0],
        device_id=(mine, sibling), device_id_type=pl.DeviceIdType.MESH)
    swap.start()
    swap.wait_recv()
    acc[...] = x_ref[:, core] + half[...]
    sent = [swap]
    for d in range(1, chips):
        target = lax.rem(chip + d, chips)
        c = pltpu.make_async_remote_copy(
            src_ref=acc.at[target], dst_ref=recv.at[chip], send_sem=send_sems.at[d], recv_sem=recv_sems.at[d],
            device_id=(mine, target * 2 + core), device_id_type=pl.DeviceIdType.MESH)
        c.start()
        sent.append(c)
    total = acc[chip]
    for d in range(1, chips):
        source = lax.rem(chip + chips - d, chips)
        pltpu.make_async_remote_copy(
            src_ref=acc.at[source], dst_ref=recv.at[source], send_sem=send_sems.at[d], recv_sem=recv_sems.at[d],
            device_id=(mine, source * 2 + core), device_id_type=pl.DeviceIdType.MESH).wait_recv()
        total = total + recv[source]
    out_ref[...] = total
    for c in sent:
        c.wait_send()


def col_scatter(x, n, collective_id):
    chips = n // 2
    block = x.shape[1:]
    return pl.pallas_call(
        functools.partial(_scatter_kernel, n),
        out_shape=jax.ShapeDtypeStruct(block, x.dtype),
        in_specs=[pl.BlockSpec(memory_space=pltpu.VMEM)],
        out_specs=pl.BlockSpec(memory_space=pltpu.VMEM),
        scratch_shapes=[
            pltpu.VMEM((chips,) + block, x.dtype),
            pltpu.VMEM((chips,) + block, x.dtype),
            pltpu.VMEM((chips,) + block, x.dtype),
            pltpu.SemaphoreType.DMA((chips,)),
            pltpu.SemaphoreType.DMA((chips,)),
        ],
        compiler_params=pltpu.CompilerParams(collective_id=collective_id, has_side_effects=True),
    )(x.reshape((chips, 2) + block))


def _route_kernel(x_ref, out_ref, send_buf, send_sems, recv_sems):
    row = lax.axis_index("row")
    col = lax.axis_index("col")
    pairs = x_ref.shape[0] // 2
    rows = lax.axis_size("row")
    block = col // 2
    half = lax.rem(col, 2)
    base = pairs * half
    source_col = 2 * row + col // pairs
    mirrored = (row == block) & (col // pairs == half)

    barrier = pltpu.get_barrier_semaphore()
    for k in range(pairs):
        target = base + k

        @pl.when((block != row) | (target != col))
        def _():
            pl.semaphore_signal(barrier, inc=1, device_id=(block, target), device_id_type=pl.DeviceIdType.MESH)
    for r in range(rows):

        @pl.when((r != row) | (source_col != col))
        def _():
            pl.semaphore_signal(barrier, inc=1, device_id=(r, source_col), device_id_type=pl.DeviceIdType.MESH)

    @pl.when(mirrored)
    def _():
        pl.semaphore_wait(barrier, pairs + rows - 2)

    @pl.when(jnp.logical_not(mirrored))
    def _():
        pl.semaphore_wait(barrier, pairs + rows)

    for k in range(pairs):
        send_buf[k] = x_ref[2 * k:2 * k + 2, :]

    def copy(k, r, device):
        return pltpu.make_async_remote_copy(
            src_ref=send_buf.at[k], dst_ref=out_ref.at[r], send_sem=send_sems.at[k], recv_sem=recv_sems.at[r],
            device_id=device, device_id_type=pl.DeviceIdType.MESH)

    for k in range(pairs):
        target = base + k

        @pl.when((block != row) | (target != col))
        def _():
            copy(k, row, (block, target)).start()

        @pl.when((block == row) & (target == col))
        def _():
            out_ref[row] = send_buf[k]
    for r in range(rows):

        @pl.when((r != row) | (source_col != col))
        def _():
            copy(0, r, (r, source_col)).wait_recv()
    for k in range(pairs):
        target = base + k

        @pl.when((block != row) | (target != col))
        def _():
            copy(k, row, (block, target)).wait_send()


def route(x, rows, collective_id):
    pairs = x.shape[0] // 2
    return pl.pallas_call(
        _route_kernel,
        out_shape=jax.ShapeDtypeStruct((rows, 2, x.shape[1]), x.dtype),
        in_specs=[pl.BlockSpec(memory_space=pltpu.VMEM)],
        out_specs=pl.BlockSpec(memory_space=pltpu.VMEM),
        scratch_shapes=[
            pltpu.VMEM((pairs, 2, x.shape[1]), x.dtype),
            pltpu.SemaphoreType.DMA((pairs,)),
            pltpu.SemaphoreType.DMA((rows,)),
        ],
        compiler_params=pltpu.CompilerParams(collective_id=collective_id, has_side_effects=True),
    )(x)


def _ring_kernel(n, chunks, partial_ref, out_ref, recv_r, recv_l, acc_r, acc_l, rs_sems, ag_sems):
    me = lax.axis_index("row")
    mine = lax.axis_index("col")
    right = lax.rem(me + 1, n)
    left = lax.rem(me + n - 1, n)
    steps_r = n // 2
    steps_l = n - 1 - steps_r
    size = partial_ref.shape[1] // chunks
    half = n * chunks
    barrier = pltpu.get_barrier_semaphore()
    for peer in (left, right):
        pl.semaphore_signal(barrier, inc=1, device_id=(peer, mine), device_id_type=pl.DeviceIdType.MESH)
    pl.semaphore_wait(barrier, 2)

    def send(src, dst, sems, k, peer):
        copy = pltpu.make_async_remote_copy(
            src_ref=src, dst_ref=dst, send_sem=sems.at[k], recv_sem=sems.at[k + 2 * half],
            device_id=(peer, mine), device_id_type=pl.DeviceIdType.MESH)
        copy.start()
        return copy

    sent = []
    got_r = {}
    got_l = {}
    for s in range(steps_r):
        for h in range(chunks):
            rows = pl.ds(h * size, size)
            d_r = lax.rem(me + steps_r - s, n)
            if s == 0:
                src = partial_ref.at[d_r, rows]
            else:
                got_r[s - 1, h].wait_recv()
                acc_r[s - 1, rows] = recv_r[s - 1, rows] + partial_ref[d_r, rows]
                src = acc_r.at[s - 1, rows]
            got_r[s, h] = send(src, recv_r.at[s, rows], rs_sems, s * chunks + h, right)
            sent.append(got_r[s, h])
            if s < steps_l:
                d_l = lax.rem(me + n - steps_l + s, n)
                if s == 0:
                    src = partial_ref.at[d_l, rows]
                else:
                    got_l[s - 1, h].wait_recv()
                    acc_l[s - 1, rows] = recv_l[s - 1, rows] + partial_ref[d_l, rows]
                    src = acc_l.at[s - 1, rows]
                got_l[s, h] = send(src, recv_l.at[s, rows], rs_sems, half + s * chunks + h, left)
                sent.append(got_l[s, h])
    for h in range(chunks):
        rows = pl.ds(h * size, size)
        got_r[steps_r - 1, h].wait_recv()
        got_l[steps_l - 1, h].wait_recv()
        total = partial_ref[me, rows] + recv_r[steps_r - 1, rows] + recv_l[steps_l - 1, rows]
        out_ref[me, rows] = total.astype(out_ref.dtype)

    ag_r = {}
    ag_l = {}
    for t in range(steps_r):
        for h in range(chunks):
            rows = pl.ds(h * size, size)
            b_r = lax.rem(me + n - t, n)
            if t:
                ag_r[t - 1, h].wait_recv()
            ag_r[t, h] = send(out_ref.at[b_r, rows], out_ref.at[b_r, rows], ag_sems, t * chunks + h, right)
            sent.append(ag_r[t, h])
            if t < steps_l:
                b_l = lax.rem(me + t, n)
                if t:
                    ag_l[t - 1, h].wait_recv()
                ag_l[t, h] = send(out_ref.at[b_l, rows], out_ref.at[b_l, rows], ag_sems, half + t * chunks + h, left)
                sent.append(ag_l[t, h])
    for h in range(chunks):
        ag_r[steps_r - 1, h].wait_recv()
        ag_l[steps_l - 1, h].wait_recv()
    for c in sent:
        c.wait_send()


def row_ring(partial, n, collective_id, chunks=2):
    blocks, rows, width = partial.shape
    steps_r = n // 2
    steps_l = n - 1 - steps_r
    return pl.pallas_call(
        functools.partial(_ring_kernel, n, chunks),
        out_shape=jax.ShapeDtypeStruct((blocks, rows, width), jnp.bfloat16),
        in_specs=[pl.BlockSpec(memory_space=pltpu.VMEM)],
        out_specs=pl.BlockSpec(memory_space=pltpu.VMEM),
        scratch_shapes=[
            pltpu.VMEM((steps_r, rows, width), jnp.float32),
            pltpu.VMEM((steps_l, rows, width), jnp.float32),
            pltpu.VMEM((steps_r - 1, rows, width), jnp.float32),
            pltpu.VMEM((steps_l - 1, rows, width), jnp.float32),
            pltpu.SemaphoreType.DMA((4 * n * chunks,)),
            pltpu.SemaphoreType.DMA((4 * n * chunks,)),
        ],
        compiler_params=pltpu.CompilerParams(collective_id=collective_id, has_side_effects=True),
    )(partial)


def shards(new_keys, precision, stored_keys, pair_batch, pair_count, batch_length, batch_slot):
    row_count = lax.axis_size("row")
    col_count = lax.axis_size("col")
    row_index = lax.axis_index("row")
    total_keys = new_keys.shape[0] * col_count
    block_keys = total_keys // row_count
    part_keys = block_keys // col_count
    local_batches, batch_keys, width = stored_keys.shape
    gathered = col_gather(new_keys, col_count, 0)
    partial_value = jnp.dot(
        gathered.reshape(total_keys, new_keys.shape[1]),
        precision,
        preferred_element_type=jnp.float32,
    )
    every_row = row_ring(partial_value.reshape(row_count, block_keys, -1), row_count, 3)
    whitened = every_row[row_index]
    terms = jnp.einsum("brd,kd->brk", every_row.reshape(row_count, block_keys, width),
                       stored_keys.reshape(local_batches * batch_keys, width), preferred_element_type=jnp.float32)
    terms = terms.reshape(col_count, block_keys // 2, local_batches * batch_keys)
    mine = col_scatter(terms, col_count, 1)
    routed = route(mine, row_count, 2)
    table = routed.reshape(row_count, part_keys, local_batches, batch_keys).transpose(0, 2, 1, 3)
    table = table.reshape(row_count * local_batches, part_keys, batch_keys)
    listed = pair_batch[row_index]
    slots = batch_slot[listed]
    lengths = batch_length[listed]
    count = pair_count[row_index]
    picked = jnp.take(table, slots, axis=0)
    places = jnp.arange(slots.shape[0], dtype=jnp.int32)
    columns = jnp.arange(batch_keys, dtype=jnp.int32)
    keep = (places < count)[:, None, None] & (columns[None, None, :] < lengths[:, None, None])
    shares = jnp.where(keep, picked, jnp.zeros_like(picked))
    return (whitened, shares[None])


def solution(mesh):
    placed = (P("col", "row"), P("row", "col"), P("row", None, "col"), P(), P(), P(), P())
    return jax.shard_map(
        shards,
        mesh=mesh,
        in_specs=placed,
        out_specs=(P("row", "col"), P("row", None, "col", None)),
        check_vma=False,
    )
```

```python
import functools

import jax
import jax.numpy as jnp
from jax import lax
from jax.experimental import pallas as pl
from jax.experimental.pallas import tpu as pltpu
from jax.sharding import PartitionSpec as P


def _exchange_kernel(axis, other, n, gather, x_ref, out_ref, send_sems, recv_sems):
    me = lax.axis_index(axis)
    mine = lax.axis_index(other)

    def at(peer):
        return (peer, mine) if axis == "row" else (mine, peer)

    barrier = pltpu.get_barrier_semaphore()
    for d in range(1, n):
        peer = lax.rem(me + d, n)
        pl.semaphore_signal(barrier, inc=1, device_id=at(peer), device_id_type=pl.DeviceIdType.MESH)
    pl.semaphore_wait(barrier, n - 1)
    copies = []
    for d in range(1, n):
        peer = lax.rem(me + d, n)
        src = x_ref if gather else x_ref.at[peer]
        copy = pltpu.make_async_remote_copy(
            src_ref=src, dst_ref=out_ref.at[me], send_sem=send_sems.at[d], recv_sem=recv_sems.at[d],
            device_id=at(peer), device_id_type=pl.DeviceIdType.MESH)
        copy.start()
        copies.append(copy)
    if gather:
        out_ref[me] = x_ref[...]
    else:
        out_ref[me] = x_ref[me]
    for d in range(1, n):
        copies[d - 1].wait_send()
        source = lax.rem(me + n - d, n)
        src = x_ref if gather else x_ref.at[source]
        incoming = pltpu.make_async_remote_copy(
            src_ref=src, dst_ref=out_ref.at[source], send_sem=send_sems.at[d], recv_sem=recv_sems.at[d],
            device_id=at(source), device_id_type=pl.DeviceIdType.MESH)
        incoming.wait_recv()


def exchange(x, axis, other, n, gather, collective_id):
    block = x.shape if gather else x.shape[1:]
    return pl.pallas_call(
        functools.partial(_exchange_kernel, axis, other, n, gather),
        out_shape=jax.ShapeDtypeStruct((n,) + tuple(block), x.dtype),
        in_specs=[pl.BlockSpec(memory_space=pltpu.VMEM)],
        out_specs=pl.BlockSpec(memory_space=pltpu.VMEM),
        scratch_shapes=[pltpu.SemaphoreType.DMA((n,)), pltpu.SemaphoreType.DMA((n,))],
        compiler_params=pltpu.CompilerParams(collective_id=collective_id, has_side_effects=True),
    )(x)


def _gather_kernel(n, x_ref, out_ref, send_sems, forward_sems, recv_sems):
    me = lax.axis_index("col")
    mine = lax.axis_index("row")
    core = lax.rem(me, 2)
    chip = me // 2
    chips = n // 2
    sibling = chip * 2 + 1 - core
    peers = [lax.rem(chip + d, chips) * 2 + core for d in range(1, chips)]
    barrier = pltpu.get_barrier_semaphore()
    for peer in peers + [sibling]:
        pl.semaphore_signal(barrier, inc=1, device_id=(mine, peer), device_id_type=pl.DeviceIdType.MESH)
    pl.semaphore_wait(barrier, chips)

    def copy(src, slot, sem, peer):
        return pltpu.make_async_remote_copy(
            src_ref=src, dst_ref=out_ref.at[slot], send_sem=sem, recv_sem=recv_sems.at[slot],
            device_id=(mine, peer), device_id_type=pl.DeviceIdType.MESH)

    sent = []
    for d, peer in enumerate(peers + [sibling]):
        c = copy(x_ref, me, send_sems.at[d], peer)
        c.start()
        sent.append(c)
    out_ref[me] = x_ref[...]
    for d, peer in enumerate(peers):
        copy(x_ref, peer, send_sems.at[d], peer).wait_recv()
        c = copy(out_ref.at[peer], peer, forward_sems.at[d], sibling)
        c.start()
        sent.append(c)
    copy(x_ref, sibling, send_sems.at[0], sibling).wait_recv()
    for d in range(1, chips):
        far = lax.rem(chip + d, chips) * 2 + 1 - core
        copy(x_ref, far, send_sems.at[0], sibling).wait_recv()
    for c in sent:
        c.wait_send()


def col_gather(x, n, collective_id):
    return pl.pallas_call(
        functools.partial(_gather_kernel, n),
        out_shape=jax.ShapeDtypeStruct((n,) + x.shape, x.dtype),
        in_specs=[pl.BlockSpec(memory_space=pltpu.VMEM)],
        out_specs=pl.BlockSpec(memory_space=pltpu.VMEM),
        scratch_shapes=[
            pltpu.SemaphoreType.DMA((n,)),
            pltpu.SemaphoreType.DMA((n,)),
            pltpu.SemaphoreType.DMA((n,)),
        ],
        compiler_params=pltpu.CompilerParams(collective_id=collective_id, has_side_effects=True),
    )(x)


def _scatter_kernel(n, x_ref, out_ref, half, recv, acc, send_sems, recv_sems):
    me = lax.axis_index("col")
    mine = lax.axis_index("row")
    core = lax.rem(me, 2)
    chip = me // 2
    chips = n // 2
    sibling = chip * 2 + 1 - core
    peers = [lax.rem(chip + d, chips) * 2 + core for d in range(1, chips)]
    barrier = pltpu.get_barrier_semaphore()
    for peer in peers + [sibling]:
        pl.semaphore_signal(barrier, inc=1, device_id=(mine, peer), device_id_type=pl.DeviceIdType.MESH)
    pl.semaphore_wait(barrier, chips)

    swap = pltpu.make_async_remote_copy(
        src_ref=x_ref.at[:, 1 - core], dst_ref=half, send_sem=send_sems.at[0], recv_sem=recv_sems.at[0],
        device_id=(mine, sibling), device_id_type=pl.DeviceIdType.MESH)
    swap.start()
    swap.wait_recv()
    acc[...] = x_ref[:, core] + half[...]
    sent = [swap]
    for d in range(1, chips):
        target = lax.rem(chip + d, chips)
        c = pltpu.make_async_remote_copy(
            src_ref=acc.at[target], dst_ref=recv.at[chip], send_sem=send_sems.at[d], recv_sem=recv_sems.at[d],
            device_id=(mine, target * 2 + core), device_id_type=pl.DeviceIdType.MESH)
        c.start()
        sent.append(c)
    total = acc[chip]
    for d in range(1, chips):
        source = lax.rem(chip + chips - d, chips)
        pltpu.make_async_remote_copy(
            src_ref=acc.at[source], dst_ref=recv.at[source], send_sem=send_sems.at[d], recv_sem=recv_sems.at[d],
            device_id=(mine, source * 2 + core), device_id_type=pl.DeviceIdType.MESH).wait_recv()
        total = total + recv[source]
    out_ref[...] = total
    for c in sent:
        c.wait_send()


def col_scatter(x, n, collective_id):
    chips = n // 2
    block = x.shape[1:]
    return pl.pallas_call(
        functools.partial(_scatter_kernel, n),
        out_shape=jax.ShapeDtypeStruct(block, x.dtype),
        in_specs=[pl.BlockSpec(memory_space=pltpu.VMEM)],
        out_specs=pl.BlockSpec(memory_space=pltpu.VMEM),
        scratch_shapes=[
            pltpu.VMEM((chips,) + block, x.dtype),
            pltpu.VMEM((chips,) + block, x.dtype),
            pltpu.VMEM((chips,) + block, x.dtype),
            pltpu.SemaphoreType.DMA((chips,)),
            pltpu.SemaphoreType.DMA((chips,)),
        ],
        compiler_params=pltpu.CompilerParams(collective_id=collective_id, has_side_effects=True),
    )(x.reshape((chips, 2) + block))


def _route_kernel(x_ref, out_ref, send_buf, send_sems, recv_sems):
    row = lax.axis_index("row")
    col = lax.axis_index("col")
    pairs = x_ref.shape[0] // 2
    rows = lax.axis_size("row")
    block = col // 2
    half = lax.rem(col, 2)
    base = pairs * half
    source_col = 2 * row + col // pairs
    mirrored = (row == block) & (col // pairs == half)

    barrier = pltpu.get_barrier_semaphore()
    for k in range(pairs):
        target = base + k

        @pl.when((block != row) | (target != col))
        def _():
            pl.semaphore_signal(barrier, inc=1, device_id=(block, target), device_id_type=pl.DeviceIdType.MESH)
    for r in range(rows):

        @pl.when((r != row) | (source_col != col))
        def _():
            pl.semaphore_signal(barrier, inc=1, device_id=(r, source_col), device_id_type=pl.DeviceIdType.MESH)

    @pl.when(mirrored)
    def _():
        pl.semaphore_wait(barrier, pairs + rows - 2)

    @pl.when(jnp.logical_not(mirrored))
    def _():
        pl.semaphore_wait(barrier, pairs + rows)

    for k in range(pairs):
        send_buf[k] = x_ref[2 * k:2 * k + 2, :]

    def copy(k, r, device):
        return pltpu.make_async_remote_copy(
            src_ref=send_buf.at[k], dst_ref=out_ref.at[r], send_sem=send_sems.at[k], recv_sem=recv_sems.at[r],
            device_id=device, device_id_type=pl.DeviceIdType.MESH)

    for k in range(pairs):
        target = base + k

        @pl.when((block != row) | (target != col))
        def _():
            copy(k, row, (block, target)).start()

        @pl.when((block == row) & (target == col))
        def _():
            out_ref[row] = send_buf[k]
    for r in range(rows):

        @pl.when((r != row) | (source_col != col))
        def _():
            copy(0, r, (r, source_col)).wait_recv()
    for k in range(pairs):
        target = base + k

        @pl.when((block != row) | (target != col))
        def _():
            copy(k, row, (block, target)).wait_send()


def route(x, rows, collective_id):
    pairs = x.shape[0] // 2
    return pl.pallas_call(
        _route_kernel,
        out_shape=jax.ShapeDtypeStruct((rows, 2, x.shape[1]), x.dtype),
        in_specs=[pl.BlockSpec(memory_space=pltpu.VMEM)],
        out_specs=pl.BlockSpec(memory_space=pltpu.VMEM),
        scratch_shapes=[
            pltpu.VMEM((pairs, 2, x.shape[1]), x.dtype),
            pltpu.SemaphoreType.DMA((pairs,)),
            pltpu.SemaphoreType.DMA((rows,)),
        ],
        compiler_params=pltpu.CompilerParams(collective_id=collective_id, has_side_effects=True),
    )(x)


def _scatter_route_kernel(n, x_ref, out_ref, half_ref, recv, acc, summed, send_buf, send_sems, recv_sems,
                          route_send, route_recv):
    me = lax.axis_index("col")
    row = lax.axis_index("row")
    rows = lax.axis_size("row")
    core = lax.rem(me, 2)
    chip = me // 2
    chips = n // 2
    pairs = summed.shape[0] // 2
    sibling = chip * 2 + 1 - core
    peers = [lax.rem(chip + d, chips) * 2 + core for d in range(1, chips)]
    block = me // 2
    base = pairs * core
    source_col = 2 * row + me // pairs
    mirrored = (row == block) & (me // pairs == core)

    barrier = pltpu.get_barrier_semaphore()
    for peer in peers + [sibling]:
        pl.semaphore_signal(barrier, inc=1, device_id=(row, peer), device_id_type=pl.DeviceIdType.MESH)
    for k in range(pairs):
        target = base + k

        @pl.when((block != row) | (target != me))
        def _():
            pl.semaphore_signal(barrier, inc=1, device_id=(block, target), device_id_type=pl.DeviceIdType.MESH)
    for r in range(rows):

        @pl.when((r != row) | (source_col != me))
        def _():
            pl.semaphore_signal(barrier, inc=1, device_id=(r, source_col), device_id_type=pl.DeviceIdType.MESH)

    @pl.when(mirrored)
    def _():
        pl.semaphore_wait(barrier, chips + pairs + rows - 2)

    @pl.when(jnp.logical_not(mirrored))
    def _():
        pl.semaphore_wait(barrier, chips + pairs + rows)

    swap = pltpu.make_async_remote_copy(
        src_ref=x_ref.at[:, 1 - core], dst_ref=half_ref, send_sem=send_sems.at[0], recv_sem=recv_sems.at[0],
        device_id=(row, sibling), device_id_type=pl.DeviceIdType.MESH)
    swap.start()
    swap.wait_recv()
    acc[...] = x_ref[:, core] + half_ref[...]
    sent = [swap]
    for d in range(1, chips):
        target = lax.rem(chip + d, chips)
        c = pltpu.make_async_remote_copy(
            src_ref=acc.at[target], dst_ref=recv.at[chip], send_sem=send_sems.at[d], recv_sem=recv_sems.at[d],
            device_id=(row, target * 2 + core), device_id_type=pl.DeviceIdType.MESH)
        c.start()
        sent.append(c)
    total = acc[chip]
    for d in range(1, chips):
        source = lax.rem(chip + chips - d, chips)
        pltpu.make_async_remote_copy(
            src_ref=acc.at[source], dst_ref=recv.at[source], send_sem=send_sems.at[d], recv_sem=recv_sems.at[d],
            device_id=(row, source * 2 + core), device_id_type=pl.DeviceIdType.MESH).wait_recv()
        total = total + recv[source]
    summed[...] = total
    for k in range(pairs):
        send_buf[k] = summed[2 * k:2 * k + 2, :]

    def copy(k, r, device):
        return pltpu.make_async_remote_copy(
            src_ref=send_buf.at[k], dst_ref=out_ref.at[r], send_sem=route_send.at[k], recv_sem=route_recv.at[r],
            device_id=device, device_id_type=pl.DeviceIdType.MESH)

    for k in range(pairs):
        target = base + k

        @pl.when((block != row) | (target != me))
        def _():
            copy(k, row, (block, target)).start()

        @pl.when((block == row) & (target == me))
        def _():
            out_ref[row] = send_buf[k]
    for r in range(rows):

        @pl.when((r != row) | (source_col != me))
        def _():
            copy(0, r, (r, source_col)).wait_recv()
    for k in range(pairs):
        target = base + k

        @pl.when((block != row) | (target != me))
        def _():
            copy(k, row, (block, target)).wait_send()
    for c in sent:
        c.wait_send()


def scatter_route(x, n, rows, collective_id):
    chips = n // 2
    block = x.shape[1:]
    pairs = block[0] // 2
    return pl.pallas_call(
        functools.partial(_scatter_route_kernel, n),
        out_shape=jax.ShapeDtypeStruct((rows, 2, block[1]), x.dtype),
        in_specs=[pl.BlockSpec(memory_space=pltpu.VMEM)],
        out_specs=pl.BlockSpec(memory_space=pltpu.VMEM),
        scratch_shapes=[
            pltpu.VMEM((chips,) + block, x.dtype),
            pltpu.VMEM((chips,) + block, x.dtype),
            pltpu.VMEM((chips,) + block, x.dtype),
            pltpu.VMEM(block, x.dtype),
            pltpu.VMEM((pairs, 2, block[1]), x.dtype),
            pltpu.SemaphoreType.DMA((chips,)),
            pltpu.SemaphoreType.DMA((chips,)),
            pltpu.SemaphoreType.DMA((pairs,)),
            pltpu.SemaphoreType.DMA((rows,)),
        ],
        compiler_params=pltpu.CompilerParams(collective_id=collective_id, has_side_effects=True),
    )(x.reshape((chips, 2) + block))


def _ring_kernel(n, chunks, partial_ref, out_ref, recv_r, recv_l, acc_r, acc_l, rs_sems, ag_sems):
    me = lax.axis_index("row")
    mine = lax.axis_index("col")
    right = lax.rem(me + 1, n)
    left = lax.rem(me + n - 1, n)
    steps_r = n // 2
    steps_l = n - 1 - steps_r
    size = partial_ref.shape[1] // chunks
    half = n * chunks
    barrier = pltpu.get_barrier_semaphore()
    for peer in (left, right):
        pl.semaphore_signal(barrier, inc=1, device_id=(peer, mine), device_id_type=pl.DeviceIdType.MESH)
    pl.semaphore_wait(barrier, 2)

    def send(src, dst, sems, k, peer):
        copy = pltpu.make_async_remote_copy(
            src_ref=src, dst_ref=dst, send_sem=sems.at[k], recv_sem=sems.at[k + 2 * half],
            device_id=(peer, mine), device_id_type=pl.DeviceIdType.MESH)
        copy.start()
        return copy

    sent = []
    got_r = {}
    got_l = {}
    for s in range(steps_r):
        for h in range(chunks):
            rows = pl.ds(h * size, size)
            d_r = lax.rem(me + steps_r - s, n)
            if s == 0:
                src = partial_ref.at[d_r, rows]
            else:
                got_r[s - 1, h].wait_recv()
                acc_r[s - 1, rows] = recv_r[s - 1, rows] + partial_ref[d_r, rows]
                src = acc_r.at[s - 1, rows]
            got_r[s, h] = send(src, recv_r.at[s, rows], rs_sems, s * chunks + h, right)
            sent.append(got_r[s, h])
            if s < steps_l:
                d_l = lax.rem(me + n - steps_l + s, n)
                if s == 0:
                    src = partial_ref.at[d_l, rows]
                else:
                    got_l[s - 1, h].wait_recv()
                    acc_l[s - 1, rows] = recv_l[s - 1, rows] + partial_ref[d_l, rows]
                    src = acc_l.at[s - 1, rows]
                got_l[s, h] = send(src, recv_l.at[s, rows], rs_sems, half + s * chunks + h, left)
                sent.append(got_l[s, h])
    for h in range(chunks):
        rows = pl.ds(h * size, size)
        got_r[steps_r - 1, h].wait_recv()
        got_l[steps_l - 1, h].wait_recv()
        total = partial_ref[me, rows] + recv_r[steps_r - 1, rows] + recv_l[steps_l - 1, rows]
        out_ref[me, rows] = total.astype(out_ref.dtype)

    ag_r = {}
    ag_l = {}
    for t in range(steps_r):
        for h in range(chunks):
            rows = pl.ds(h * size, size)
            b_r = lax.rem(me + n - t, n)
            if t:
                ag_r[t - 1, h].wait_recv()
            ag_r[t, h] = send(out_ref.at[b_r, rows], out_ref.at[b_r, rows], ag_sems, t * chunks + h, right)
            sent.append(ag_r[t, h])
            if t < steps_l:
                b_l = lax.rem(me + t, n)
                if t:
                    ag_l[t - 1, h].wait_recv()
                ag_l[t, h] = send(out_ref.at[b_l, rows], out_ref.at[b_l, rows], ag_sems, half + t * chunks + h, left)
                sent.append(ag_l[t, h])
    for h in range(chunks):
        ag_r[steps_r - 1, h].wait_recv()
        ag_l[steps_l - 1, h].wait_recv()
    for c in sent:
        c.wait_send()


def row_ring(partial, n, collective_id, chunks=2):
    blocks, rows, width = partial.shape
    steps_r = n // 2
    steps_l = n - 1 - steps_r
    return pl.pallas_call(
        functools.partial(_ring_kernel, n, chunks),
        out_shape=jax.ShapeDtypeStruct((blocks, rows, width), jnp.bfloat16),
        in_specs=[pl.BlockSpec(memory_space=pltpu.VMEM)],
        out_specs=pl.BlockSpec(memory_space=pltpu.VMEM),
        scratch_shapes=[
            pltpu.VMEM((steps_r, rows, width), jnp.float32),
            pltpu.VMEM((steps_l, rows, width), jnp.float32),
            pltpu.VMEM((steps_r - 1, rows, width), jnp.float32),
            pltpu.VMEM((steps_l - 1, rows, width), jnp.float32),
            pltpu.SemaphoreType.DMA((4 * n * chunks,)),
            pltpu.SemaphoreType.DMA((4 * n * chunks,)),
        ],
        compiler_params=pltpu.CompilerParams(collective_id=collective_id, has_side_effects=True),
    )(partial)


def shards(new_keys, precision, stored_keys, pair_batch, pair_count, batch_length, batch_slot):
    row_count = lax.axis_size("row")
    col_count = lax.axis_size("col")
    row_index = lax.axis_index("row")
    total_keys = new_keys.shape[0] * col_count
    block_keys = total_keys // row_count
    part_keys = block_keys // col_count
    local_batches, batch_keys, width = stored_keys.shape
    gathered = col_gather(new_keys, col_count, 0)
    partial_value = jnp.dot(
        gathered.reshape(total_keys, new_keys.shape[1]),
        precision,
        preferred_element_type=jnp.float32,
    )
    every_row = row_ring(partial_value.reshape(row_count, block_keys, -1), row_count, 3)
    whitened = every_row[row_index]
    terms = jnp.einsum("brd,kd->brk", every_row.reshape(row_count, block_keys, width),
                       stored_keys.reshape(local_batches * batch_keys, width), preferred_element_type=jnp.float32)
    terms = terms.reshape(col_count, block_keys // 2, local_batches * batch_keys)
    routed = scatter_route(terms, col_count, row_count, 1)
    table = routed.reshape(row_count, part_keys, local_batches, batch_keys).transpose(0, 2, 1, 3)
    table = table.reshape(row_count * local_batches, part_keys, batch_keys)
    listed = pair_batch[row_index]
    slots = batch_slot[listed]
    lengths = batch_length[listed]
    count = pair_count[row_index]
    picked = jnp.take(table, slots, axis=0)
    places = jnp.arange(slots.shape[0], dtype=jnp.int32)
    columns = jnp.arange(batch_keys, dtype=jnp.int32)
    keep = (places < count)[:, None, None] & (columns[None, None, :] < lengths[:, None, None])
    shares = jnp.where(keep, picked, jnp.zeros_like(picked))
    return (whitened, shares[None])


def solution(mesh):
    placed = (P("col", "row"), P("row", "col"), P("row", None, "col"), P(), P(), P(), P())
    return jax.shard_map(
        shards,
        mesh=mesh,
        in_specs=placed,
        out_specs=(P("row", "col"), P("row", None, "col", None)),
        check_vma=False,
    )
```

```python
import functools

import jax
import jax.numpy as jnp
from jax import lax
from jax.experimental import pallas as pl
from jax.experimental.pallas import tpu as pltpu
from jax.sharding import PartitionSpec as P


def _exchange_kernel(axis, other, n, gather, x_ref, out_ref, send_sems, recv_sems):
    me = lax.axis_index(axis)
    mine = lax.axis_index(other)

    def at(peer):
        return (peer, mine) if axis == "row" else (mine, peer)

    barrier = pltpu.get_barrier_semaphore()
    for d in range(1, n):
        peer = lax.rem(me + d, n)
        pl.semaphore_signal(barrier, inc=1, device_id=at(peer), device_id_type=pl.DeviceIdType.MESH)
    pl.semaphore_wait(barrier, n - 1)
    copies = []
    for d in range(1, n):
        peer = lax.rem(me + d, n)
        src = x_ref if gather else x_ref.at[peer]
        copy = pltpu.make_async_remote_copy(
            src_ref=src, dst_ref=out_ref.at[me], send_sem=send_sems.at[d], recv_sem=recv_sems.at[d],
            device_id=at(peer), device_id_type=pl.DeviceIdType.MESH)
        copy.start()
        copies.append(copy)
    if gather:
        out_ref[me] = x_ref[...]
    else:
        out_ref[me] = x_ref[me]
    for d in range(1, n):
        copies[d - 1].wait_send()
        source = lax.rem(me + n - d, n)
        src = x_ref if gather else x_ref.at[source]
        incoming = pltpu.make_async_remote_copy(
            src_ref=src, dst_ref=out_ref.at[source], send_sem=send_sems.at[d], recv_sem=recv_sems.at[d],
            device_id=at(source), device_id_type=pl.DeviceIdType.MESH)
        incoming.wait_recv()


def exchange(x, axis, other, n, gather, collective_id):
    block = x.shape if gather else x.shape[1:]
    return pl.pallas_call(
        functools.partial(_exchange_kernel, axis, other, n, gather),
        out_shape=jax.ShapeDtypeStruct((n,) + tuple(block), x.dtype),
        in_specs=[pl.BlockSpec(memory_space=pltpu.VMEM)],
        out_specs=pl.BlockSpec(memory_space=pltpu.VMEM),
        scratch_shapes=[pltpu.SemaphoreType.DMA((n,)), pltpu.SemaphoreType.DMA((n,))],
        compiler_params=pltpu.CompilerParams(collective_id=collective_id, has_side_effects=True),
    )(x)


def _gather_kernel(n, x_ref, out_ref, send_sems, forward_sems, recv_sems):
    me = lax.axis_index("col")
    mine = lax.axis_index("row")
    core = lax.rem(me, 2)
    chip = me // 2
    chips = n // 2
    sibling = chip * 2 + 1 - core
    peers = [lax.rem(chip + d, chips) * 2 + core for d in range(1, chips)]
    barrier = pltpu.get_barrier_semaphore()
    for peer in peers + [sibling]:
        pl.semaphore_signal(barrier, inc=1, device_id=(mine, peer), device_id_type=pl.DeviceIdType.MESH)
    pl.semaphore_wait(barrier, chips)

    def copy(src, slot, sem, peer):
        return pltpu.make_async_remote_copy(
            src_ref=src, dst_ref=out_ref.at[slot], send_sem=sem, recv_sem=recv_sems.at[slot],
            device_id=(mine, peer), device_id_type=pl.DeviceIdType.MESH)

    sent = []
    for d, peer in enumerate(peers + [sibling]):
        c = copy(x_ref, me, send_sems.at[d], peer)
        c.start()
        sent.append(c)
    out_ref[me] = x_ref[...]
    for d, peer in enumerate(peers):
        copy(x_ref, peer, send_sems.at[d], peer).wait_recv()
        c = copy(out_ref.at[peer], peer, forward_sems.at[d], sibling)
        c.start()
        sent.append(c)
    copy(x_ref, sibling, send_sems.at[0], sibling).wait_recv()
    for d in range(1, chips):
        far = lax.rem(chip + d, chips) * 2 + 1 - core
        copy(x_ref, far, send_sems.at[0], sibling).wait_recv()
    for c in sent:
        c.wait_send()


def col_gather(x, n, collective_id):
    return pl.pallas_call(
        functools.partial(_gather_kernel, n),
        out_shape=jax.ShapeDtypeStruct((n,) + x.shape, x.dtype),
        in_specs=[pl.BlockSpec(memory_space=pltpu.VMEM)],
        out_specs=pl.BlockSpec(memory_space=pltpu.VMEM),
        scratch_shapes=[
            pltpu.SemaphoreType.DMA((n,)),
            pltpu.SemaphoreType.DMA((n,)),
            pltpu.SemaphoreType.DMA((n,)),
        ],
        compiler_params=pltpu.CompilerParams(collective_id=collective_id, has_side_effects=True),
    )(x)


def _scatter_kernel(n, x_ref, out_ref, half, recv, acc, send_sems, recv_sems):
    me = lax.axis_index("col")
    mine = lax.axis_index("row")
    core = lax.rem(me, 2)
    chip = me // 2
    chips = n // 2
    sibling = chip * 2 + 1 - core
    peers = [lax.rem(chip + d, chips) * 2 + core for d in range(1, chips)]
    barrier = pltpu.get_barrier_semaphore()
    for peer in peers + [sibling]:
        pl.semaphore_signal(barrier, inc=1, device_id=(mine, peer), device_id_type=pl.DeviceIdType.MESH)
    pl.semaphore_wait(barrier, chips)

    swap = pltpu.make_async_remote_copy(
        src_ref=x_ref.at[:, 1 - core], dst_ref=half, send_sem=send_sems.at[0], recv_sem=recv_sems.at[0],
        device_id=(mine, sibling), device_id_type=pl.DeviceIdType.MESH)
    swap.start()
    swap.wait_recv()
    acc[...] = x_ref[:, core] + half[...]
    sent = [swap]
    for d in range(1, chips):
        target = lax.rem(chip + d, chips)
        c = pltpu.make_async_remote_copy(
            src_ref=acc.at[target], dst_ref=recv.at[chip], send_sem=send_sems.at[d], recv_sem=recv_sems.at[d],
            device_id=(mine, target * 2 + core), device_id_type=pl.DeviceIdType.MESH)
        c.start()
        sent.append(c)
    total = acc[chip]
    for d in range(1, chips):
        source = lax.rem(chip + chips - d, chips)
        pltpu.make_async_remote_copy(
            src_ref=acc.at[source], dst_ref=recv.at[source], send_sem=send_sems.at[d], recv_sem=recv_sems.at[d],
            device_id=(mine, source * 2 + core), device_id_type=pl.DeviceIdType.MESH).wait_recv()
        total = total + recv[source]
    out_ref[...] = total
    for c in sent:
        c.wait_send()


def col_scatter(x, n, collective_id):
    chips = n // 2
    block = x.shape[1:]
    return pl.pallas_call(
        functools.partial(_scatter_kernel, n),
        out_shape=jax.ShapeDtypeStruct(block, x.dtype),
        in_specs=[pl.BlockSpec(memory_space=pltpu.VMEM)],
        out_specs=pl.BlockSpec(memory_space=pltpu.VMEM),
        scratch_shapes=[
            pltpu.VMEM((chips,) + block, x.dtype),
            pltpu.VMEM((chips,) + block, x.dtype),
            pltpu.VMEM((chips,) + block, x.dtype),
            pltpu.SemaphoreType.DMA((chips,)),
            pltpu.SemaphoreType.DMA((chips,)),
        ],
        compiler_params=pltpu.CompilerParams(collective_id=collective_id, has_side_effects=True),
    )(x.reshape((chips, 2) + block))


def _route_kernel(x_ref, out_ref, send_buf, send_sems, recv_sems):
    row = lax.axis_index("row")
    col = lax.axis_index("col")
    pairs = x_ref.shape[0] // 2
    rows = lax.axis_size("row")
    block = col // 2
    half = lax.rem(col, 2)
    base = pairs * half
    source_col = 2 * row + col // pairs
    mirrored = (row == block) & (col // pairs == half)

    barrier = pltpu.get_barrier_semaphore()
    for k in range(pairs):
        target = base + k

        @pl.when((block != row) | (target != col))
        def _():
            pl.semaphore_signal(barrier, inc=1, device_id=(block, target), device_id_type=pl.DeviceIdType.MESH)
    for r in range(rows):

        @pl.when((r != row) | (source_col != col))
        def _():
            pl.semaphore_signal(barrier, inc=1, device_id=(r, source_col), device_id_type=pl.DeviceIdType.MESH)

    @pl.when(mirrored)
    def _():
        pl.semaphore_wait(barrier, pairs + rows - 2)

    @pl.when(jnp.logical_not(mirrored))
    def _():
        pl.semaphore_wait(barrier, pairs + rows)

    for k in range(pairs):
        send_buf[k] = x_ref[2 * k:2 * k + 2, :]

    def copy(k, r, device):
        return pltpu.make_async_remote_copy(
            src_ref=send_buf.at[k], dst_ref=out_ref.at[r], send_sem=send_sems.at[k], recv_sem=recv_sems.at[r],
            device_id=device, device_id_type=pl.DeviceIdType.MESH)

    for k in range(pairs):
        target = base + k

        @pl.when((block != row) | (target != col))
        def _():
            copy(k, row, (block, target)).start()

        @pl.when((block == row) & (target == col))
        def _():
            out_ref[row] = send_buf[k]
    for r in range(rows):

        @pl.when((r != row) | (source_col != col))
        def _():
            copy(0, r, (r, source_col)).wait_recv()
    for k in range(pairs):
        target = base + k

        @pl.when((block != row) | (target != col))
        def _():
            copy(k, row, (block, target)).wait_send()


def route(x, rows, collective_id):
    pairs = x.shape[0] // 2
    return pl.pallas_call(
        _route_kernel,
        out_shape=jax.ShapeDtypeStruct((rows, 2, x.shape[1]), x.dtype),
        in_specs=[pl.BlockSpec(memory_space=pltpu.VMEM)],
        out_specs=pl.BlockSpec(memory_space=pltpu.VMEM),
        scratch_shapes=[
            pltpu.VMEM((pairs, 2, x.shape[1]), x.dtype),
            pltpu.SemaphoreType.DMA((pairs,)),
            pltpu.SemaphoreType.DMA((rows,)),
        ],
        compiler_params=pltpu.CompilerParams(collective_id=collective_id, has_side_effects=True),
    )(x)


def _scatter_route_kernel(n, x_ref, out_ref, half_ref, recv, acc, summed, send_buf, send_sems, recv_sems,
                          route_send, route_recv):
    me = lax.axis_index("col")
    row = lax.axis_index("row")
    rows = lax.axis_size("row")
    core = lax.rem(me, 2)
    chip = me // 2
    chips = n // 2
    pairs = summed.shape[0] // 2
    sibling = chip * 2 + 1 - core
    peers = [lax.rem(chip + d, chips) * 2 + core for d in range(1, chips)]
    block = me // 2
    base = pairs * core
    source_col = 2 * row + me // pairs
    mirrored = (row == block) & (me // pairs == core)

    barrier = pltpu.get_barrier_semaphore()
    for peer in peers + [sibling]:
        pl.semaphore_signal(barrier, inc=1, device_id=(row, peer), device_id_type=pl.DeviceIdType.MESH)
    for k in range(pairs):
        target = base + k

        @pl.when((block != row) | (target != me))
        def _():
            pl.semaphore_signal(barrier, inc=1, device_id=(block, target), device_id_type=pl.DeviceIdType.MESH)
    for r in range(rows):

        @pl.when((r != row) | (source_col != me))
        def _():
            pl.semaphore_signal(barrier, inc=1, device_id=(r, source_col), device_id_type=pl.DeviceIdType.MESH)

    @pl.when(mirrored)
    def _():
        pl.semaphore_wait(barrier, chips + pairs + rows - 2)

    @pl.when(jnp.logical_not(mirrored))
    def _():
        pl.semaphore_wait(barrier, chips + pairs + rows)

    swap = pltpu.make_async_remote_copy(
        src_ref=x_ref.at[:, 1 - core], dst_ref=half_ref, send_sem=send_sems.at[0], recv_sem=recv_sems.at[0],
        device_id=(row, sibling), device_id_type=pl.DeviceIdType.MESH)
    swap.start()
    swap.wait_recv()
    acc[...] = x_ref[:, core] + half_ref[...]
    sent = [swap]
    for d in range(1, chips):
        target = lax.rem(chip + d, chips)
        c = pltpu.make_async_remote_copy(
            src_ref=acc.at[target], dst_ref=recv.at[chip], send_sem=send_sems.at[d], recv_sem=recv_sems.at[d],
            device_id=(row, target * 2 + core), device_id_type=pl.DeviceIdType.MESH)
        c.start()
        sent.append(c)
    total = acc[chip]
    for d in range(1, chips):
        source = lax.rem(chip + chips - d, chips)
        pltpu.make_async_remote_copy(
            src_ref=acc.at[source], dst_ref=recv.at[source], send_sem=send_sems.at[d], recv_sem=recv_sems.at[d],
            device_id=(row, source * 2 + core), device_id_type=pl.DeviceIdType.MESH).wait_recv()
        total = total + recv[source]
    summed[...] = total
    for k in range(pairs):
        send_buf[k] = summed[2 * k:2 * k + 2, :]

    def copy(k, r, device):
        return pltpu.make_async_remote_copy(
            src_ref=send_buf.at[k], dst_ref=out_ref.at[r], send_sem=route_send.at[k], recv_sem=route_recv.at[r],
            device_id=device, device_id_type=pl.DeviceIdType.MESH)

    for k in range(pairs):
        target = base + k

        @pl.when((block != row) | (target != me))
        def _():
            copy(k, row, (block, target)).start()

        @pl.when((block == row) & (target == me))
        def _():
            out_ref[row] = send_buf[k]
    for r in range(rows):

        @pl.when((r != row) | (source_col != me))
        def _():
            copy(0, r, (r, source_col)).wait_recv()
    for k in range(pairs):
        target = base + k

        @pl.when((block != row) | (target != me))
        def _():
            copy(k, row, (block, target)).wait_send()
    for c in sent:
        c.wait_send()


def scatter_route(x, n, rows, collective_id):
    chips = n // 2
    block = x.shape[1:]
    pairs = block[0] // 2
    return pl.pallas_call(
        functools.partial(_scatter_route_kernel, n),
        out_shape=jax.ShapeDtypeStruct((rows, 2, block[1]), x.dtype),
        in_specs=[pl.BlockSpec(memory_space=pltpu.VMEM)],
        out_specs=pl.BlockSpec(memory_space=pltpu.VMEM),
        scratch_shapes=[
            pltpu.VMEM((chips,) + block, x.dtype),
            pltpu.VMEM((chips,) + block, x.dtype),
            pltpu.VMEM((chips,) + block, x.dtype),
            pltpu.VMEM(block, x.dtype),
            pltpu.VMEM((pairs, 2, block[1]), x.dtype),
            pltpu.SemaphoreType.DMA((chips,)),
            pltpu.SemaphoreType.DMA((chips,)),
            pltpu.SemaphoreType.DMA((pairs,)),
            pltpu.SemaphoreType.DMA((rows,)),
        ],
        compiler_params=pltpu.CompilerParams(collective_id=collective_id, has_side_effects=True),
    )(x.reshape((chips, 2) + block))


def _ring_kernel(n, chunks, keys_ref, weights_ref, out_ref, own_ref, partial_ref, recv_r, recv_l, acc_r, acc_l,
                 rs_sems, ag_sems):
    me = lax.axis_index("row")
    mine = lax.axis_index("col")
    right = lax.rem(me + 1, n)
    left = lax.rem(me + n - 1, n)
    steps_r = n // 2
    steps_l = n - 1 - steps_r
    block = partial_ref.shape[1]
    size = block // chunks
    half = n * chunks
    barrier = pltpu.get_barrier_semaphore()
    for peer in (left, right):
        pl.semaphore_signal(barrier, inc=1, device_id=(peer, mine), device_id_type=pl.DeviceIdType.MESH)
    pl.semaphore_wait(barrier, 2)

    def whiten(d):
        start = pl.multiple_of(d * block, block)
        partial_ref[d] = jnp.dot(keys_ref[pl.ds(start, block), :], weights_ref[...],
                                 preferred_element_type=jnp.float32)

    def send(src, dst, sems, k, peer):
        copy = pltpu.make_async_remote_copy(
            src_ref=src, dst_ref=dst, send_sem=sems.at[k], recv_sem=sems.at[k + 2 * half],
            device_id=(peer, mine), device_id_type=pl.DeviceIdType.MESH)
        copy.start()
        return copy

    sent = []
    got_r = {}
    got_l = {}
    for s in range(steps_r):
        d_r = lax.rem(me + steps_r - s, n)
        d_l = lax.rem(me + n - steps_l + s, n)
        whiten(d_r)
        if s < steps_l:
            whiten(d_l)
        for h in range(chunks):
            rows = pl.ds(h * size, size)
            if s == 0:
                src = partial_ref.at[d_r, rows]
            else:
                got_r[s - 1, h].wait_recv()
                acc_r[s - 1, rows] = recv_r[s - 1, rows] + partial_ref[d_r, rows]
                src = acc_r.at[s - 1, rows]
            got_r[s, h] = send(src, recv_r.at[s, rows], rs_sems, s * chunks + h, right)
            sent.append(got_r[s, h])
            if s < steps_l:
                if s == 0:
                    src = partial_ref.at[d_l, rows]
                else:
                    got_l[s - 1, h].wait_recv()
                    acc_l[s - 1, rows] = recv_l[s - 1, rows] + partial_ref[d_l, rows]
                    src = acc_l.at[s - 1, rows]
                got_l[s, h] = send(src, recv_l.at[s, rows], rs_sems, half + s * chunks + h, left)
                sent.append(got_l[s, h])
    whiten(me)
    for h in range(chunks):
        rows = pl.ds(h * size, size)
        got_r[steps_r - 1, h].wait_recv()
        got_l[steps_l - 1, h].wait_recv()
        total = partial_ref[me, rows] + recv_r[steps_r - 1, rows] + recv_l[steps_l - 1, rows]
        rounded = total.astype(out_ref.dtype)
        out_ref[me, rows] = rounded
        own_ref[rows] = rounded

    ag_r = {}
    ag_l = {}
    for t in range(steps_r):
        for h in range(chunks):
            rows = pl.ds(h * size, size)
            b_r = lax.rem(me + n - t, n)
            if t:
                ag_r[t - 1, h].wait_recv()
            ag_r[t, h] = send(out_ref.at[b_r, rows], out_ref.at[b_r, rows], ag_sems, t * chunks + h, right)
            sent.append(ag_r[t, h])
            if t < steps_l:
                b_l = lax.rem(me + t, n)
                if t:
                    ag_l[t - 1, h].wait_recv()
                ag_l[t, h] = send(out_ref.at[b_l, rows], out_ref.at[b_l, rows], ag_sems, half + t * chunks + h, left)
                sent.append(ag_l[t, h])
    for h in range(chunks):
        ag_r[steps_r - 1, h].wait_recv()
        ag_l[steps_l - 1, h].wait_recv()
    for c in sent:
        c.wait_send()


def row_ring(keys, weights, n, collective_id, chunks=2):
    rows = keys.shape[0] // n
    width = weights.shape[1]
    steps_r = n // 2
    steps_l = n - 1 - steps_r
    return pl.pallas_call(
        functools.partial(_ring_kernel, n, chunks),
        out_shape=(jax.ShapeDtypeStruct((n, rows, width), jnp.bfloat16),
                   jax.ShapeDtypeStruct((rows, width), jnp.bfloat16)),
        in_specs=[pl.BlockSpec(memory_space=pltpu.VMEM)] * 2,
        out_specs=(pl.BlockSpec(memory_space=pltpu.VMEM), pl.BlockSpec(memory_space=pltpu.VMEM)),
        scratch_shapes=[
            pltpu.VMEM((n, rows, width), jnp.float32),
            pltpu.VMEM((steps_r, rows, width), jnp.float32),
            pltpu.VMEM((steps_l, rows, width), jnp.float32),
            pltpu.VMEM((steps_r - 1, rows, width), jnp.float32),
            pltpu.VMEM((steps_l - 1, rows, width), jnp.float32),
            pltpu.SemaphoreType.DMA((4 * n * chunks,)),
            pltpu.SemaphoreType.DMA((4 * n * chunks,)),
        ],
        compiler_params=pltpu.CompilerParams(collective_id=collective_id, has_side_effects=True),
    )(keys, weights)


def shards(new_keys, precision, stored_keys, pair_batch, pair_count, batch_length, batch_slot):
    row_count = lax.axis_size("row")
    col_count = lax.axis_size("col")
    row_index = lax.axis_index("row")
    total_keys = new_keys.shape[0] * col_count
    block_keys = total_keys // row_count
    part_keys = block_keys // col_count
    local_batches, batch_keys, width = stored_keys.shape
    gathered = col_gather(new_keys, col_count, 0)
    every_row, whitened = row_ring(gathered.reshape(total_keys, new_keys.shape[1]), precision, row_count, 3)
    terms = jnp.einsum("brd,kd->brk", every_row.reshape(row_count, block_keys, width),
                       stored_keys.reshape(local_batches * batch_keys, width), preferred_element_type=jnp.float32)
    terms = terms.reshape(col_count, block_keys // 2, local_batches * batch_keys)
    routed = scatter_route(terms, col_count, row_count, 1)
    table = routed.reshape(row_count, part_keys, local_batches, batch_keys).transpose(0, 2, 1, 3)
    table = table.reshape(row_count * local_batches, part_keys, batch_keys)
    listed = pair_batch[row_index]
    slots = batch_slot[listed]
    lengths = batch_length[listed]
    count = pair_count[row_index]
    picked = jnp.take(table, slots, axis=0)
    places = jnp.arange(slots.shape[0], dtype=jnp.int32)
    columns = jnp.arange(batch_keys, dtype=jnp.int32)
    keep = (places < count)[:, None, None] & (columns[None, None, :] < lengths[:, None, None])
    shares = jnp.where(keep, picked, jnp.zeros_like(picked))
    return (whitened, shares[None])


def solution(mesh):
    placed = (P("col", "row"), P("row", "col"), P("row", None, "col"), P(), P(), P(), P())
    return jax.shard_map(
        shards,
        mesh=mesh,
        in_specs=placed,
        out_specs=(P("row", "col"), P("row", None, "col", None)),
        check_vma=False,
    )
```

```python
import functools

import jax
import jax.numpy as jnp
from jax import lax
from jax.experimental import pallas as pl
from jax.experimental.pallas import tpu as pltpu
from jax.sharding import PartitionSpec as P


def _exchange_kernel(axis, other, n, gather, x_ref, out_ref, send_sems, recv_sems):
    me = lax.axis_index(axis)
    mine = lax.axis_index(other)

    def at(peer):
        return (peer, mine) if axis == "row" else (mine, peer)

    barrier = pltpu.get_barrier_semaphore()
    for d in range(1, n):
        peer = lax.rem(me + d, n)
        pl.semaphore_signal(barrier, inc=1, device_id=at(peer), device_id_type=pl.DeviceIdType.MESH)
    pl.semaphore_wait(barrier, n - 1)
    copies = []
    for d in range(1, n):
        peer = lax.rem(me + d, n)
        src = x_ref if gather else x_ref.at[peer]
        copy = pltpu.make_async_remote_copy(
            src_ref=src, dst_ref=out_ref.at[me], send_sem=send_sems.at[d], recv_sem=recv_sems.at[d],
            device_id=at(peer), device_id_type=pl.DeviceIdType.MESH)
        copy.start()
        copies.append(copy)
    if gather:
        out_ref[me] = x_ref[...]
    else:
        out_ref[me] = x_ref[me]
    for d in range(1, n):
        copies[d - 1].wait_send()
        source = lax.rem(me + n - d, n)
        src = x_ref if gather else x_ref.at[source]
        incoming = pltpu.make_async_remote_copy(
            src_ref=src, dst_ref=out_ref.at[source], send_sem=send_sems.at[d], recv_sem=recv_sems.at[d],
            device_id=at(source), device_id_type=pl.DeviceIdType.MESH)
        incoming.wait_recv()


def exchange(x, axis, other, n, gather, collective_id):
    block = x.shape if gather else x.shape[1:]
    return pl.pallas_call(
        functools.partial(_exchange_kernel, axis, other, n, gather),
        out_shape=jax.ShapeDtypeStruct((n,) + tuple(block), x.dtype),
        in_specs=[pl.BlockSpec(memory_space=pltpu.VMEM)],
        out_specs=pl.BlockSpec(memory_space=pltpu.VMEM),
        scratch_shapes=[pltpu.SemaphoreType.DMA((n,)), pltpu.SemaphoreType.DMA((n,))],
        compiler_params=pltpu.CompilerParams(collective_id=collective_id, has_side_effects=True),
    )(x)


def _gather_kernel(n, x_ref, out_ref, send_sems, forward_sems, recv_sems):
    me = lax.axis_index("col")
    mine = lax.axis_index("row")
    core = lax.rem(me, 2)
    chip = me // 2
    chips = n // 2
    sibling = chip * 2 + 1 - core
    peers = [lax.rem(chip + d, chips) * 2 + core for d in range(1, chips)]
    barrier = pltpu.get_barrier_semaphore()
    for peer in peers + [sibling]:
        pl.semaphore_signal(barrier, inc=1, device_id=(mine, peer), device_id_type=pl.DeviceIdType.MESH)
    pl.semaphore_wait(barrier, chips)

    def copy(src, slot, sem, peer):
        return pltpu.make_async_remote_copy(
            src_ref=src, dst_ref=out_ref.at[slot], send_sem=sem, recv_sem=recv_sems.at[slot],
            device_id=(mine, peer), device_id_type=pl.DeviceIdType.MESH)

    sent = []
    for d, peer in enumerate(peers + [sibling]):
        c = copy(x_ref, me, send_sems.at[d], peer)
        c.start()
        sent.append(c)
    out_ref[me] = x_ref[...]
    for d, peer in enumerate(peers):
        copy(x_ref, peer, send_sems.at[d], peer).wait_recv()
        c = copy(out_ref.at[peer], peer, forward_sems.at[d], sibling)
        c.start()
        sent.append(c)
    copy(x_ref, sibling, send_sems.at[0], sibling).wait_recv()
    for d in range(1, chips):
        far = lax.rem(chip + d, chips) * 2 + 1 - core
        copy(x_ref, far, send_sems.at[0], sibling).wait_recv()
    for c in sent:
        c.wait_send()


def col_gather(x, n, collective_id):
    return pl.pallas_call(
        functools.partial(_gather_kernel, n),
        out_shape=jax.ShapeDtypeStruct((n,) + x.shape, x.dtype),
        in_specs=[pl.BlockSpec(memory_space=pltpu.VMEM)],
        out_specs=pl.BlockSpec(memory_space=pltpu.VMEM),
        scratch_shapes=[
            pltpu.SemaphoreType.DMA((n,)),
            pltpu.SemaphoreType.DMA((n,)),
            pltpu.SemaphoreType.DMA((n,)),
        ],
        compiler_params=pltpu.CompilerParams(collective_id=collective_id, has_side_effects=True),
    )(x)


def _scatter_kernel(n, x_ref, out_ref, half, recv, acc, send_sems, recv_sems):
    me = lax.axis_index("col")
    mine = lax.axis_index("row")
    core = lax.rem(me, 2)
    chip = me // 2
    chips = n // 2
    sibling = chip * 2 + 1 - core
    peers = [lax.rem(chip + d, chips) * 2 + core for d in range(1, chips)]
    barrier = pltpu.get_barrier_semaphore()
    for peer in peers + [sibling]:
        pl.semaphore_signal(barrier, inc=1, device_id=(mine, peer), device_id_type=pl.DeviceIdType.MESH)
    pl.semaphore_wait(barrier, chips)

    swap = pltpu.make_async_remote_copy(
        src_ref=x_ref.at[:, 1 - core], dst_ref=half, send_sem=send_sems.at[0], recv_sem=recv_sems.at[0],
        device_id=(mine, sibling), device_id_type=pl.DeviceIdType.MESH)
    swap.start()
    swap.wait_recv()
    acc[...] = x_ref[:, core] + half[...]
    sent = [swap]
    for d in range(1, chips):
        target = lax.rem(chip + d, chips)
        c = pltpu.make_async_remote_copy(
            src_ref=acc.at[target], dst_ref=recv.at[chip], send_sem=send_sems.at[d], recv_sem=recv_sems.at[d],
            device_id=(mine, target * 2 + core), device_id_type=pl.DeviceIdType.MESH)
        c.start()
        sent.append(c)
    total = acc[chip]
    for d in range(1, chips):
        source = lax.rem(chip + chips - d, chips)
        pltpu.make_async_remote_copy(
            src_ref=acc.at[source], dst_ref=recv.at[source], send_sem=send_sems.at[d], recv_sem=recv_sems.at[d],
            device_id=(mine, source * 2 + core), device_id_type=pl.DeviceIdType.MESH).wait_recv()
        total = total + recv[source]
    out_ref[...] = total
    for c in sent:
        c.wait_send()


def col_scatter(x, n, collective_id):
    chips = n // 2
    block = x.shape[1:]
    return pl.pallas_call(
        functools.partial(_scatter_kernel, n),
        out_shape=jax.ShapeDtypeStruct(block, x.dtype),
        in_specs=[pl.BlockSpec(memory_space=pltpu.VMEM)],
        out_specs=pl.BlockSpec(memory_space=pltpu.VMEM),
        scratch_shapes=[
            pltpu.VMEM((chips,) + block, x.dtype),
            pltpu.VMEM((chips,) + block, x.dtype),
            pltpu.VMEM((chips,) + block, x.dtype),
            pltpu.SemaphoreType.DMA((chips,)),
            pltpu.SemaphoreType.DMA((chips,)),
        ],
        compiler_params=pltpu.CompilerParams(collective_id=collective_id, has_side_effects=True),
    )(x.reshape((chips, 2) + block))


def _route_kernel(x_ref, out_ref, send_buf, send_sems, recv_sems):
    row = lax.axis_index("row")
    col = lax.axis_index("col")
    pairs = x_ref.shape[0] // 2
    rows = lax.axis_size("row")
    block = col // 2
    half = lax.rem(col, 2)
    base = pairs * half
    source_col = 2 * row + col // pairs
    mirrored = (row == block) & (col // pairs == half)

    barrier = pltpu.get_barrier_semaphore()
    for k in range(pairs):
        target = base + k

        @pl.when((block != row) | (target != col))
        def _():
            pl.semaphore_signal(barrier, inc=1, device_id=(block, target), device_id_type=pl.DeviceIdType.MESH)
    for r in range(rows):

        @pl.when((r != row) | (source_col != col))
        def _():
            pl.semaphore_signal(barrier, inc=1, device_id=(r, source_col), device_id_type=pl.DeviceIdType.MESH)

    @pl.when(mirrored)
    def _():
        pl.semaphore_wait(barrier, pairs + rows - 2)

    @pl.when(jnp.logical_not(mirrored))
    def _():
        pl.semaphore_wait(barrier, pairs + rows)

    for k in range(pairs):
        send_buf[k] = x_ref[2 * k:2 * k + 2, :]

    def copy(k, r, device):
        return pltpu.make_async_remote_copy(
            src_ref=send_buf.at[k], dst_ref=out_ref.at[r], send_sem=send_sems.at[k], recv_sem=recv_sems.at[r],
            device_id=device, device_id_type=pl.DeviceIdType.MESH)

    for k in range(pairs):
        target = base + k

        @pl.when((block != row) | (target != col))
        def _():
            copy(k, row, (block, target)).start()

        @pl.when((block == row) & (target == col))
        def _():
            out_ref[row] = send_buf[k]
    for r in range(rows):

        @pl.when((r != row) | (source_col != col))
        def _():
            copy(0, r, (r, source_col)).wait_recv()
    for k in range(pairs):
        target = base + k

        @pl.when((block != row) | (target != col))
        def _():
            copy(k, row, (block, target)).wait_send()


def route(x, rows, collective_id):
    pairs = x.shape[0] // 2
    return pl.pallas_call(
        _route_kernel,
        out_shape=jax.ShapeDtypeStruct((rows, 2, x.shape[1]), x.dtype),
        in_specs=[pl.BlockSpec(memory_space=pltpu.VMEM)],
        out_specs=pl.BlockSpec(memory_space=pltpu.VMEM),
        scratch_shapes=[
            pltpu.VMEM((pairs, 2, x.shape[1]), x.dtype),
            pltpu.SemaphoreType.DMA((pairs,)),
            pltpu.SemaphoreType.DMA((rows,)),
        ],
        compiler_params=pltpu.CompilerParams(collective_id=collective_id, has_side_effects=True),
    )(x)


def _scatter_route_kernel(n, x_ref, out_ref, half_ref, recv, acc, summed, send_buf, send_sems, recv_sems,
                          route_send, route_recv):
    me = lax.axis_index("col")
    row = lax.axis_index("row")
    rows = lax.axis_size("row")
    core = lax.rem(me, 2)
    chip = me // 2
    chips = n // 2
    pairs = summed.shape[0] // 2
    sibling = chip * 2 + 1 - core
    peers = [lax.rem(chip + d, chips) * 2 + core for d in range(1, chips)]
    block = me // 2
    base = pairs * core
    source_col = 2 * row + me // pairs
    mirrored = (row == block) & (me // pairs == core)

    barrier = pltpu.get_barrier_semaphore()
    for peer in peers + [sibling]:
        pl.semaphore_signal(barrier, inc=1, device_id=(row, peer), device_id_type=pl.DeviceIdType.MESH)
    for k in range(pairs):
        target = base + k

        @pl.when((block != row) | (target != me))
        def _():
            pl.semaphore_signal(barrier, inc=1, device_id=(block, target), device_id_type=pl.DeviceIdType.MESH)
    for r in range(rows):

        @pl.when((r != row) | (source_col != me))
        def _():
            pl.semaphore_signal(barrier, inc=1, device_id=(r, source_col), device_id_type=pl.DeviceIdType.MESH)

    @pl.when(mirrored)
    def _():
        pl.semaphore_wait(barrier, chips + pairs + rows - 2)

    @pl.when(jnp.logical_not(mirrored))
    def _():
        pl.semaphore_wait(barrier, chips + pairs + rows)

    swap = pltpu.make_async_remote_copy(
        src_ref=x_ref.at[:, 1 - core], dst_ref=half_ref, send_sem=send_sems.at[0], recv_sem=recv_sems.at[0],
        device_id=(row, sibling), device_id_type=pl.DeviceIdType.MESH)
    swap.start()
    swap.wait_recv()
    acc[...] = x_ref[:, core] + half_ref[...]
    sent = [swap]
    for d in range(1, chips):
        target = lax.rem(chip + d, chips)
        c = pltpu.make_async_remote_copy(
            src_ref=acc.at[target], dst_ref=recv.at[chip], send_sem=send_sems.at[d], recv_sem=recv_sems.at[d],
            device_id=(row, target * 2 + core), device_id_type=pl.DeviceIdType.MESH)
        c.start()
        sent.append(c)
    total = acc[chip]
    for d in range(1, chips):
        source = lax.rem(chip + chips - d, chips)
        pltpu.make_async_remote_copy(
            src_ref=acc.at[source], dst_ref=recv.at[source], send_sem=send_sems.at[d], recv_sem=recv_sems.at[d],
            device_id=(row, source * 2 + core), device_id_type=pl.DeviceIdType.MESH).wait_recv()
        total = total + recv[source]
    summed[...] = total
    for k in range(pairs):
        send_buf[k] = summed[2 * k:2 * k + 2, :]

    def copy(k, r, device):
        return pltpu.make_async_remote_copy(
            src_ref=send_buf.at[k], dst_ref=out_ref.at[r], send_sem=route_send.at[k], recv_sem=route_recv.at[r],
            device_id=device, device_id_type=pl.DeviceIdType.MESH)

    for k in range(pairs):
        target = base + k

        @pl.when((block != row) | (target != me))
        def _():
            copy(k, row, (block, target)).start()

        @pl.when((block == row) & (target == me))
        def _():
            out_ref[row] = send_buf[k]
    for r in range(rows):

        @pl.when((r != row) | (source_col != me))
        def _():
            copy(0, r, (r, source_col)).wait_recv()
    for k in range(pairs):
        target = base + k

        @pl.when((block != row) | (target != me))
        def _():
            copy(k, row, (block, target)).wait_send()
    for c in sent:
        c.wait_send()


def scatter_route(x, n, rows, collective_id):
    chips = n // 2
    block = x.shape[1:]
    pairs = block[0] // 2
    return pl.pallas_call(
        functools.partial(_scatter_route_kernel, n),
        out_shape=jax.ShapeDtypeStruct((rows, 2, block[1]), x.dtype),
        in_specs=[pl.BlockSpec(memory_space=pltpu.VMEM)],
        out_specs=pl.BlockSpec(memory_space=pltpu.VMEM),
        scratch_shapes=[
            pltpu.VMEM((chips,) + block, x.dtype),
            pltpu.VMEM((chips,) + block, x.dtype),
            pltpu.VMEM((chips,) + block, x.dtype),
            pltpu.VMEM(block, x.dtype),
            pltpu.VMEM((pairs, 2, block[1]), x.dtype),
            pltpu.SemaphoreType.DMA((chips,)),
            pltpu.SemaphoreType.DMA((chips,)),
            pltpu.SemaphoreType.DMA((pairs,)),
            pltpu.SemaphoreType.DMA((rows,)),
        ],
        compiler_params=pltpu.CompilerParams(collective_id=collective_id, has_side_effects=True),
    )(x.reshape((chips, 2) + block))


def _ring_kernel(n, chunks, keys_ref, weights_ref, stored_ref, terms_ref, own_ref, out_ref, partial_ref, recv_r, recv_l, acc_r, acc_l,
                 rs_sems, ag_sems):
    me = lax.axis_index("row")
    mine = lax.axis_index("col")
    right = lax.rem(me + 1, n)
    left = lax.rem(me + n - 1, n)
    steps_r = n // 2
    steps_l = n - 1 - steps_r
    block = partial_ref.shape[1]
    size = block // chunks
    half = n * chunks
    barrier = pltpu.get_barrier_semaphore()
    for peer in (left, right):
        pl.semaphore_signal(barrier, inc=1, device_id=(peer, mine), device_id_type=pl.DeviceIdType.MESH)
    pl.semaphore_wait(barrier, 2)

    def whiten(d):
        start = pl.multiple_of(d * block, block)
        partial_ref[d] = jnp.dot(keys_ref[pl.ds(start, block), :], weights_ref[...],
                                 preferred_element_type=jnp.float32)

    def intersect(b):
        terms_ref[b] = lax.dot_general(out_ref[b], stored_ref[...], (((1,), (1,)), ((), ())),
                                       preferred_element_type=jnp.float32)

    def send(src, dst, sems, k, peer):
        copy = pltpu.make_async_remote_copy(
            src_ref=src, dst_ref=dst, send_sem=sems.at[k], recv_sem=sems.at[k + 2 * half],
            device_id=(peer, mine), device_id_type=pl.DeviceIdType.MESH)
        copy.start()
        return copy

    sent = []
    got_r = {}
    got_l = {}
    for s in range(steps_r):
        d_r = lax.rem(me + steps_r - s, n)
        d_l = lax.rem(me + n - steps_l + s, n)
        whiten(d_r)
        if s < steps_l:
            whiten(d_l)
        for h in range(chunks):
            rows = pl.ds(h * size, size)
            if s == 0:
                src = partial_ref.at[d_r, rows]
            else:
                got_r[s - 1, h].wait_recv()
                acc_r[s - 1, rows] = recv_r[s - 1, rows] + partial_ref[d_r, rows]
                src = acc_r.at[s - 1, rows]
            got_r[s, h] = send(src, recv_r.at[s, rows], rs_sems, s * chunks + h, right)
            sent.append(got_r[s, h])
            if s < steps_l:
                if s == 0:
                    src = partial_ref.at[d_l, rows]
                else:
                    got_l[s - 1, h].wait_recv()
                    acc_l[s - 1, rows] = recv_l[s - 1, rows] + partial_ref[d_l, rows]
                    src = acc_l.at[s - 1, rows]
                got_l[s, h] = send(src, recv_l.at[s, rows], rs_sems, half + s * chunks + h, left)
                sent.append(got_l[s, h])
    whiten(me)
    for h in range(chunks):
        rows = pl.ds(h * size, size)
        got_r[steps_r - 1, h].wait_recv()
        got_l[steps_l - 1, h].wait_recv()
        total = partial_ref[me, rows] + recv_r[steps_r - 1, rows] + recv_l[steps_l - 1, rows]
        rounded = total.astype(out_ref.dtype)
        out_ref[me, rows] = rounded
        own_ref[rows] = rounded

    ag_r = {}
    ag_l = {}
    for t in range(steps_r):
        for h in range(chunks):
            rows = pl.ds(h * size, size)
            b_r = lax.rem(me + n - t, n)
            if t:
                ag_r[t - 1, h].wait_recv()
            ag_r[t, h] = send(out_ref.at[b_r, rows], out_ref.at[b_r, rows], ag_sems, t * chunks + h, right)
            sent.append(ag_r[t, h])
            if t < steps_l:
                b_l = lax.rem(me + t, n)
                if t:
                    ag_l[t - 1, h].wait_recv()
                ag_l[t, h] = send(out_ref.at[b_l, rows], out_ref.at[b_l, rows], ag_sems, half + t * chunks + h, left)
                sent.append(ag_l[t, h])
        intersect(lax.rem(me + n - t, n))
        if t and t < steps_l:
            intersect(lax.rem(me + t, n))
    for h in range(chunks):
        ag_r[steps_r - 1, h].wait_recv()
        ag_l[steps_l - 1, h].wait_recv()
    intersect(lax.rem(me + n - steps_r, n))
    intersect(lax.rem(me + steps_l, n))
    for c in sent:
        c.wait_send()


def row_ring(keys, weights, stored, n, collective_id, chunks=2):
    rows = keys.shape[0] // n
    width = weights.shape[1]
    slots = stored.shape[0]
    steps_r = n // 2
    steps_l = n - 1 - steps_r
    return pl.pallas_call(
        functools.partial(_ring_kernel, n, chunks),
        out_shape=(jax.ShapeDtypeStruct((n, rows, slots), jnp.float32),
                   jax.ShapeDtypeStruct((rows, width), jnp.bfloat16)),
        in_specs=[pl.BlockSpec(memory_space=pltpu.VMEM)] * 3,
        out_specs=(pl.BlockSpec(memory_space=pltpu.VMEM), pl.BlockSpec(memory_space=pltpu.VMEM)),
        scratch_shapes=[
            pltpu.VMEM((n, rows, width), jnp.bfloat16),
            pltpu.VMEM((n, rows, width), jnp.float32),
            pltpu.VMEM((steps_r, rows, width), jnp.float32),
            pltpu.VMEM((steps_l, rows, width), jnp.float32),
            pltpu.VMEM((steps_r - 1, rows, width), jnp.float32),
            pltpu.VMEM((steps_l - 1, rows, width), jnp.float32),
            pltpu.SemaphoreType.DMA((4 * n * chunks,)),
            pltpu.SemaphoreType.DMA((4 * n * chunks,)),
        ],
        compiler_params=pltpu.CompilerParams(collective_id=collective_id, has_side_effects=True),
    )(keys, weights, stored)


def shards(new_keys, precision, stored_keys, pair_batch, pair_count, batch_length, batch_slot):
    row_count = lax.axis_size("row")
    col_count = lax.axis_size("col")
    row_index = lax.axis_index("row")
    total_keys = new_keys.shape[0] * col_count
    block_keys = total_keys // row_count
    part_keys = block_keys // col_count
    local_batches, batch_keys, width = stored_keys.shape
    gathered = col_gather(new_keys, col_count, 0)
    terms, whitened = row_ring(gathered.reshape(total_keys, new_keys.shape[1]), precision,
                               stored_keys.reshape(local_batches * batch_keys, width), row_count, 3)
    terms = terms.reshape(col_count, block_keys // 2, local_batches * batch_keys)
    routed = scatter_route(terms, col_count, row_count, 1)
    table = routed.reshape(row_count, part_keys, local_batches, batch_keys).transpose(0, 2, 1, 3)
    table = table.reshape(row_count * local_batches, part_keys, batch_keys)
    listed = pair_batch[row_index]
    slots = batch_slot[listed]
    lengths = batch_length[listed]
    count = pair_count[row_index]
    picked = jnp.take(table, slots, axis=0)
    places = jnp.arange(slots.shape[0], dtype=jnp.int32)
    columns = jnp.arange(batch_keys, dtype=jnp.int32)
    keep = (places < count)[:, None, None] & (columns[None, None, :] < lengths[:, None, None])
    shares = jnp.where(keep, picked, jnp.zeros_like(picked))
    return (whitened, shares[None])


def solution(mesh):
    placed = (P("col", "row"), P("row", "col"), P("row", None, "col"), P(), P(), P(), P())
    return jax.shard_map(
        shards,
        mesh=mesh,
        in_specs=placed,
        out_specs=(P("row", "col"), P("row", None, "col", None)),
        check_vma=False,
    )
```

```python
import functools

import jax
import jax.numpy as jnp
from jax import lax
from jax.experimental import pallas as pl
from jax.experimental.pallas import tpu as pltpu
from jax.sharding import PartitionSpec as P


def _exchange_kernel(axis, other, n, gather, x_ref, out_ref, send_sems, recv_sems):
    me = lax.axis_index(axis)
    mine = lax.axis_index(other)

    def at(peer):
        return (peer, mine) if axis == "row" else (mine, peer)

    barrier = pltpu.get_barrier_semaphore()
    for d in range(1, n):
        peer = lax.rem(me + d, n)
        pl.semaphore_signal(barrier, inc=1, device_id=at(peer), device_id_type=pl.DeviceIdType.MESH)
    pl.semaphore_wait(barrier, n - 1)
    copies = []
    for d in range(1, n):
        peer = lax.rem(me + d, n)
        src = x_ref if gather else x_ref.at[peer]
        copy = pltpu.make_async_remote_copy(
            src_ref=src, dst_ref=out_ref.at[me], send_sem=send_sems.at[d], recv_sem=recv_sems.at[d],
            device_id=at(peer), device_id_type=pl.DeviceIdType.MESH)
        copy.start()
        copies.append(copy)
    if gather:
        out_ref[me] = x_ref[...]
    else:
        out_ref[me] = x_ref[me]
    for d in range(1, n):
        copies[d - 1].wait_send()
        source = lax.rem(me + n - d, n)
        src = x_ref if gather else x_ref.at[source]
        incoming = pltpu.make_async_remote_copy(
            src_ref=src, dst_ref=out_ref.at[source], send_sem=send_sems.at[d], recv_sem=recv_sems.at[d],
            device_id=at(source), device_id_type=pl.DeviceIdType.MESH)
        incoming.wait_recv()


def exchange(x, axis, other, n, gather, collective_id):
    block = x.shape if gather else x.shape[1:]
    return pl.pallas_call(
        functools.partial(_exchange_kernel, axis, other, n, gather),
        out_shape=jax.ShapeDtypeStruct((n,) + tuple(block), x.dtype),
        in_specs=[pl.BlockSpec(memory_space=pltpu.VMEM)],
        out_specs=pl.BlockSpec(memory_space=pltpu.VMEM),
        scratch_shapes=[pltpu.SemaphoreType.DMA((n,)), pltpu.SemaphoreType.DMA((n,))],
        compiler_params=pltpu.CompilerParams(collective_id=collective_id, has_side_effects=True),
    )(x)


def _gather_kernel(n, x_ref, out_ref, send_sems, forward_sems, recv_sems):
    me = lax.axis_index("col")
    mine = lax.axis_index("row")
    core = lax.rem(me, 2)
    chip = me // 2
    chips = n // 2
    sibling = chip * 2 + 1 - core
    peers = [lax.rem(chip + d, chips) * 2 + core for d in range(1, chips)]
    barrier = pltpu.get_barrier_semaphore()
    for peer in peers + [sibling]:
        pl.semaphore_signal(barrier, inc=1, device_id=(mine, peer), device_id_type=pl.DeviceIdType.MESH)
    pl.semaphore_wait(barrier, chips)

    def copy(src, slot, sem, peer):
        return pltpu.make_async_remote_copy(
            src_ref=src, dst_ref=out_ref.at[slot], send_sem=sem, recv_sem=recv_sems.at[slot],
            device_id=(mine, peer), device_id_type=pl.DeviceIdType.MESH)

    sent = []
    for d, peer in enumerate(peers + [sibling]):
        c = copy(x_ref, me, send_sems.at[d], peer)
        c.start()
        sent.append(c)
    out_ref[me] = x_ref[...]
    for d, peer in enumerate(peers):
        copy(x_ref, peer, send_sems.at[d], peer).wait_recv()
        c = copy(out_ref.at[peer], peer, forward_sems.at[d], sibling)
        c.start()
        sent.append(c)
    copy(x_ref, sibling, send_sems.at[0], sibling).wait_recv()
    for d in range(1, chips):
        far = lax.rem(chip + d, chips) * 2 + 1 - core
        copy(x_ref, far, send_sems.at[0], sibling).wait_recv()
    for c in sent:
        c.wait_send()


def col_gather(x, n, collective_id):
    return pl.pallas_call(
        functools.partial(_gather_kernel, n),
        out_shape=jax.ShapeDtypeStruct((n,) + x.shape, x.dtype),
        in_specs=[pl.BlockSpec(memory_space=pltpu.VMEM)],
        out_specs=pl.BlockSpec(memory_space=pltpu.VMEM),
        scratch_shapes=[
            pltpu.SemaphoreType.DMA((n,)),
            pltpu.SemaphoreType.DMA((n,)),
            pltpu.SemaphoreType.DMA((n,)),
        ],
        compiler_params=pltpu.CompilerParams(collective_id=collective_id, has_side_effects=True),
    )(x)


def _scatter_kernel(n, x_ref, out_ref, half, recv, acc, send_sems, recv_sems):
    me = lax.axis_index("col")
    mine = lax.axis_index("row")
    core = lax.rem(me, 2)
    chip = me // 2
    chips = n // 2
    sibling = chip * 2 + 1 - core
    peers = [lax.rem(chip + d, chips) * 2 + core for d in range(1, chips)]
    barrier = pltpu.get_barrier_semaphore()
    for peer in peers + [sibling]:
        pl.semaphore_signal(barrier, inc=1, device_id=(mine, peer), device_id_type=pl.DeviceIdType.MESH)
    pl.semaphore_wait(barrier, chips)

    swap = pltpu.make_async_remote_copy(
        src_ref=x_ref.at[:, 1 - core], dst_ref=half, send_sem=send_sems.at[0], recv_sem=recv_sems.at[0],
        device_id=(mine, sibling), device_id_type=pl.DeviceIdType.MESH)
    swap.start()
    swap.wait_recv()
    acc[...] = x_ref[:, core] + half[...]
    sent = [swap]
    for d in range(1, chips):
        target = lax.rem(chip + d, chips)
        c = pltpu.make_async_remote_copy(
            src_ref=acc.at[target], dst_ref=recv.at[chip], send_sem=send_sems.at[d], recv_sem=recv_sems.at[d],
            device_id=(mine, target * 2 + core), device_id_type=pl.DeviceIdType.MESH)
        c.start()
        sent.append(c)
    total = acc[chip]
    for d in range(1, chips):
        source = lax.rem(chip + chips - d, chips)
        pltpu.make_async_remote_copy(
            src_ref=acc.at[source], dst_ref=recv.at[source], send_sem=send_sems.at[d], recv_sem=recv_sems.at[d],
            device_id=(mine, source * 2 + core), device_id_type=pl.DeviceIdType.MESH).wait_recv()
        total = total + recv[source]
    out_ref[...] = total
    for c in sent:
        c.wait_send()


def col_scatter(x, n, collective_id):
    chips = n // 2
    block = x.shape[1:]
    return pl.pallas_call(
        functools.partial(_scatter_kernel, n),
        out_shape=jax.ShapeDtypeStruct(block, x.dtype),
        in_specs=[pl.BlockSpec(memory_space=pltpu.VMEM)],
        out_specs=pl.BlockSpec(memory_space=pltpu.VMEM),
        scratch_shapes=[
            pltpu.VMEM((chips,) + block, x.dtype),
            pltpu.VMEM((chips,) + block, x.dtype),
            pltpu.VMEM((chips,) + block, x.dtype),
            pltpu.SemaphoreType.DMA((chips,)),
            pltpu.SemaphoreType.DMA((chips,)),
        ],
        compiler_params=pltpu.CompilerParams(collective_id=collective_id, has_side_effects=True),
    )(x.reshape((chips, 2) + block))


def _route_kernel(x_ref, out_ref, send_buf, send_sems, recv_sems):
    row = lax.axis_index("row")
    col = lax.axis_index("col")
    pairs = x_ref.shape[0] // 2
    rows = lax.axis_size("row")
    block = col // 2
    half = lax.rem(col, 2)
    base = pairs * half
    source_col = 2 * row + col // pairs
    mirrored = (row == block) & (col // pairs == half)

    barrier = pltpu.get_barrier_semaphore()
    for k in range(pairs):
        target = base + k

        @pl.when((block != row) | (target != col))
        def _():
            pl.semaphore_signal(barrier, inc=1, device_id=(block, target), device_id_type=pl.DeviceIdType.MESH)
    for r in range(rows):

        @pl.when((r != row) | (source_col != col))
        def _():
            pl.semaphore_signal(barrier, inc=1, device_id=(r, source_col), device_id_type=pl.DeviceIdType.MESH)

    @pl.when(mirrored)
    def _():
        pl.semaphore_wait(barrier, pairs + rows - 2)

    @pl.when(jnp.logical_not(mirrored))
    def _():
        pl.semaphore_wait(barrier, pairs + rows)

    for k in range(pairs):
        send_buf[k] = x_ref[2 * k:2 * k + 2, :]

    def copy(k, r, device):
        return pltpu.make_async_remote_copy(
            src_ref=send_buf.at[k], dst_ref=out_ref.at[r], send_sem=send_sems.at[k], recv_sem=recv_sems.at[r],
            device_id=device, device_id_type=pl.DeviceIdType.MESH)

    for k in range(pairs):
        target = base + k

        @pl.when((block != row) | (target != col))
        def _():
            copy(k, row, (block, target)).start()

        @pl.when((block == row) & (target == col))
        def _():
            out_ref[row] = send_buf[k]
    for r in range(rows):

        @pl.when((r != row) | (source_col != col))
        def _():
            copy(0, r, (r, source_col)).wait_recv()
    for k in range(pairs):
        target = base + k

        @pl.when((block != row) | (target != col))
        def _():
            copy(k, row, (block, target)).wait_send()


def route(x, rows, collective_id):
    pairs = x.shape[0] // 2
    return pl.pallas_call(
        _route_kernel,
        out_shape=jax.ShapeDtypeStruct((rows, 2, x.shape[1]), x.dtype),
        in_specs=[pl.BlockSpec(memory_space=pltpu.VMEM)],
        out_specs=pl.BlockSpec(memory_space=pltpu.VMEM),
        scratch_shapes=[
            pltpu.VMEM((pairs, 2, x.shape[1]), x.dtype),
            pltpu.SemaphoreType.DMA((pairs,)),
            pltpu.SemaphoreType.DMA((rows,)),
        ],
        compiler_params=pltpu.CompilerParams(collective_id=collective_id, has_side_effects=True),
    )(x)


def _scatter_route_kernel(n, x_ref, out_ref, half_ref, recv, acc, summed, send_buf, send_sems, recv_sems,
                          route_send, route_recv):
    me = lax.axis_index("col")
    row = lax.axis_index("row")
    rows = lax.axis_size("row")
    core = lax.rem(me, 2)
    chip = me // 2
    chips = n // 2
    pairs = summed.shape[0] // 2
    sibling = chip * 2 + 1 - core
    peers = [lax.rem(chip + d, chips) * 2 + core for d in range(1, chips)]
    block = me // 2
    base = pairs * core
    source_col = 2 * row + me // pairs
    mirrored = (row == block) & (me // pairs == core)

    barrier = pltpu.get_barrier_semaphore()
    for peer in peers + [sibling]:
        pl.semaphore_signal(barrier, inc=1, device_id=(row, peer), device_id_type=pl.DeviceIdType.MESH)
    for k in range(pairs):
        target = base + k

        @pl.when((block != row) | (target != me))
        def _():
            pl.semaphore_signal(barrier, inc=1, device_id=(block, target), device_id_type=pl.DeviceIdType.MESH)
    for r in range(rows):

        @pl.when((r != row) | (source_col != me))
        def _():
            pl.semaphore_signal(barrier, inc=1, device_id=(r, source_col), device_id_type=pl.DeviceIdType.MESH)

    @pl.when(mirrored)
    def _():
        pl.semaphore_wait(barrier, chips + pairs + rows - 2)

    @pl.when(jnp.logical_not(mirrored))
    def _():
        pl.semaphore_wait(barrier, chips + pairs + rows)

    swap = pltpu.make_async_remote_copy(
        src_ref=x_ref.at[:, 1 - core], dst_ref=half_ref, send_sem=send_sems.at[0], recv_sem=recv_sems.at[0],
        device_id=(row, sibling), device_id_type=pl.DeviceIdType.MESH)
    swap.start()
    swap.wait_recv()
    acc[...] = x_ref[:, core] + half_ref[...]
    sent = [swap]
    for d in range(1, chips):
        target = lax.rem(chip + d, chips)
        c = pltpu.make_async_remote_copy(
            src_ref=acc.at[target], dst_ref=recv.at[chip], send_sem=send_sems.at[d], recv_sem=recv_sems.at[d],
            device_id=(row, target * 2 + core), device_id_type=pl.DeviceIdType.MESH)
        c.start()
        sent.append(c)
    total = acc[chip]
    for d in range(1, chips):
        source = lax.rem(chip + chips - d, chips)
        pltpu.make_async_remote_copy(
            src_ref=acc.at[source], dst_ref=recv.at[source], send_sem=send_sems.at[d], recv_sem=recv_sems.at[d],
            device_id=(row, source * 2 + core), device_id_type=pl.DeviceIdType.MESH).wait_recv()
        total = total + recv[source]
    summed[...] = total
    for k in range(pairs):
        send_buf[k] = summed[2 * k:2 * k + 2, :]

    def copy(k, r, device):
        return pltpu.make_async_remote_copy(
            src_ref=send_buf.at[k], dst_ref=out_ref.at[r], send_sem=route_send.at[k], recv_sem=route_recv.at[r],
            device_id=device, device_id_type=pl.DeviceIdType.MESH)

    for k in range(pairs):
        target = base + k

        @pl.when((block != row) | (target != me))
        def _():
            copy(k, row, (block, target)).start()

        @pl.when((block == row) & (target == me))
        def _():
            out_ref[row] = send_buf[k]
    for r in range(rows):

        @pl.when((r != row) | (source_col != me))
        def _():
            copy(0, r, (r, source_col)).wait_recv()
    for k in range(pairs):
        target = base + k

        @pl.when((block != row) | (target != me))
        def _():
            copy(k, row, (block, target)).wait_send()
    for c in sent:
        c.wait_send()


def scatter_route(x, n, rows, collective_id):
    chips = n // 2
    block = x.shape[1:]
    pairs = block[0] // 2
    return pl.pallas_call(
        functools.partial(_scatter_route_kernel, n),
        out_shape=jax.ShapeDtypeStruct((rows, 2, block[1]), x.dtype),
        in_specs=[pl.BlockSpec(memory_space=pltpu.VMEM)],
        out_specs=pl.BlockSpec(memory_space=pltpu.VMEM),
        scratch_shapes=[
            pltpu.VMEM((chips,) + block, x.dtype),
            pltpu.VMEM((chips,) + block, x.dtype),
            pltpu.VMEM((chips,) + block, x.dtype),
            pltpu.VMEM(block, x.dtype),
            pltpu.VMEM((pairs, 2, block[1]), x.dtype),
            pltpu.SemaphoreType.DMA((chips,)),
            pltpu.SemaphoreType.DMA((chips,)),
            pltpu.SemaphoreType.DMA((pairs,)),
            pltpu.SemaphoreType.DMA((rows,)),
        ],
        compiler_params=pltpu.CompilerParams(collective_id=collective_id, has_side_effects=True),
    )(x.reshape((chips, 2) + block))


def _torus_gather_kernel(n, side, x_ref, out_ref, send_sems, recv_sems):
    me = lax.axis_index("col")
    mine = lax.axis_index("row")
    core = lax.rem(me, 2)
    chip = me // 2
    chips = n // 2
    across = lax.rem(chip, side)
    down = chip // side
    sibling = chip * 2 + 1 - core
    width = x_ref.shape[1] // 2
    x_peers = [(down * side + lax.rem(across + d, side)) * 2 + core for d in range(1, side)]
    y_peers = [(lax.rem(down + d, chips // side) * side + across) * 2 + core for d in range(1, chips // side)]
    barrier = pltpu.get_barrier_semaphore()
    for peer in x_peers + y_peers + [sibling]:
        pl.semaphore_signal(barrier, inc=1, device_id=(mine, peer), device_id_type=pl.DeviceIdType.MESH)
    pl.semaphore_wait(barrier, len(x_peers) + len(y_peers) + 1)

    count = [0]
    sent = []

    def push(slot, part, peer, src=None):
        cols = pl.ds(part * width, width)
        copy = pltpu.make_async_remote_copy(
            src_ref=out_ref.at[slot, :, cols] if src is None else src, dst_ref=out_ref.at[slot, :, cols],
            send_sem=send_sems.at[count[0]], recv_sem=recv_sems.at[slot * 2 + part],
            device_id=(mine, peer), device_id_type=pl.DeviceIdType.MESH)
        copy.start()
        count[0] += 1
        sent.append(copy)

    def arrived(slot, part):
        cols = pl.ds(part * width, width)
        pltpu.make_async_remote_copy(
            src_ref=out_ref.at[slot, :, cols], dst_ref=out_ref.at[slot, :, cols],
            send_sem=send_sems.at[0], recv_sem=recv_sems.at[slot * 2 + part],
            device_id=(mine, sibling), device_id_type=pl.DeviceIdType.MESH).wait_recv()

    out_ref[me] = x_ref[...]
    for part, first, second in ((0, x_peers, y_peers), (1, y_peers, x_peers)):
        for peer in first + second + [sibling]:
            push(me, part, peer, x_ref.at[:, pl.ds(part * width, width)])
    for part, first, second in ((0, x_peers, y_peers), (1, y_peers, x_peers)):
        for peer in first:
            arrived(peer, part)
            for other in second + [sibling]:
                push(peer, part, other)
    for part, first, second in ((0, x_peers, y_peers), (1, y_peers, x_peers)):
        for peer in second:
            for line in [peer] + [lax.rem(p + 2 * chips + peer - me, 2 * chips) for p in first]:
                arrived(line, part)
                push(line, part, sibling)
    for slot_chip in range(chips):
        for part in range(2):
            arrived(slot_chip * 2 + 1 - core, part)
    for c in sent:
        c.wait_send()


def torus_gather(x, n, side, collective_id):
    sends = 4 * n
    return pl.pallas_call(
        functools.partial(_torus_gather_kernel, n, side),
        out_shape=jax.ShapeDtypeStruct((n,) + x.shape, x.dtype),
        in_specs=[pl.BlockSpec(memory_space=pltpu.VMEM)],
        out_specs=pl.BlockSpec(memory_space=pltpu.VMEM),
        scratch_shapes=[
            pltpu.SemaphoreType.DMA((sends,)),
            pltpu.SemaphoreType.DMA((2 * n,)),
        ],
        compiler_params=pltpu.CompilerParams(collective_id=collective_id, has_side_effects=True),
    )(x)


def _ring_kernel(n, chunks, keys_ref, weights_ref, stored_ref, terms_ref, own_ref, out_ref, partial_ref, recv_r, recv_l, acc_r, acc_l,
                 rs_sems, ag_sems):
    me = lax.axis_index("row")
    mine = lax.axis_index("col")
    right = lax.rem(me + 1, n)
    left = lax.rem(me + n - 1, n)
    steps_r = n // 2
    steps_l = n - 1 - steps_r
    block = partial_ref.shape[1]
    size = block // chunks
    half = n * chunks
    barrier = pltpu.get_barrier_semaphore()
    for peer in (left, right):
        pl.semaphore_signal(barrier, inc=1, device_id=(peer, mine), device_id_type=pl.DeviceIdType.MESH)
    pl.semaphore_wait(barrier, 2)

    def whiten(d):
        start = pl.multiple_of(d * block, block)
        partial_ref[d] = jnp.dot(keys_ref[pl.ds(start, block), :], weights_ref[...],
                                 preferred_element_type=jnp.float32)

    def intersect(b):
        terms_ref[b] = lax.dot_general(out_ref[b], stored_ref[...], (((1,), (1,)), ((), ())),
                                       preferred_element_type=jnp.float32)

    def send(src, dst, sems, k, peer):
        copy = pltpu.make_async_remote_copy(
            src_ref=src, dst_ref=dst, send_sem=sems.at[k], recv_sem=sems.at[k + 2 * half],
            device_id=(peer, mine), device_id_type=pl.DeviceIdType.MESH)
        copy.start()
        return copy

    sent = []
    got_r = {}
    got_l = {}
    for s in range(steps_r):
        d_r = lax.rem(me + steps_r - s, n)
        d_l = lax.rem(me + n - steps_l + s, n)
        whiten(d_r)
        if s < steps_l:
            whiten(d_l)
        for h in range(chunks):
            rows = pl.ds(h * size, size)
            if s == 0:
                src = partial_ref.at[d_r, rows]
            else:
                got_r[s - 1, h].wait_recv()
                acc_r[s - 1, rows] = recv_r[s - 1, rows] + partial_ref[d_r, rows]
                src = acc_r.at[s - 1, rows]
            got_r[s, h] = send(src, recv_r.at[s, rows], rs_sems, s * chunks + h, right)
            sent.append(got_r[s, h])
            if s < steps_l:
                if s == 0:
                    src = partial_ref.at[d_l, rows]
                else:
                    got_l[s - 1, h].wait_recv()
                    acc_l[s - 1, rows] = recv_l[s - 1, rows] + partial_ref[d_l, rows]
                    src = acc_l.at[s - 1, rows]
                got_l[s, h] = send(src, recv_l.at[s, rows], rs_sems, half + s * chunks + h, left)
                sent.append(got_l[s, h])
    whiten(me)
    for h in range(chunks):
        rows = pl.ds(h * size, size)
        got_r[steps_r - 1, h].wait_recv()
        got_l[steps_l - 1, h].wait_recv()
        total = partial_ref[me, rows] + recv_r[steps_r - 1, rows] + recv_l[steps_l - 1, rows]
        rounded = total.astype(out_ref.dtype)
        out_ref[me, rows] = rounded
        own_ref[rows] = rounded

    ag_r = {}
    ag_l = {}
    for t in range(steps_r):
        for h in range(chunks):
            rows = pl.ds(h * size, size)
            b_r = lax.rem(me + n - t, n)
            if t:
                ag_r[t - 1, h].wait_recv()
            ag_r[t, h] = send(out_ref.at[b_r, rows], out_ref.at[b_r, rows], ag_sems, t * chunks + h, right)
            sent.append(ag_r[t, h])
            if t < steps_l:
                b_l = lax.rem(me + t, n)
                if t:
                    ag_l[t - 1, h].wait_recv()
                ag_l[t, h] = send(out_ref.at[b_l, rows], out_ref.at[b_l, rows], ag_sems, half + t * chunks + h, left)
                sent.append(ag_l[t, h])
        intersect(lax.rem(me + n - t, n))
        if t and t < steps_l:
            intersect(lax.rem(me + t, n))
    for h in range(chunks):
        ag_r[steps_r - 1, h].wait_recv()
        ag_l[steps_l - 1, h].wait_recv()
    intersect(lax.rem(me + n - steps_r, n))
    intersect(lax.rem(me + steps_l, n))
    for c in sent:
        c.wait_send()


def row_ring(keys, weights, stored, n, collective_id, chunks=2):
    rows = keys.shape[0] // n
    width = weights.shape[1]
    slots = stored.shape[0]
    steps_r = n // 2
    steps_l = n - 1 - steps_r
    return pl.pallas_call(
        functools.partial(_ring_kernel, n, chunks),
        out_shape=(jax.ShapeDtypeStruct((n, rows, slots), jnp.float32),
                   jax.ShapeDtypeStruct((rows, width), jnp.bfloat16)),
        in_specs=[pl.BlockSpec(memory_space=pltpu.VMEM)] * 3,
        out_specs=(pl.BlockSpec(memory_space=pltpu.VMEM), pl.BlockSpec(memory_space=pltpu.VMEM)),
        scratch_shapes=[
            pltpu.VMEM((n, rows, width), jnp.bfloat16),
            pltpu.VMEM((n, rows, width), jnp.float32),
            pltpu.VMEM((steps_r, rows, width), jnp.float32),
            pltpu.VMEM((steps_l, rows, width), jnp.float32),
            pltpu.VMEM((steps_r - 1, rows, width), jnp.float32),
            pltpu.VMEM((steps_l - 1, rows, width), jnp.float32),
            pltpu.SemaphoreType.DMA((4 * n * chunks,)),
            pltpu.SemaphoreType.DMA((4 * n * chunks,)),
        ],
        compiler_params=pltpu.CompilerParams(collective_id=collective_id, has_side_effects=True),
    )(keys, weights, stored)


def shards(new_keys, precision, stored_keys, pair_batch, pair_count, batch_length, batch_slot):
    row_count = lax.axis_size("row")
    col_count = lax.axis_size("col")
    row_index = lax.axis_index("row")
    total_keys = new_keys.shape[0] * col_count
    block_keys = total_keys // row_count
    part_keys = block_keys // col_count
    local_batches, batch_keys, width = stored_keys.shape
    gathered = torus_gather(new_keys, col_count, 4, 0)
    terms, whitened = row_ring(gathered.reshape(total_keys, new_keys.shape[1]), precision,
                               stored_keys.reshape(local_batches * batch_keys, width), row_count, 3)
    terms = terms.reshape(col_count, block_keys // 2, local_batches * batch_keys)
    routed = scatter_route(terms, col_count, row_count, 1)
    table = routed.reshape(row_count, part_keys, local_batches, batch_keys).transpose(0, 2, 1, 3)
    table = table.reshape(row_count * local_batches, part_keys, batch_keys)
    listed = pair_batch[row_index]
    slots = batch_slot[listed]
    lengths = batch_length[listed]
    count = pair_count[row_index]
    picked = jnp.take(table, slots, axis=0)
    places = jnp.arange(slots.shape[0], dtype=jnp.int32)
    columns = jnp.arange(batch_keys, dtype=jnp.int32)
    keep = (places < count)[:, None, None] & (columns[None, None, :] < lengths[:, None, None])
    shares = jnp.where(keep, picked, jnp.zeros_like(picked))
    return (whitened, shares[None])


def solution(mesh):
    placed = (P("col", "row"), P("row", "col"), P("row", None, "col"), P(), P(), P(), P())
    return jax.shard_map(
        shards,
        mesh=mesh,
        in_specs=placed,
        out_specs=(P("row", "col"), P("row", None, "col", None)),
        check_vma=False,
    )
```

```python
import functools

import jax
import jax.numpy as jnp
from jax import lax
from jax.experimental import pallas as pl
from jax.experimental.pallas import tpu as pltpu
from jax.sharding import PartitionSpec as P


def _exchange_kernel(axis, other, n, gather, x_ref, out_ref, send_sems, recv_sems):
    me = lax.axis_index(axis)
    mine = lax.axis_index(other)

    def at(peer):
        return (peer, mine) if axis == "row" else (mine, peer)

    barrier = pltpu.get_barrier_semaphore()
    for d in range(1, n):
        peer = lax.rem(me + d, n)
        pl.semaphore_signal(barrier, inc=1, device_id=at(peer), device_id_type=pl.DeviceIdType.MESH)
    pl.semaphore_wait(barrier, n - 1)
    copies = []
    for d in range(1, n):
        peer = lax.rem(me + d, n)
        src = x_ref if gather else x_ref.at[peer]
        copy = pltpu.make_async_remote_copy(
            src_ref=src, dst_ref=out_ref.at[me], send_sem=send_sems.at[d], recv_sem=recv_sems.at[d],
            device_id=at(peer), device_id_type=pl.DeviceIdType.MESH)
        copy.start()
        copies.append(copy)
    if gather:
        out_ref[me] = x_ref[...]
    else:
        out_ref[me] = x_ref[me]
    for d in range(1, n):
        copies[d - 1].wait_send()
        source = lax.rem(me + n - d, n)
        src = x_ref if gather else x_ref.at[source]
        incoming = pltpu.make_async_remote_copy(
            src_ref=src, dst_ref=out_ref.at[source], send_sem=send_sems.at[d], recv_sem=recv_sems.at[d],
            device_id=at(source), device_id_type=pl.DeviceIdType.MESH)
        incoming.wait_recv()


def exchange(x, axis, other, n, gather, collective_id):
    block = x.shape if gather else x.shape[1:]
    return pl.pallas_call(
        functools.partial(_exchange_kernel, axis, other, n, gather),
        out_shape=jax.ShapeDtypeStruct((n,) + tuple(block), x.dtype),
        in_specs=[pl.BlockSpec(memory_space=pltpu.VMEM)],
        out_specs=pl.BlockSpec(memory_space=pltpu.VMEM),
        scratch_shapes=[pltpu.SemaphoreType.DMA((n,)), pltpu.SemaphoreType.DMA((n,))],
        compiler_params=pltpu.CompilerParams(collective_id=collective_id, has_side_effects=True),
    )(x)


def _gather_kernel(n, x_ref, out_ref, send_sems, forward_sems, recv_sems):
    me = lax.axis_index("col")
    mine = lax.axis_index("row")
    core = lax.rem(me, 2)
    chip = me // 2
    chips = n // 2
    sibling = chip * 2 + 1 - core
    peers = [lax.rem(chip + d, chips) * 2 + core for d in range(1, chips)]
    barrier = pltpu.get_barrier_semaphore()
    for peer in peers + [sibling]:
        pl.semaphore_signal(barrier, inc=1, device_id=(mine, peer), device_id_type=pl.DeviceIdType.MESH)
    pl.semaphore_wait(barrier, chips)

    def copy(src, slot, sem, peer):
        return pltpu.make_async_remote_copy(
            src_ref=src, dst_ref=out_ref.at[slot], send_sem=sem, recv_sem=recv_sems.at[slot],
            device_id=(mine, peer), device_id_type=pl.DeviceIdType.MESH)

    sent = []
    for d, peer in enumerate(peers + [sibling]):
        c = copy(x_ref, me, send_sems.at[d], peer)
        c.start()
        sent.append(c)
    out_ref[me] = x_ref[...]
    for d, peer in enumerate(peers):
        copy(x_ref, peer, send_sems.at[d], peer).wait_recv()
        c = copy(out_ref.at[peer], peer, forward_sems.at[d], sibling)
        c.start()
        sent.append(c)
    copy(x_ref, sibling, send_sems.at[0], sibling).wait_recv()
    for d in range(1, chips):
        far = lax.rem(chip + d, chips) * 2 + 1 - core
        copy(x_ref, far, send_sems.at[0], sibling).wait_recv()
    for c in sent:
        c.wait_send()


def col_gather(x, n, collective_id):
    return pl.pallas_call(
        functools.partial(_gather_kernel, n),
        out_shape=jax.ShapeDtypeStruct((n,) + x.shape, x.dtype),
        in_specs=[pl.BlockSpec(memory_space=pltpu.VMEM)],
        out_specs=pl.BlockSpec(memory_space=pltpu.VMEM),
        scratch_shapes=[
            pltpu.SemaphoreType.DMA((n,)),
            pltpu.SemaphoreType.DMA((n,)),
            pltpu.SemaphoreType.DMA((n,)),
        ],
        compiler_params=pltpu.CompilerParams(collective_id=collective_id, has_side_effects=True),
    )(x)


def _scatter_kernel(n, x_ref, out_ref, half, recv, acc, send_sems, recv_sems):
    me = lax.axis_index("col")
    mine = lax.axis_index("row")
    core = lax.rem(me, 2)
    chip = me // 2
    chips = n // 2
    sibling = chip * 2 + 1 - core
    peers = [lax.rem(chip + d, chips) * 2 + core for d in range(1, chips)]
    barrier = pltpu.get_barrier_semaphore()
    for peer in peers + [sibling]:
        pl.semaphore_signal(barrier, inc=1, device_id=(mine, peer), device_id_type=pl.DeviceIdType.MESH)
    pl.semaphore_wait(barrier, chips)

    swap = pltpu.make_async_remote_copy(
        src_ref=x_ref.at[:, 1 - core], dst_ref=half, send_sem=send_sems.at[0], recv_sem=recv_sems.at[0],
        device_id=(mine, sibling), device_id_type=pl.DeviceIdType.MESH)
    swap.start()
    swap.wait_recv()
    acc[...] = x_ref[:, core] + half[...]
    sent = [swap]
    for d in range(1, chips):
        target = lax.rem(chip + d, chips)
        c = pltpu.make_async_remote_copy(
            src_ref=acc.at[target], dst_ref=recv.at[chip], send_sem=send_sems.at[d], recv_sem=recv_sems.at[d],
            device_id=(mine, target * 2 + core), device_id_type=pl.DeviceIdType.MESH)
        c.start()
        sent.append(c)
    total = acc[chip]
    for d in range(1, chips):
        source = lax.rem(chip + chips - d, chips)
        pltpu.make_async_remote_copy(
            src_ref=acc.at[source], dst_ref=recv.at[source], send_sem=send_sems.at[d], recv_sem=recv_sems.at[d],
            device_id=(mine, source * 2 + core), device_id_type=pl.DeviceIdType.MESH).wait_recv()
        total = total + recv[source]
    out_ref[...] = total
    for c in sent:
        c.wait_send()


def col_scatter(x, n, collective_id):
    chips = n // 2
    block = x.shape[1:]
    return pl.pallas_call(
        functools.partial(_scatter_kernel, n),
        out_shape=jax.ShapeDtypeStruct(block, x.dtype),
        in_specs=[pl.BlockSpec(memory_space=pltpu.VMEM)],
        out_specs=pl.BlockSpec(memory_space=pltpu.VMEM),
        scratch_shapes=[
            pltpu.VMEM((chips,) + block, x.dtype),
            pltpu.VMEM((chips,) + block, x.dtype),
            pltpu.VMEM((chips,) + block, x.dtype),
            pltpu.SemaphoreType.DMA((chips,)),
            pltpu.SemaphoreType.DMA((chips,)),
        ],
        compiler_params=pltpu.CompilerParams(collective_id=collective_id, has_side_effects=True),
    )(x.reshape((chips, 2) + block))


def _route_kernel(x_ref, out_ref, send_buf, send_sems, recv_sems):
    row = lax.axis_index("row")
    col = lax.axis_index("col")
    pairs = x_ref.shape[0] // 2
    rows = lax.axis_size("row")
    block = col // 2
    half = lax.rem(col, 2)
    base = pairs * half
    source_col = 2 * row + col // pairs
    mirrored = (row == block) & (col // pairs == half)

    barrier = pltpu.get_barrier_semaphore()
    for k in range(pairs):
        target = base + k

        @pl.when((block != row) | (target != col))
        def _():
            pl.semaphore_signal(barrier, inc=1, device_id=(block, target), device_id_type=pl.DeviceIdType.MESH)
    for r in range(rows):

        @pl.when((r != row) | (source_col != col))
        def _():
            pl.semaphore_signal(barrier, inc=1, device_id=(r, source_col), device_id_type=pl.DeviceIdType.MESH)

    @pl.when(mirrored)
    def _():
        pl.semaphore_wait(barrier, pairs + rows - 2)

    @pl.when(jnp.logical_not(mirrored))
    def _():
        pl.semaphore_wait(barrier, pairs + rows)

    for k in range(pairs):
        send_buf[k] = x_ref[2 * k:2 * k + 2, :]

    def copy(k, r, device):
        return pltpu.make_async_remote_copy(
            src_ref=send_buf.at[k], dst_ref=out_ref.at[r], send_sem=send_sems.at[k], recv_sem=recv_sems.at[r],
            device_id=device, device_id_type=pl.DeviceIdType.MESH)

    for k in range(pairs):
        target = base + k

        @pl.when((block != row) | (target != col))
        def _():
            copy(k, row, (block, target)).start()

        @pl.when((block == row) & (target == col))
        def _():
            out_ref[row] = send_buf[k]
    for r in range(rows):

        @pl.when((r != row) | (source_col != col))
        def _():
            copy(0, r, (r, source_col)).wait_recv()
    for k in range(pairs):
        target = base + k

        @pl.when((block != row) | (target != col))
        def _():
            copy(k, row, (block, target)).wait_send()


def route(x, rows, collective_id):
    pairs = x.shape[0] // 2
    return pl.pallas_call(
        _route_kernel,
        out_shape=jax.ShapeDtypeStruct((rows, 2, x.shape[1]), x.dtype),
        in_specs=[pl.BlockSpec(memory_space=pltpu.VMEM)],
        out_specs=pl.BlockSpec(memory_space=pltpu.VMEM),
        scratch_shapes=[
            pltpu.VMEM((pairs, 2, x.shape[1]), x.dtype),
            pltpu.SemaphoreType.DMA((pairs,)),
            pltpu.SemaphoreType.DMA((rows,)),
        ],
        compiler_params=pltpu.CompilerParams(collective_id=collective_id, has_side_effects=True),
    )(x)


def _scatter_route_kernel(n, side, x_ref, out_ref, half_ref, recv_a, recv_b, part_sum, acc, summed, send_buf,
                          send_sems, recv_sems, route_send, route_recv):
    me = lax.axis_index("col")
    row = lax.axis_index("row")
    rows = lax.axis_size("row")
    core = lax.rem(me, 2)
    chip = me // 2
    chips = n // 2
    pairs = summed.shape[0] // 2
    sibling = chip * 2 + 1 - core
    across = lax.rem(chip, side)
    down = chip // side
    lines = chips // side
    peers = [(down * side + lax.rem(across + d, side)) * 2 + core for d in range(1, side)]
    peers += [(lax.rem(down + d, lines) * side + across) * 2 + core for d in range(1, lines)]
    block = me // 2
    base = pairs * core
    source_col = 2 * row + me // pairs
    mirrored = (row == block) & (me // pairs == core)

    barrier = pltpu.get_barrier_semaphore()
    for peer in peers + [sibling]:
        pl.semaphore_signal(barrier, inc=1, device_id=(row, peer), device_id_type=pl.DeviceIdType.MESH)
    for k in range(pairs):
        target = base + k

        @pl.when((block != row) | (target != me))
        def _():
            pl.semaphore_signal(barrier, inc=1, device_id=(block, target), device_id_type=pl.DeviceIdType.MESH)
    for r in range(rows):

        @pl.when((r != row) | (source_col != me))
        def _():
            pl.semaphore_signal(barrier, inc=1, device_id=(r, source_col), device_id_type=pl.DeviceIdType.MESH)

    @pl.when(mirrored)
    def _():
        pl.semaphore_wait(barrier, len(peers) + 1 + pairs + rows - 2)

    @pl.when(jnp.logical_not(mirrored))
    def _():
        pl.semaphore_wait(barrier, len(peers) + 1 + pairs + rows)

    swap = pltpu.make_async_remote_copy(
        src_ref=x_ref.at[:, 1 - core], dst_ref=half_ref, send_sem=send_sems.at[0], recv_sem=recv_sems.at[0],
        device_id=(row, sibling), device_id_type=pl.DeviceIdType.MESH)
    swap.start()
    swap.wait_recv()
    acc[...] = x_ref[:, core] + half_ref[...]
    sent = [swap]
    width = acc.shape[2] // 2
    count = [1]

    def chip_at(y, x):
        return y * side + x

    def copy(src, dst, sem, peer_chip):
        c = pltpu.make_async_remote_copy(
            src_ref=src, dst_ref=dst, send_sem=send_sems.at[count[0]], recv_sem=recv_sems.at[sem],
            device_id=(row, peer_chip * 2 + core), device_id_type=pl.DeviceIdType.MESH)
        return c

    for part in range(2):
        cols = pl.ds(part * width, width)
        mine_first, mine_second = (across, down) if part == 0 else (down, across)
        size_first, size_second = (side, lines) if part == 0 else (lines, side)

        def place(first, second):
            return chip_at(second, first) if part == 0 else chip_at(first, second)

        for d in range(1, size_first):
            far = lax.rem(mine_first + d, size_first)
            for k in range(size_second):
                c = copy(acc.at[place(far, k), :, cols], recv_a.at[part, mine_first, k],
                         16 + part * 16 + mine_first * 4 + k, place(far, mine_second))
                c.start()
                count[0] += 1
                sent.append(c)
        for d in range(1, size_first):
            near = lax.rem(mine_first + size_first - d, size_first)
            for k in range(size_second):
                copy(acc.at[0, :, cols], recv_a.at[part, near, k], 16 + part * 16 + near * 4 + k, 0).wait_recv()
        for k in range(size_second):
            total = acc[place(mine_first, k), :, cols]
            for d in range(1, size_first):
                total = total + recv_a[part, lax.rem(mine_first + d, size_first), k]
            part_sum[part, k] = total
        for d in range(1, size_second):
            far = lax.rem(mine_second + d, size_second)
            c = copy(part_sum.at[part, far], recv_b.at[part, mine_second], 48 + part * 4 + mine_second,
                     place(mine_first, far))
            c.start()
            count[0] += 1
            sent.append(c)
        total = part_sum[part, mine_second]
        for d in range(1, size_second):
            near = lax.rem(mine_second + size_second - d, size_second)
            copy(part_sum.at[part, 0], recv_b.at[part, near], 48 + part * 4 + near, 0).wait_recv()
            total = total + recv_b[part, near]
        summed[:, cols] = total
    for k in range(pairs):
        send_buf[k] = summed[2 * k:2 * k + 2, :]

    def copy(k, r, device):
        return pltpu.make_async_remote_copy(
            src_ref=send_buf.at[k], dst_ref=out_ref.at[r], send_sem=route_send.at[k], recv_sem=route_recv.at[r],
            device_id=device, device_id_type=pl.DeviceIdType.MESH)

    for k in range(pairs):
        target = base + k

        @pl.when((block != row) | (target != me))
        def _():
            copy(k, row, (block, target)).start()

        @pl.when((block == row) & (target == me))
        def _():
            out_ref[row] = send_buf[k]
    for r in range(rows):

        @pl.when((r != row) | (source_col != me))
        def _():
            copy(0, r, (r, source_col)).wait_recv()
    for k in range(pairs):
        target = base + k

        @pl.when((block != row) | (target != me))
        def _():
            copy(k, row, (block, target)).wait_send()
    for c in sent:
        c.wait_send()


def scatter_route(x, n, rows, collective_id, side=4):
    chips = n // 2
    block = x.shape[1:]
    pairs = block[0] // 2
    lines = chips // side
    width = block[1] // 2
    return pl.pallas_call(
        functools.partial(_scatter_route_kernel, n, side),
        out_shape=jax.ShapeDtypeStruct((rows, 2, block[1]), x.dtype),
        in_specs=[pl.BlockSpec(memory_space=pltpu.VMEM)],
        out_specs=pl.BlockSpec(memory_space=pltpu.VMEM),
        scratch_shapes=[
            pltpu.VMEM((chips,) + block, x.dtype),
            pltpu.VMEM((2, max(side, lines), max(side, lines), block[0], width), x.dtype),
            pltpu.VMEM((2, max(side, lines), block[0], width), x.dtype),
            pltpu.VMEM((2, max(side, lines), block[0], width), x.dtype),
            pltpu.VMEM((chips,) + block, x.dtype),
            pltpu.VMEM(block, x.dtype),
            pltpu.VMEM((pairs, 2, block[1]), x.dtype),
            pltpu.SemaphoreType.DMA((64,)),
            pltpu.SemaphoreType.DMA((64,)),
            pltpu.SemaphoreType.DMA((pairs,)),
            pltpu.SemaphoreType.DMA((rows,)),
        ],
        compiler_params=pltpu.CompilerParams(collective_id=collective_id, has_side_effects=True),
    )(x.reshape((chips, 2) + block))


def _torus_gather_kernel(n, side, x_ref, out_ref, send_sems, recv_sems):
    me = lax.axis_index("col")
    mine = lax.axis_index("row")
    core = lax.rem(me, 2)
    chip = me // 2
    chips = n // 2
    across = lax.rem(chip, side)
    down = chip // side
    sibling = chip * 2 + 1 - core
    width = x_ref.shape[1] // 2
    x_peers = [(down * side + lax.rem(across + d, side)) * 2 + core for d in range(1, side)]
    y_peers = [(lax.rem(down + d, chips // side) * side + across) * 2 + core for d in range(1, chips // side)]
    barrier = pltpu.get_barrier_semaphore()
    for peer in x_peers + y_peers + [sibling]:
        pl.semaphore_signal(barrier, inc=1, device_id=(mine, peer), device_id_type=pl.DeviceIdType.MESH)
    pl.semaphore_wait(barrier, len(x_peers) + len(y_peers) + 1)

    count = [0]
    sent = []

    def push(slot, part, peer, src=None):
        cols = pl.ds(part * width, width)
        copy = pltpu.make_async_remote_copy(
            src_ref=out_ref.at[slot, :, cols] if src is None else src, dst_ref=out_ref.at[slot, :, cols],
            send_sem=send_sems.at[count[0]], recv_sem=recv_sems.at[slot * 2 + part],
            device_id=(mine, peer), device_id_type=pl.DeviceIdType.MESH)
        copy.start()
        count[0] += 1
        sent.append(copy)

    def arrived(slot, part):
        cols = pl.ds(part * width, width)
        pltpu.make_async_remote_copy(
            src_ref=out_ref.at[slot, :, cols], dst_ref=out_ref.at[slot, :, cols],
            send_sem=send_sems.at[0], recv_sem=recv_sems.at[slot * 2 + part],
            device_id=(mine, sibling), device_id_type=pl.DeviceIdType.MESH).wait_recv()

    out_ref[me] = x_ref[...]
    for part, first, second in ((0, x_peers, y_peers), (1, y_peers, x_peers)):
        for peer in first + second + [sibling]:
            push(me, part, peer, x_ref.at[:, pl.ds(part * width, width)])
    for part, first, second in ((0, x_peers, y_peers), (1, y_peers, x_peers)):
        for peer in first:
            arrived(peer, part)
            for other in second + [sibling]:
                push(peer, part, other)
    for part, first, second in ((0, x_peers, y_peers), (1, y_peers, x_peers)):
        for peer in second:
            for line in [peer] + [lax.rem(p + 2 * chips + peer - me, 2 * chips) for p in first]:
                arrived(line, part)
                push(line, part, sibling)
    for slot_chip in range(chips):
        for part in range(2):
            arrived(slot_chip * 2 + 1 - core, part)
    for c in sent:
        c.wait_send()


def torus_gather(x, n, side, collective_id):
    sends = 4 * n
    return pl.pallas_call(
        functools.partial(_torus_gather_kernel, n, side),
        out_shape=jax.ShapeDtypeStruct((n,) + x.shape, x.dtype),
        in_specs=[pl.BlockSpec(memory_space=pltpu.VMEM)],
        out_specs=pl.BlockSpec(memory_space=pltpu.VMEM),
        scratch_shapes=[
            pltpu.SemaphoreType.DMA((sends,)),
            pltpu.SemaphoreType.DMA((2 * n,)),
        ],
        compiler_params=pltpu.CompilerParams(collective_id=collective_id, has_side_effects=True),
    )(x)


def _ring_kernel(n, chunks, keys_ref, weights_ref, stored_ref, terms_ref, own_ref, out_ref, partial_ref, recv_r, recv_l, acc_r, acc_l,
                 rs_sems, ag_sems):
    me = lax.axis_index("row")
    mine = lax.axis_index("col")
    right = lax.rem(me + 1, n)
    left = lax.rem(me + n - 1, n)
    steps_r = n // 2
    steps_l = n - 1 - steps_r
    block = partial_ref.shape[1]
    size = block // chunks
    half = n * chunks
    barrier = pltpu.get_barrier_semaphore()
    for peer in (left, right):
        pl.semaphore_signal(barrier, inc=1, device_id=(peer, mine), device_id_type=pl.DeviceIdType.MESH)
    pl.semaphore_wait(barrier, 2)

    def whiten(d):
        start = pl.multiple_of(d * block, block)
        partial_ref[d] = jnp.dot(keys_ref[pl.ds(start, block), :], weights_ref[...],
                                 preferred_element_type=jnp.float32)

    def intersect(b):
        terms_ref[b] = lax.dot_general(out_ref[b], stored_ref[...], (((1,), (1,)), ((), ())),
                                       preferred_element_type=jnp.float32)

    def send(src, dst, sems, k, peer):
        copy = pltpu.make_async_remote_copy(
            src_ref=src, dst_ref=dst, send_sem=sems.at[k], recv_sem=sems.at[k + 2 * half],
            device_id=(peer, mine), device_id_type=pl.DeviceIdType.MESH)
        copy.start()
        return copy

    sent = []
    got_r = {}
    got_l = {}
    for s in range(steps_r):
        d_r = lax.rem(me + steps_r - s, n)
        d_l = lax.rem(me + n - steps_l + s, n)
        whiten(d_r)
        if s < steps_l:
            whiten(d_l)
        for h in range(chunks):
            rows = pl.ds(h * size, size)
            if s == 0:
                src = partial_ref.at[d_r, rows]
            else:
                got_r[s - 1, h].wait_recv()
                acc_r[s - 1, rows] = recv_r[s - 1, rows] + partial_ref[d_r, rows]
                src = acc_r.at[s - 1, rows]
            got_r[s, h] = send(src, recv_r.at[s, rows], rs_sems, s * chunks + h, right)
            sent.append(got_r[s, h])
            if s < steps_l:
                if s == 0:
                    src = partial_ref.at[d_l, rows]
                else:
                    got_l[s - 1, h].wait_recv()
                    acc_l[s - 1, rows] = recv_l[s - 1, rows] + partial_ref[d_l, rows]
                    src = acc_l.at[s - 1, rows]
                got_l[s, h] = send(src, recv_l.at[s, rows], rs_sems, half + s * chunks + h, left)
                sent.append(got_l[s, h])
    whiten(me)
    for h in range(chunks):
        rows = pl.ds(h * size, size)
        got_r[steps_r - 1, h].wait_recv()
        got_l[steps_l - 1, h].wait_recv()
        total = partial_ref[me, rows] + recv_r[steps_r - 1, rows] + recv_l[steps_l - 1, rows]
        rounded = total.astype(out_ref.dtype)
        out_ref[me, rows] = rounded
        own_ref[rows] = rounded

    ag_r = {}
    ag_l = {}
    for t in range(steps_r):
        for h in range(chunks):
            rows = pl.ds(h * size, size)
            b_r = lax.rem(me + n - t, n)
            if t:
                ag_r[t - 1, h].wait_recv()
            ag_r[t, h] = send(out_ref.at[b_r, rows], out_ref.at[b_r, rows], ag_sems, t * chunks + h, right)
            sent.append(ag_r[t, h])
            if t < steps_l:
                b_l = lax.rem(me + t, n)
                if t:
                    ag_l[t - 1, h].wait_recv()
                ag_l[t, h] = send(out_ref.at[b_l, rows], out_ref.at[b_l, rows], ag_sems, half + t * chunks + h, left)
                sent.append(ag_l[t, h])
        intersect(lax.rem(me + n - t, n))
        if t and t < steps_l:
            intersect(lax.rem(me + t, n))
    for h in range(chunks):
        ag_r[steps_r - 1, h].wait_recv()
        ag_l[steps_l - 1, h].wait_recv()
    intersect(lax.rem(me + n - steps_r, n))
    intersect(lax.rem(me + steps_l, n))
    for c in sent:
        c.wait_send()


def row_ring(keys, weights, stored, n, collective_id, chunks=2):
    rows = keys.shape[0] // n
    width = weights.shape[1]
    slots = stored.shape[0]
    steps_r = n // 2
    steps_l = n - 1 - steps_r
    return pl.pallas_call(
        functools.partial(_ring_kernel, n, chunks),
        out_shape=(jax.ShapeDtypeStruct((n, rows, slots), jnp.float32),
                   jax.ShapeDtypeStruct((rows, width), jnp.bfloat16)),
        in_specs=[pl.BlockSpec(memory_space=pltpu.VMEM)] * 3,
        out_specs=(pl.BlockSpec(memory_space=pltpu.VMEM), pl.BlockSpec(memory_space=pltpu.VMEM)),
        scratch_shapes=[
            pltpu.VMEM((n, rows, width), jnp.bfloat16),
            pltpu.VMEM((n, rows, width), jnp.float32),
            pltpu.VMEM((steps_r, rows, width), jnp.float32),
            pltpu.VMEM((steps_l, rows, width), jnp.float32),
            pltpu.VMEM((steps_r - 1, rows, width), jnp.float32),
            pltpu.VMEM((steps_l - 1, rows, width), jnp.float32),
            pltpu.SemaphoreType.DMA((4 * n * chunks,)),
            pltpu.SemaphoreType.DMA((4 * n * chunks,)),
        ],
        compiler_params=pltpu.CompilerParams(collective_id=collective_id, has_side_effects=True),
    )(keys, weights, stored)


def shards(new_keys, precision, stored_keys, pair_batch, pair_count, batch_length, batch_slot):
    row_count = lax.axis_size("row")
    col_count = lax.axis_size("col")
    row_index = lax.axis_index("row")
    total_keys = new_keys.shape[0] * col_count
    block_keys = total_keys // row_count
    part_keys = block_keys // col_count
    local_batches, batch_keys, width = stored_keys.shape
    gathered = torus_gather(new_keys, col_count, 4, 0)
    terms, whitened = row_ring(gathered.reshape(total_keys, new_keys.shape[1]), precision,
                               stored_keys.reshape(local_batches * batch_keys, width), row_count, 3)
    terms = terms.reshape(col_count, block_keys // 2, local_batches * batch_keys)
    routed = scatter_route(terms, col_count, row_count, 1)
    table = routed.reshape(row_count, part_keys, local_batches, batch_keys).transpose(0, 2, 1, 3)
    table = table.reshape(row_count * local_batches, part_keys, batch_keys)
    listed = pair_batch[row_index]
    slots = batch_slot[listed]
    lengths = batch_length[listed]
    count = pair_count[row_index]
    picked = jnp.take(table, slots, axis=0)
    places = jnp.arange(slots.shape[0], dtype=jnp.int32)
    columns = jnp.arange(batch_keys, dtype=jnp.int32)
    keep = (places < count)[:, None, None] & (columns[None, None, :] < lengths[:, None, None])
    shares = jnp.where(keep, picked, jnp.zeros_like(picked))
    return (whitened, shares[None])


def solution(mesh):
    placed = (P("col", "row"), P("row", "col"), P("row", None, "col"), P(), P(), P(), P())
    return jax.shard_map(
        shards,
        mesh=mesh,
        in_specs=placed,
        out_specs=(P("row", "col"), P("row", None, "col", None)),
        check_vma=False,
    )
```

```python
import functools

import jax
import jax.numpy as jnp
from jax import lax
from jax.experimental import pallas as pl
from jax.experimental.pallas import tpu as pltpu
from jax.sharding import PartitionSpec as P


def _exchange_kernel(axis, other, n, gather, x_ref, out_ref, send_sems, recv_sems):
    me = lax.axis_index(axis)
    mine = lax.axis_index(other)

    def at(peer):
        return (peer, mine) if axis == "row" else (mine, peer)

    barrier = pltpu.get_barrier_semaphore()
    for d in range(1, n):
        peer = lax.rem(me + d, n)
        pl.semaphore_signal(barrier, inc=1, device_id=at(peer), device_id_type=pl.DeviceIdType.MESH)
    pl.semaphore_wait(barrier, n - 1)
    copies = []
    for d in range(1, n):
        peer = lax.rem(me + d, n)
        src = x_ref if gather else x_ref.at[peer]
        copy = pltpu.make_async_remote_copy(
            src_ref=src, dst_ref=out_ref.at[me], send_sem=send_sems.at[d], recv_sem=recv_sems.at[d],
            device_id=at(peer), device_id_type=pl.DeviceIdType.MESH)
        copy.start()
        copies.append(copy)
    if gather:
        out_ref[me] = x_ref[...]
    else:
        out_ref[me] = x_ref[me]
    for d in range(1, n):
        copies[d - 1].wait_send()
        source = lax.rem(me + n - d, n)
        src = x_ref if gather else x_ref.at[source]
        incoming = pltpu.make_async_remote_copy(
            src_ref=src, dst_ref=out_ref.at[source], send_sem=send_sems.at[d], recv_sem=recv_sems.at[d],
            device_id=at(source), device_id_type=pl.DeviceIdType.MESH)
        incoming.wait_recv()


def exchange(x, axis, other, n, gather, collective_id):
    block = x.shape if gather else x.shape[1:]
    return pl.pallas_call(
        functools.partial(_exchange_kernel, axis, other, n, gather),
        out_shape=jax.ShapeDtypeStruct((n,) + tuple(block), x.dtype),
        in_specs=[pl.BlockSpec(memory_space=pltpu.VMEM)],
        out_specs=pl.BlockSpec(memory_space=pltpu.VMEM),
        scratch_shapes=[pltpu.SemaphoreType.DMA((n,)), pltpu.SemaphoreType.DMA((n,))],
        compiler_params=pltpu.CompilerParams(collective_id=collective_id, has_side_effects=True),
    )(x)


def _gather_kernel(n, x_ref, out_ref, send_sems, forward_sems, recv_sems):
    me = lax.axis_index("col")
    mine = lax.axis_index("row")
    core = lax.rem(me, 2)
    chip = me // 2
    chips = n // 2
    sibling = chip * 2 + 1 - core
    peers = [lax.rem(chip + d, chips) * 2 + core for d in range(1, chips)]
    barrier = pltpu.get_barrier_semaphore()
    for peer in peers + [sibling]:
        pl.semaphore_signal(barrier, inc=1, device_id=(mine, peer), device_id_type=pl.DeviceIdType.MESH)
    pl.semaphore_wait(barrier, chips)

    def copy(src, slot, sem, peer):
        return pltpu.make_async_remote_copy(
            src_ref=src, dst_ref=out_ref.at[slot], send_sem=sem, recv_sem=recv_sems.at[slot],
            device_id=(mine, peer), device_id_type=pl.DeviceIdType.MESH)

    sent = []
    for d, peer in enumerate(peers + [sibling]):
        c = copy(x_ref, me, send_sems.at[d], peer)
        c.start()
        sent.append(c)
    out_ref[me] = x_ref[...]
    for d, peer in enumerate(peers):
        copy(x_ref, peer, send_sems.at[d], peer).wait_recv()
        c = copy(out_ref.at[peer], peer, forward_sems.at[d], sibling)
        c.start()
        sent.append(c)
    copy(x_ref, sibling, send_sems.at[0], sibling).wait_recv()
    for d in range(1, chips):
        far = lax.rem(chip + d, chips) * 2 + 1 - core
        copy(x_ref, far, send_sems.at[0], sibling).wait_recv()
    for c in sent:
        c.wait_send()


def col_gather(x, n, collective_id):
    return pl.pallas_call(
        functools.partial(_gather_kernel, n),
        out_shape=jax.ShapeDtypeStruct((n,) + x.shape, x.dtype),
        in_specs=[pl.BlockSpec(memory_space=pltpu.VMEM)],
        out_specs=pl.BlockSpec(memory_space=pltpu.VMEM),
        scratch_shapes=[
            pltpu.SemaphoreType.DMA((n,)),
            pltpu.SemaphoreType.DMA((n,)),
            pltpu.SemaphoreType.DMA((n,)),
        ],
        compiler_params=pltpu.CompilerParams(collective_id=collective_id, has_side_effects=True),
    )(x)


def _scatter_kernel(n, x_ref, out_ref, half, recv, acc, send_sems, recv_sems):
    me = lax.axis_index("col")
    mine = lax.axis_index("row")
    core = lax.rem(me, 2)
    chip = me // 2
    chips = n // 2
    sibling = chip * 2 + 1 - core
    peers = [lax.rem(chip + d, chips) * 2 + core for d in range(1, chips)]
    barrier = pltpu.get_barrier_semaphore()
    for peer in peers + [sibling]:
        pl.semaphore_signal(barrier, inc=1, device_id=(mine, peer), device_id_type=pl.DeviceIdType.MESH)
    pl.semaphore_wait(barrier, chips)

    swap = pltpu.make_async_remote_copy(
        src_ref=x_ref.at[:, 1 - core], dst_ref=half, send_sem=send_sems.at[0], recv_sem=recv_sems.at[0],
        device_id=(mine, sibling), device_id_type=pl.DeviceIdType.MESH)
    swap.start()
    swap.wait_recv()
    acc[...] = x_ref[:, core] + half[...]
    sent = [swap]
    for d in range(1, chips):
        target = lax.rem(chip + d, chips)
        c = pltpu.make_async_remote_copy(
            src_ref=acc.at[target], dst_ref=recv.at[chip], send_sem=send_sems.at[d], recv_sem=recv_sems.at[d],
            device_id=(mine, target * 2 + core), device_id_type=pl.DeviceIdType.MESH)
        c.start()
        sent.append(c)
    total = acc[chip]
    for d in range(1, chips):
        source = lax.rem(chip + chips - d, chips)
        pltpu.make_async_remote_copy(
            src_ref=acc.at[source], dst_ref=recv.at[source], send_sem=send_sems.at[d], recv_sem=recv_sems.at[d],
            device_id=(mine, source * 2 + core), device_id_type=pl.DeviceIdType.MESH).wait_recv()
        total = total + recv[source]
    out_ref[...] = total
    for c in sent:
        c.wait_send()


def col_scatter(x, n, collective_id):
    chips = n // 2
    block = x.shape[1:]
    return pl.pallas_call(
        functools.partial(_scatter_kernel, n),
        out_shape=jax.ShapeDtypeStruct(block, x.dtype),
        in_specs=[pl.BlockSpec(memory_space=pltpu.VMEM)],
        out_specs=pl.BlockSpec(memory_space=pltpu.VMEM),
        scratch_shapes=[
            pltpu.VMEM((chips,) + block, x.dtype),
            pltpu.VMEM((chips,) + block, x.dtype),
            pltpu.VMEM((chips,) + block, x.dtype),
            pltpu.SemaphoreType.DMA((chips,)),
            pltpu.SemaphoreType.DMA((chips,)),
        ],
        compiler_params=pltpu.CompilerParams(collective_id=collective_id, has_side_effects=True),
    )(x.reshape((chips, 2) + block))


def _route_kernel(x_ref, out_ref, send_buf, send_sems, recv_sems):
    row = lax.axis_index("row")
    col = lax.axis_index("col")
    pairs = x_ref.shape[0] // 2
    rows = lax.axis_size("row")
    block = col // 2
    half = lax.rem(col, 2)
    base = pairs * half
    source_col = 2 * row + col // pairs
    mirrored = (row == block) & (col // pairs == half)

    barrier = pltpu.get_barrier_semaphore()
    for k in range(pairs):
        target = base + k

        @pl.when((block != row) | (target != col))
        def _():
            pl.semaphore_signal(barrier, inc=1, device_id=(block, target), device_id_type=pl.DeviceIdType.MESH)
    for r in range(rows):

        @pl.when((r != row) | (source_col != col))
        def _():
            pl.semaphore_signal(barrier, inc=1, device_id=(r, source_col), device_id_type=pl.DeviceIdType.MESH)

    @pl.when(mirrored)
    def _():
        pl.semaphore_wait(barrier, pairs + rows - 2)

    @pl.when(jnp.logical_not(mirrored))
    def _():
        pl.semaphore_wait(barrier, pairs + rows)

    for k in range(pairs):
        send_buf[k] = x_ref[2 * k:2 * k + 2, :]

    def copy(k, r, device):
        return pltpu.make_async_remote_copy(
            src_ref=send_buf.at[k], dst_ref=out_ref.at[r], send_sem=send_sems.at[k], recv_sem=recv_sems.at[r],
            device_id=device, device_id_type=pl.DeviceIdType.MESH)

    for k in range(pairs):
        target = base + k

        @pl.when((block != row) | (target != col))
        def _():
            copy(k, row, (block, target)).start()

        @pl.when((block == row) & (target == col))
        def _():
            out_ref[row] = send_buf[k]
    for r in range(rows):

        @pl.when((r != row) | (source_col != col))
        def _():
            copy(0, r, (r, source_col)).wait_recv()
    for k in range(pairs):
        target = base + k

        @pl.when((block != row) | (target != col))
        def _():
            copy(k, row, (block, target)).wait_send()


def route(x, rows, collective_id):
    pairs = x.shape[0] // 2
    return pl.pallas_call(
        _route_kernel,
        out_shape=jax.ShapeDtypeStruct((rows, 2, x.shape[1]), x.dtype),
        in_specs=[pl.BlockSpec(memory_space=pltpu.VMEM)],
        out_specs=pl.BlockSpec(memory_space=pltpu.VMEM),
        scratch_shapes=[
            pltpu.VMEM((pairs, 2, x.shape[1]), x.dtype),
            pltpu.SemaphoreType.DMA((pairs,)),
            pltpu.SemaphoreType.DMA((rows,)),
        ],
        compiler_params=pltpu.CompilerParams(collective_id=collective_id, has_side_effects=True),
    )(x)


def _scatter_route_kernel(n, x_ref, out_ref, half_ref, recv, acc, summed, send_buf, send_sems, recv_sems,
                          route_send, route_recv):
    me = lax.axis_index("col")
    row = lax.axis_index("row")
    rows = lax.axis_size("row")
    core = lax.rem(me, 2)
    chip = me // 2
    chips = n // 2
    pairs = summed.shape[0] // 2
    sibling = chip * 2 + 1 - core
    peers = [lax.rem(chip + d, chips) * 2 + core for d in range(1, chips)]
    block = me // 2
    base = pairs * core
    source_col = 2 * row + me // pairs
    mirrored = (row == block) & (me // pairs == core)

    barrier = pltpu.get_barrier_semaphore()
    for peer in peers + [sibling]:
        pl.semaphore_signal(barrier, inc=1, device_id=(row, peer), device_id_type=pl.DeviceIdType.MESH)
    for k in range(pairs):
        target = base + k

        @pl.when((block != row) | (target != me))
        def _():
            pl.semaphore_signal(barrier, inc=1, device_id=(block, target), device_id_type=pl.DeviceIdType.MESH)
    for r in range(rows):

        @pl.when((r != row) | (source_col != me))
        def _():
            pl.semaphore_signal(barrier, inc=1, device_id=(r, source_col), device_id_type=pl.DeviceIdType.MESH)

    @pl.when(mirrored)
    def _():
        pl.semaphore_wait(barrier, chips + pairs + rows - 2)

    @pl.when(jnp.logical_not(mirrored))
    def _():
        pl.semaphore_wait(barrier, chips + pairs + rows)

    swap = pltpu.make_async_remote_copy(
        src_ref=x_ref.at[:, 1 - core], dst_ref=half_ref, send_sem=send_sems.at[0], recv_sem=recv_sems.at[0],
        device_id=(row, sibling), device_id_type=pl.DeviceIdType.MESH)
    swap.start()
    swap.wait_recv()
    acc[...] = x_ref[:, core] + half_ref[...]
    sent = [swap]
    for d in range(1, chips):
        target = lax.rem(chip + d, chips)
        c = pltpu.make_async_remote_copy(
            src_ref=acc.at[target], dst_ref=recv.at[chip], send_sem=send_sems.at[d], recv_sem=recv_sems.at[d],
            device_id=(row, target * 2 + core), device_id_type=pl.DeviceIdType.MESH)
        c.start()
        sent.append(c)
    total = acc[chip]
    for d in range(1, chips):
        source = lax.rem(chip + chips - d, chips)
        pltpu.make_async_remote_copy(
            src_ref=acc.at[source], dst_ref=recv.at[source], send_sem=send_sems.at[d], recv_sem=recv_sems.at[d],
            device_id=(row, source * 2 + core), device_id_type=pl.DeviceIdType.MESH).wait_recv()
        total = total + recv[source]
    summed[...] = total
    for k in range(pairs):
        send_buf[k] = summed[2 * k:2 * k + 2, :]

    def copy(k, r, device):
        return pltpu.make_async_remote_copy(
            src_ref=send_buf.at[k], dst_ref=out_ref.at[r], send_sem=route_send.at[k], recv_sem=route_recv.at[r],
            device_id=device, device_id_type=pl.DeviceIdType.MESH)

    for k in range(pairs):
        target = base + k

        @pl.when((block != row) | (target != me))
        def _():
            copy(k, row, (block, target)).start()

        @pl.when((block == row) & (target == me))
        def _():
            out_ref[row] = send_buf[k]
    for r in range(rows):

        @pl.when((r != row) | (source_col != me))
        def _():
            copy(0, r, (r, source_col)).wait_recv()
    for k in range(pairs):
        target = base + k

        @pl.when((block != row) | (target != me))
        def _():
            copy(k, row, (block, target)).wait_send()
    for c in sent:
        c.wait_send()


def scatter_route(x, n, rows, collective_id):
    chips = n // 2
    block = x.shape[1:]
    pairs = block[0] // 2
    return pl.pallas_call(
        functools.partial(_scatter_route_kernel, n),
        out_shape=jax.ShapeDtypeStruct((rows, 2, block[1]), x.dtype),
        in_specs=[pl.BlockSpec(memory_space=pltpu.VMEM)],
        out_specs=pl.BlockSpec(memory_space=pltpu.VMEM),
        scratch_shapes=[
            pltpu.VMEM((chips,) + block, x.dtype),
            pltpu.VMEM((chips,) + block, x.dtype),
            pltpu.VMEM((chips,) + block, x.dtype),
            pltpu.VMEM(block, x.dtype),
            pltpu.VMEM((pairs, 2, block[1]), x.dtype),
            pltpu.SemaphoreType.DMA((chips,)),
            pltpu.SemaphoreType.DMA((chips,)),
            pltpu.SemaphoreType.DMA((pairs,)),
            pltpu.SemaphoreType.DMA((rows,)),
        ],
        compiler_params=pltpu.CompilerParams(collective_id=collective_id, has_side_effects=True),
    )(x.reshape((chips, 2) + block))


def _torus_gather_kernel(n, side, x_ref, out_ref, send_sems, recv_sems):
    me = lax.axis_index("col")
    mine = lax.axis_index("row")
    core = lax.rem(me, 2)
    chip = me // 2
    chips = n // 2
    across = lax.rem(chip, side)
    down = chip // side
    sibling = chip * 2 + 1 - core
    width = x_ref.shape[1] // 2
    x_peers = [(down * side + lax.rem(across + d, side)) * 2 + core for d in range(1, side)]
    y_peers = [(lax.rem(down + d, chips // side) * side + across) * 2 + core for d in range(1, chips // side)]
    barrier = pltpu.get_barrier_semaphore()
    for peer in x_peers + y_peers + [sibling]:
        pl.semaphore_signal(barrier, inc=1, device_id=(mine, peer), device_id_type=pl.DeviceIdType.MESH)
    pl.semaphore_wait(barrier, len(x_peers) + len(y_peers) + 1)

    count = [0]
    sent = []

    def push(slot, part, peer, src=None):
        cols = pl.ds(part * width, width)
        copy = pltpu.make_async_remote_copy(
            src_ref=out_ref.at[slot, :, cols] if src is None else src, dst_ref=out_ref.at[slot, :, cols],
            send_sem=send_sems.at[count[0]], recv_sem=recv_sems.at[slot * 2 + part],
            device_id=(mine, peer), device_id_type=pl.DeviceIdType.MESH)
        copy.start()
        count[0] += 1
        sent.append(copy)

    def arrived(slot, part):
        cols = pl.ds(part * width, width)
        pltpu.make_async_remote_copy(
            src_ref=out_ref.at[slot, :, cols], dst_ref=out_ref.at[slot, :, cols],
            send_sem=send_sems.at[0], recv_sem=recv_sems.at[slot * 2 + part],
            device_id=(mine, sibling), device_id_type=pl.DeviceIdType.MESH).wait_recv()

    out_ref[me] = x_ref[...]
    for part, first, second in ((0, x_peers, y_peers), (1, y_peers, x_peers)):
        for peer in first + second + [sibling]:
            push(me, part, peer, x_ref.at[:, pl.ds(part * width, width)])
    for part, first, second in ((0, x_peers, y_peers), (1, y_peers, x_peers)):
        for peer in first:
            arrived(peer, part)
            for other in second + [sibling]:
                push(peer, part, other)
    for part, first, second in ((0, x_peers, y_peers), (1, y_peers, x_peers)):
        for peer in second:
            for line in [peer] + [lax.rem(p + 2 * chips + peer - me, 2 * chips) for p in first]:
                arrived(line, part)
                push(line, part, sibling)
    for slot_chip in range(chips):
        for part in range(2):
            arrived(slot_chip * 2 + 1 - core, part)
    for c in sent:
        c.wait_send()


def torus_gather(x, n, side, collective_id):
    sends = 4 * n
    return pl.pallas_call(
        functools.partial(_torus_gather_kernel, n, side),
        out_shape=jax.ShapeDtypeStruct((n,) + x.shape, x.dtype),
        in_specs=[pl.BlockSpec(memory_space=pltpu.VMEM)],
        out_specs=pl.BlockSpec(memory_space=pltpu.VMEM),
        scratch_shapes=[
            pltpu.SemaphoreType.DMA((sends,)),
            pltpu.SemaphoreType.DMA((2 * n,)),
        ],
        compiler_params=pltpu.CompilerParams(collective_id=collective_id, has_side_effects=True),
    )(x)


def _ring_kernel(n, chunks, keys_ref, weights_ref, stored_ref, terms_ref, own_ref, out_ref, partial_ref, recv_r, recv_l, acc_r, acc_l,
                 rs_sems, ag_sems):
    me = lax.axis_index("row")
    mine = lax.axis_index("col")
    right = lax.rem(me + 1, n)
    left = lax.rem(me + n - 1, n)
    steps_r = n // 2
    steps_l = n - 1 - steps_r
    block = partial_ref.shape[1]
    size = block // chunks
    half = n * chunks
    barrier = pltpu.get_barrier_semaphore()
    for peer in (left, right):
        pl.semaphore_signal(barrier, inc=1, device_id=(peer, mine), device_id_type=pl.DeviceIdType.MESH)
    pl.semaphore_wait(barrier, 2)

    def whiten(d):
        start = pl.multiple_of(d * block, block)
        partial_ref[d] = jnp.dot(keys_ref[pl.ds(start, block), :], weights_ref[...],
                                 preferred_element_type=jnp.float32)

    def intersect(b):
        terms_ref[b] = lax.dot_general(out_ref[b], stored_ref[...], (((1,), (1,)), ((), ())),
                                       preferred_element_type=jnp.float32)

    def send(src, dst, sems, k, peer):
        copy = pltpu.make_async_remote_copy(
            src_ref=src, dst_ref=dst, send_sem=sems.at[k], recv_sem=sems.at[k + 2 * half],
            device_id=(peer, mine), device_id_type=pl.DeviceIdType.MESH)
        copy.start()
        return copy

    sent = []
    got_r = {}
    got_l = {}
    for s in range(steps_r):
        d_r = lax.rem(me + steps_r - s, n)
        d_l = lax.rem(me + n - steps_l + s, n)
        whiten(d_r)
        if s < steps_l:
            whiten(d_l)
        for h in range(chunks):
            rows = pl.ds(h * size, size)
            if s == 0:
                src = partial_ref.at[d_r, rows]
            else:
                got_r[s - 1, h].wait_recv()
                acc_r[s - 1, rows] = recv_r[s - 1, rows] + partial_ref[d_r, rows]
                src = acc_r.at[s - 1, rows]
            got_r[s, h] = send(src, recv_r.at[s, rows], rs_sems, s * chunks + h, right)
            sent.append(got_r[s, h])
            if s < steps_l:
                if s == 0:
                    src = partial_ref.at[d_l, rows]
                else:
                    got_l[s - 1, h].wait_recv()
                    acc_l[s - 1, rows] = recv_l[s - 1, rows] + partial_ref[d_l, rows]
                    src = acc_l.at[s - 1, rows]
                got_l[s, h] = send(src, recv_l.at[s, rows], rs_sems, half + s * chunks + h, left)
                sent.append(got_l[s, h])
    whiten(me)
    for h in range(chunks):
        rows = pl.ds(h * size, size)
        got_r[steps_r - 1, h].wait_recv()
        got_l[steps_l - 1, h].wait_recv()
        total = partial_ref[me, rows] + recv_r[steps_r - 1, rows] + recv_l[steps_l - 1, rows]
        rounded = total.astype(out_ref.dtype)
        out_ref[me, rows] = rounded
        own_ref[rows] = rounded

    ag_r = {}
    ag_l = {}
    for t in range(steps_r):
        for h in range(chunks):
            rows = pl.ds(h * size, size)
            b_r = lax.rem(me + n - t, n)
            if t:
                ag_r[t - 1, h].wait_recv()
            ag_r[t, h] = send(out_ref.at[b_r, rows], out_ref.at[b_r, rows], ag_sems, t * chunks + h, right)
            sent.append(ag_r[t, h])
            if t < steps_l:
                b_l = lax.rem(me + t, n)
                if t:
                    ag_l[t - 1, h].wait_recv()
                ag_l[t, h] = send(out_ref.at[b_l, rows], out_ref.at[b_l, rows], ag_sems, half + t * chunks + h, left)
                sent.append(ag_l[t, h])
        intersect(lax.rem(me + n - t, n))
        if t and t < steps_l:
            intersect(lax.rem(me + t, n))
    for h in range(chunks):
        ag_r[steps_r - 1, h].wait_recv()
        ag_l[steps_l - 1, h].wait_recv()
    intersect(lax.rem(me + n - steps_r, n))
    intersect(lax.rem(me + steps_l, n))
    for c in sent:
        c.wait_send()


def row_ring(keys, weights, stored, n, collective_id, chunks=2):
    rows = keys.shape[0] // n
    width = weights.shape[1]
    slots = stored.shape[0]
    steps_r = n // 2
    steps_l = n - 1 - steps_r
    return pl.pallas_call(
        functools.partial(_ring_kernel, n, chunks),
        out_shape=(jax.ShapeDtypeStruct((n, rows, slots), jnp.float32),
                   jax.ShapeDtypeStruct((rows, width), jnp.bfloat16)),
        in_specs=[pl.BlockSpec(memory_space=pltpu.VMEM)] * 3,
        out_specs=(pl.BlockSpec(memory_space=pltpu.VMEM), pl.BlockSpec(memory_space=pltpu.VMEM)),
        scratch_shapes=[
            pltpu.VMEM((n, rows, width), jnp.bfloat16),
            pltpu.VMEM((n, rows, width), jnp.float32),
            pltpu.VMEM((steps_r, rows, width), jnp.float32),
            pltpu.VMEM((steps_l, rows, width), jnp.float32),
            pltpu.VMEM((steps_r - 1, rows, width), jnp.float32),
            pltpu.VMEM((steps_l - 1, rows, width), jnp.float32),
            pltpu.SemaphoreType.DMA((4 * n * chunks,)),
            pltpu.SemaphoreType.DMA((4 * n * chunks,)),
        ],
        compiler_params=pltpu.CompilerParams(collective_id=collective_id, has_side_effects=True),
    )(keys, weights, stored)


def shards(new_keys, precision, stored_keys, pair_batch, pair_count, batch_length, batch_slot):
    row_count = lax.axis_size("row")
    col_count = lax.axis_size("col")
    row_index = lax.axis_index("row")
    total_keys = new_keys.shape[0] * col_count
    block_keys = total_keys // row_count
    part_keys = block_keys // col_count
    local_batches, batch_keys, width = stored_keys.shape
    gathered = torus_gather(new_keys, col_count, 4, 0)
    terms, whitened = row_ring(gathered.reshape(total_keys, new_keys.shape[1]), precision,
                               stored_keys.reshape(local_batches * batch_keys, width), row_count, 3)
    terms = terms.reshape(col_count, block_keys // 2, local_batches * batch_keys)
    routed = scatter_route(terms, col_count, row_count, 1)
    table = routed.reshape(row_count, part_keys, local_batches, batch_keys).transpose(0, 2, 1, 3)
    table = table.reshape(row_count * local_batches, part_keys, batch_keys)
    listed = lax.dynamic_index_in_dim(pair_batch, row_index, 0, keepdims=False)
    count = lax.dynamic_index_in_dim(pair_count, row_index, 0, keepdims=False)
    places = jnp.arange(listed.shape[0], dtype=jnp.int32)
    batches = jnp.arange(batch_slot.shape[0], dtype=jnp.int32)
    hit = (listed[:, None] == batches[None, :]) & (places < count)[:, None]
    lengths = jnp.sum(jnp.where(hit, batch_length[None, :], 0), axis=1)
    choose = jnp.where(hit[:, :, None] & (batch_slot[None, :, None] == batches[None, None, :]), 1.0, 0.0)
    choose = jnp.sum(choose, axis=1)
    picked = jnp.einsum("ps,sk->pk", choose, table.reshape(table.shape[0], -1),
                        precision=lax.Precision.HIGHEST, preferred_element_type=jnp.float32)
    picked = picked.reshape(listed.shape[0], part_keys, batch_keys)
    columns = jnp.arange(batch_keys, dtype=jnp.int32)
    shares = jnp.where(columns[None, None, :] < lengths[:, None, None], picked, 0.0)
    return (whitened, shares[None])


def solution(mesh):
    placed = (P("col", "row"), P("row", "col"), P("row", None, "col"), P(), P(), P(), P())
    return jax.shard_map(
        shards,
        mesh=mesh,
        in_specs=placed,
        out_specs=(P("row", "col"), P("row", None, "col", None)),
        check_vma=False,
    )
```

```python
import functools

import jax
import jax.numpy as jnp
from jax import lax
from jax.experimental import pallas as pl
from jax.experimental.pallas import tpu as pltpu
from jax.sharding import PartitionSpec as P


def _exchange_kernel(axis, other, n, gather, x_ref, out_ref, send_sems, recv_sems):
    me = lax.axis_index(axis)
    mine = lax.axis_index(other)

    def at(peer):
        return (peer, mine) if axis == "row" else (mine, peer)

    barrier = pltpu.get_barrier_semaphore()
    for d in range(1, n):
        peer = lax.rem(me + d, n)
        pl.semaphore_signal(barrier, inc=1, device_id=at(peer), device_id_type=pl.DeviceIdType.MESH)
    pl.semaphore_wait(barrier, n - 1)
    copies = []
    for d in range(1, n):
        peer = lax.rem(me + d, n)
        src = x_ref if gather else x_ref.at[peer]
        copy = pltpu.make_async_remote_copy(
            src_ref=src, dst_ref=out_ref.at[me], send_sem=send_sems.at[d], recv_sem=recv_sems.at[d],
            device_id=at(peer), device_id_type=pl.DeviceIdType.MESH)
        copy.start()
        copies.append(copy)
    if gather:
        out_ref[me] = x_ref[...]
    else:
        out_ref[me] = x_ref[me]
    for d in range(1, n):
        copies[d - 1].wait_send()
        source = lax.rem(me + n - d, n)
        src = x_ref if gather else x_ref.at[source]
        incoming = pltpu.make_async_remote_copy(
            src_ref=src, dst_ref=out_ref.at[source], send_sem=send_sems.at[d], recv_sem=recv_sems.at[d],
            device_id=at(source), device_id_type=pl.DeviceIdType.MESH)
        incoming.wait_recv()


def exchange(x, axis, other, n, gather, collective_id):
    block = x.shape if gather else x.shape[1:]
    return pl.pallas_call(
        functools.partial(_exchange_kernel, axis, other, n, gather),
        out_shape=jax.ShapeDtypeStruct((n,) + tuple(block), x.dtype),
        in_specs=[pl.BlockSpec(memory_space=pltpu.VMEM)],
        out_specs=pl.BlockSpec(memory_space=pltpu.VMEM),
        scratch_shapes=[pltpu.SemaphoreType.DMA((n,)), pltpu.SemaphoreType.DMA((n,))],
        compiler_params=pltpu.CompilerParams(collective_id=collective_id, has_side_effects=True),
    )(x)


def _gather_kernel(n, x_ref, out_ref, send_sems, forward_sems, recv_sems):
    me = lax.axis_index("col")
    mine = lax.axis_index("row")
    core = lax.rem(me, 2)
    chip = me // 2
    chips = n // 2
    sibling = chip * 2 + 1 - core
    peers = [lax.rem(chip + d, chips) * 2 + core for d in range(1, chips)]
    barrier = pltpu.get_barrier_semaphore()
    for peer in peers + [sibling]:
        pl.semaphore_signal(barrier, inc=1, device_id=(mine, peer), device_id_type=pl.DeviceIdType.MESH)
    pl.semaphore_wait(barrier, chips)

    def copy(src, slot, sem, peer):
        return pltpu.make_async_remote_copy(
            src_ref=src, dst_ref=out_ref.at[slot], send_sem=sem, recv_sem=recv_sems.at[slot],
            device_id=(mine, peer), device_id_type=pl.DeviceIdType.MESH)

    sent = []
    for d, peer in enumerate(peers + [sibling]):
        c = copy(x_ref, me, send_sems.at[d], peer)
        c.start()
        sent.append(c)
    out_ref[me] = x_ref[...]
    for d, peer in enumerate(peers):
        copy(x_ref, peer, send_sems.at[d], peer).wait_recv()
        c = copy(out_ref.at[peer], peer, forward_sems.at[d], sibling)
        c.start()
        sent.append(c)
    copy(x_ref, sibling, send_sems.at[0], sibling).wait_recv()
    for d in range(1, chips):
        far = lax.rem(chip + d, chips) * 2 + 1 - core
        copy(x_ref, far, send_sems.at[0], sibling).wait_recv()
    for c in sent:
        c.wait_send()


def col_gather(x, n, collective_id):
    return pl.pallas_call(
        functools.partial(_gather_kernel, n),
        out_shape=jax.ShapeDtypeStruct((n,) + x.shape, x.dtype),
        in_specs=[pl.BlockSpec(memory_space=pltpu.VMEM)],
        out_specs=pl.BlockSpec(memory_space=pltpu.VMEM),
        scratch_shapes=[
            pltpu.SemaphoreType.DMA((n,)),
            pltpu.SemaphoreType.DMA((n,)),
            pltpu.SemaphoreType.DMA((n,)),
        ],
        compiler_params=pltpu.CompilerParams(collective_id=collective_id, has_side_effects=True),
    )(x)


def _scatter_kernel(n, x_ref, out_ref, half, recv, acc, send_sems, recv_sems):
    me = lax.axis_index("col")
    mine = lax.axis_index("row")
    core = lax.rem(me, 2)
    chip = me // 2
    chips = n // 2
    sibling = chip * 2 + 1 - core
    peers = [lax.rem(chip + d, chips) * 2 + core for d in range(1, chips)]
    barrier = pltpu.get_barrier_semaphore()
    for peer in peers + [sibling]:
        pl.semaphore_signal(barrier, inc=1, device_id=(mine, peer), device_id_type=pl.DeviceIdType.MESH)
    pl.semaphore_wait(barrier, chips)

    swap = pltpu.make_async_remote_copy(
        src_ref=x_ref.at[:, 1 - core], dst_ref=half, send_sem=send_sems.at[0], recv_sem=recv_sems.at[0],
        device_id=(mine, sibling), device_id_type=pl.DeviceIdType.MESH)
    swap.start()
    swap.wait_recv()
    acc[...] = x_ref[:, core] + half[...]
    sent = [swap]
    for d in range(1, chips):
        target = lax.rem(chip + d, chips)
        c = pltpu.make_async_remote_copy(
            src_ref=acc.at[target], dst_ref=recv.at[chip], send_sem=send_sems.at[d], recv_sem=recv_sems.at[d],
            device_id=(mine, target * 2 + core), device_id_type=pl.DeviceIdType.MESH)
        c.start()
        sent.append(c)
    total = acc[chip]
    for d in range(1, chips):
        source = lax.rem(chip + chips - d, chips)
        pltpu.make_async_remote_copy(
            src_ref=acc.at[source], dst_ref=recv.at[source], send_sem=send_sems.at[d], recv_sem=recv_sems.at[d],
            device_id=(mine, source * 2 + core), device_id_type=pl.DeviceIdType.MESH).wait_recv()
        total = total + recv[source]
    out_ref[...] = total
    for c in sent:
        c.wait_send()


def col_scatter(x, n, collective_id):
    chips = n // 2
    block = x.shape[1:]
    return pl.pallas_call(
        functools.partial(_scatter_kernel, n),
        out_shape=jax.ShapeDtypeStruct(block, x.dtype),
        in_specs=[pl.BlockSpec(memory_space=pltpu.VMEM)],
        out_specs=pl.BlockSpec(memory_space=pltpu.VMEM),
        scratch_shapes=[
            pltpu.VMEM((chips,) + block, x.dtype),
            pltpu.VMEM((chips,) + block, x.dtype),
            pltpu.VMEM((chips,) + block, x.dtype),
            pltpu.SemaphoreType.DMA((chips,)),
            pltpu.SemaphoreType.DMA((chips,)),
        ],
        compiler_params=pltpu.CompilerParams(collective_id=collective_id, has_side_effects=True),
    )(x.reshape((chips, 2) + block))


def _route_kernel(x_ref, out_ref, send_buf, send_sems, recv_sems):
    row = lax.axis_index("row")
    col = lax.axis_index("col")
    pairs = x_ref.shape[0] // 2
    rows = lax.axis_size("row")
    block = col // 2
    half = lax.rem(col, 2)
    base = pairs * half
    source_col = 2 * row + col // pairs
    mirrored = (row == block) & (col // pairs == half)

    barrier = pltpu.get_barrier_semaphore()
    for k in range(pairs):
        target = base + k

        @pl.when((block != row) | (target != col))
        def _():
            pl.semaphore_signal(barrier, inc=1, device_id=(block, target), device_id_type=pl.DeviceIdType.MESH)
    for r in range(rows):

        @pl.when((r != row) | (source_col != col))
        def _():
            pl.semaphore_signal(barrier, inc=1, device_id=(r, source_col), device_id_type=pl.DeviceIdType.MESH)

    @pl.when(mirrored)
    def _():
        pl.semaphore_wait(barrier, pairs + rows - 2)

    @pl.when(jnp.logical_not(mirrored))
    def _():
        pl.semaphore_wait(barrier, pairs + rows)

    for k in range(pairs):
        send_buf[k] = x_ref[2 * k:2 * k + 2, :]

    def copy(k, r, device):
        return pltpu.make_async_remote_copy(
            src_ref=send_buf.at[k], dst_ref=out_ref.at[r], send_sem=send_sems.at[k], recv_sem=recv_sems.at[r],
            device_id=device, device_id_type=pl.DeviceIdType.MESH)

    for k in range(pairs):
        target = base + k

        @pl.when((block != row) | (target != col))
        def _():
            copy(k, row, (block, target)).start()

        @pl.when((block == row) & (target == col))
        def _():
            out_ref[row] = send_buf[k]
    for r in range(rows):

        @pl.when((r != row) | (source_col != col))
        def _():
            copy(0, r, (r, source_col)).wait_recv()
    for k in range(pairs):
        target = base + k

        @pl.when((block != row) | (target != col))
        def _():
            copy(k, row, (block, target)).wait_send()


def route(x, rows, collective_id):
    pairs = x.shape[0] // 2
    return pl.pallas_call(
        _route_kernel,
        out_shape=jax.ShapeDtypeStruct((rows, 2, x.shape[1]), x.dtype),
        in_specs=[pl.BlockSpec(memory_space=pltpu.VMEM)],
        out_specs=pl.BlockSpec(memory_space=pltpu.VMEM),
        scratch_shapes=[
            pltpu.VMEM((pairs, 2, x.shape[1]), x.dtype),
            pltpu.SemaphoreType.DMA((pairs,)),
            pltpu.SemaphoreType.DMA((rows,)),
        ],
        compiler_params=pltpu.CompilerParams(collective_id=collective_id, has_side_effects=True),
    )(x)


def _scatter_route_kernel(n, x_ref, out_ref, half_ref, recv, acc, summed, send_buf, send_sems, recv_sems,
                          route_send, route_recv):
    me = lax.axis_index("col")
    row = lax.axis_index("row")
    rows = lax.axis_size("row")
    core = lax.rem(me, 2)
    chip = me // 2
    chips = n // 2
    pairs = summed.shape[0] // 2
    sibling = chip * 2 + 1 - core
    peers = [lax.rem(chip + d, chips) * 2 + core for d in range(1, chips)]
    block = me // 2
    base = pairs * core
    source_col = 2 * row + me // pairs
    mirrored = (row == block) & (me // pairs == core)

    barrier = pltpu.get_barrier_semaphore()
    for peer in peers + [sibling]:
        pl.semaphore_signal(barrier, inc=1, device_id=(row, peer), device_id_type=pl.DeviceIdType.MESH)
    for k in range(pairs):
        target = base + k

        @pl.when((block != row) | (target != me))
        def _():
            pl.semaphore_signal(barrier, inc=1, device_id=(block, target), device_id_type=pl.DeviceIdType.MESH)
    for r in range(rows):

        @pl.when((r != row) | (source_col != me))
        def _():
            pl.semaphore_signal(barrier, inc=1, device_id=(r, source_col), device_id_type=pl.DeviceIdType.MESH)

    @pl.when(mirrored)
    def _():
        pl.semaphore_wait(barrier, chips + pairs + rows - 2)

    @pl.when(jnp.logical_not(mirrored))
    def _():
        pl.semaphore_wait(barrier, chips + pairs + rows)

    swap = pltpu.make_async_remote_copy(
        src_ref=x_ref.at[:, 1 - core], dst_ref=half_ref, send_sem=send_sems.at[0], recv_sem=recv_sems.at[0],
        device_id=(row, sibling), device_id_type=pl.DeviceIdType.MESH)
    swap.start()
    swap.wait_recv()
    acc[...] = x_ref[:, core] + half_ref[...]
    sent = [swap]
    for d in range(1, chips):
        target = lax.rem(chip + d, chips)
        c = pltpu.make_async_remote_copy(
            src_ref=acc.at[target], dst_ref=recv.at[chip], send_sem=send_sems.at[d], recv_sem=recv_sems.at[d],
            device_id=(row, target * 2 + core), device_id_type=pl.DeviceIdType.MESH)
        c.start()
        sent.append(c)
    total = acc[chip]
    for d in range(1, chips):
        source = lax.rem(chip + chips - d, chips)
        pltpu.make_async_remote_copy(
            src_ref=acc.at[source], dst_ref=recv.at[source], send_sem=send_sems.at[d], recv_sem=recv_sems.at[d],
            device_id=(row, source * 2 + core), device_id_type=pl.DeviceIdType.MESH).wait_recv()
        total = total + recv[source]
    summed[...] = total
    for k in range(pairs):
        send_buf[k] = summed[2 * k:2 * k + 2, :]

    def copy(k, r, device):
        return pltpu.make_async_remote_copy(
            src_ref=send_buf.at[k], dst_ref=out_ref.at[r], send_sem=route_send.at[k], recv_sem=route_recv.at[r],
            device_id=device, device_id_type=pl.DeviceIdType.MESH)

    for k in range(pairs):
        target = base + k

        @pl.when((block != row) | (target != me))
        def _():
            copy(k, row, (block, target)).start()

        @pl.when((block == row) & (target == me))
        def _():
            out_ref[row] = send_buf[k]
    for r in range(rows):

        @pl.when((r != row) | (source_col != me))
        def _():
            copy(0, r, (r, source_col)).wait_recv()
    for k in range(pairs):
        target = base + k

        @pl.when((block != row) | (target != me))
        def _():
            copy(k, row, (block, target)).wait_send()
    for c in sent:
        c.wait_send()


def scatter_route(x, n, rows, collective_id):
    chips = n // 2
    block = x.shape[1:]
    pairs = block[0] // 2
    return pl.pallas_call(
        functools.partial(_scatter_route_kernel, n),
        out_shape=jax.ShapeDtypeStruct((rows, 2, block[1]), x.dtype),
        in_specs=[pl.BlockSpec(memory_space=pltpu.VMEM)],
        out_specs=pl.BlockSpec(memory_space=pltpu.VMEM),
        scratch_shapes=[
            pltpu.VMEM((chips,) + block, x.dtype),
            pltpu.VMEM((chips,) + block, x.dtype),
            pltpu.VMEM((chips,) + block, x.dtype),
            pltpu.VMEM(block, x.dtype),
            pltpu.VMEM((pairs, 2, block[1]), x.dtype),
            pltpu.SemaphoreType.DMA((chips,)),
            pltpu.SemaphoreType.DMA((chips,)),
            pltpu.SemaphoreType.DMA((pairs,)),
            pltpu.SemaphoreType.DMA((rows,)),
        ],
        compiler_params=pltpu.CompilerParams(collective_id=collective_id, has_side_effects=True),
    )(x.reshape((chips, 2) + block))


def _torus_gather_kernel(n, side, x_ref, out_ref, send_sems, recv_sems):
    me = lax.axis_index("col")
    mine = lax.axis_index("row")
    core = lax.rem(me, 2)
    chip = me // 2
    chips = n // 2
    across = lax.rem(chip, side)
    down = chip // side
    sibling = chip * 2 + 1 - core
    width = x_ref.shape[1] // 2
    x_peers = [(down * side + lax.rem(across + d, side)) * 2 + core for d in range(1, side)]
    y_peers = [(lax.rem(down + d, chips // side) * side + across) * 2 + core for d in range(1, chips // side)]
    barrier = pltpu.get_barrier_semaphore()
    for peer in x_peers + y_peers + [sibling]:
        pl.semaphore_signal(barrier, inc=1, device_id=(mine, peer), device_id_type=pl.DeviceIdType.MESH)
    pl.semaphore_wait(barrier, len(x_peers) + len(y_peers) + 1)

    count = [0]
    sent = []

    def push(slot, part, peer, src=None):
        cols = pl.ds(part * width, width)
        copy = pltpu.make_async_remote_copy(
            src_ref=out_ref.at[slot, :, cols] if src is None else src, dst_ref=out_ref.at[slot, :, cols],
            send_sem=send_sems.at[count[0]], recv_sem=recv_sems.at[slot * 2 + part],
            device_id=(mine, peer), device_id_type=pl.DeviceIdType.MESH)
        copy.start()
        count[0] += 1
        sent.append(copy)

    def arrived(slot, part):
        cols = pl.ds(part * width, width)
        pltpu.make_async_remote_copy(
            src_ref=out_ref.at[slot, :, cols], dst_ref=out_ref.at[slot, :, cols],
            send_sem=send_sems.at[0], recv_sem=recv_sems.at[slot * 2 + part],
            device_id=(mine, sibling), device_id_type=pl.DeviceIdType.MESH).wait_recv()

    out_ref[me] = x_ref[...]
    for part, first, second in ((0, x_peers, y_peers), (1, y_peers, x_peers)):
        for peer in first + second + [sibling]:
            push(me, part, peer, x_ref.at[:, pl.ds(part * width, width)])
    for part, first, second in ((0, x_peers, y_peers), (1, y_peers, x_peers)):
        for peer in first:
            arrived(peer, part)
            for other in second + [sibling]:
                push(peer, part, other)
    for part, first, second in ((0, x_peers, y_peers), (1, y_peers, x_peers)):
        for peer in second:
            for line in [peer] + [lax.rem(p + 2 * chips + peer - me, 2 * chips) for p in first]:
                arrived(line, part)
                push(line, part, sibling)
    for slot_chip in range(chips):
        for part in range(2):
            arrived(slot_chip * 2 + 1 - core, part)
    for c in sent:
        c.wait_send()


def torus_gather(x, n, side, collective_id):
    sends = 4 * n
    return pl.pallas_call(
        functools.partial(_torus_gather_kernel, n, side),
        out_shape=jax.ShapeDtypeStruct((n,) + x.shape, x.dtype),
        in_specs=[pl.BlockSpec(memory_space=pltpu.VMEM)],
        out_specs=pl.BlockSpec(memory_space=pltpu.VMEM),
        scratch_shapes=[
            pltpu.SemaphoreType.DMA((sends,)),
            pltpu.SemaphoreType.DMA((2 * n,)),
        ],
        compiler_params=pltpu.CompilerParams(collective_id=collective_id, has_side_effects=True),
    )(x)


def _ring_kernel(n, chunks, keys_ref, weights_ref, stored_ref, terms_ref, own_ref, out_ref, partial_ref, recv_r, recv_l, acc_r, acc_l,
                 rs_sems, ag_sems):
    me = lax.axis_index("row")
    mine = lax.axis_index("col")
    right = lax.rem(me + 1, n)
    left = lax.rem(me + n - 1, n)
    steps_r = n // 2
    steps_l = n - 1 - steps_r
    block = partial_ref.shape[1]
    size = block // chunks
    half = n * chunks
    barrier = pltpu.get_barrier_semaphore()
    for peer in (left, right):
        pl.semaphore_signal(barrier, inc=1, device_id=(peer, mine), device_id_type=pl.DeviceIdType.MESH)
    pl.semaphore_wait(barrier, 2)

    def whiten(d):
        start = pl.multiple_of(d * block, block)
        partial_ref[d] = jnp.dot(keys_ref[pl.ds(start, block), :], weights_ref[...],
                                 preferred_element_type=jnp.float32)

    def intersect(b):
        terms_ref[b] = lax.dot_general(out_ref[b], stored_ref[...], (((1,), (1,)), ((), ())),
                                       preferred_element_type=jnp.float32)

    def send(src, dst, sems, k, peer):
        copy = pltpu.make_async_remote_copy(
            src_ref=src, dst_ref=dst, send_sem=sems.at[k], recv_sem=sems.at[k + 2 * half],
            device_id=(peer, mine), device_id_type=pl.DeviceIdType.MESH)
        copy.start()
        return copy

    sent = []
    got_r = {}
    got_l = {}
    for s in range(steps_r):
        d_r = lax.rem(me + steps_r - s, n)
        d_l = lax.rem(me + n - steps_l + s, n)
        whiten(d_r)
        if s < steps_l:
            whiten(d_l)
        for h in range(chunks):
            rows = pl.ds(h * size, size)
            if s == 0:
                src = partial_ref.at[d_r, rows]
            else:
                got_r[s - 1, h].wait_recv()
                acc_r[s - 1, rows] = recv_r[s - 1, rows] + partial_ref[d_r, rows]
                src = acc_r.at[s - 1, rows]
            got_r[s, h] = send(src, recv_r.at[s, rows], rs_sems, s * chunks + h, right)
            sent.append(got_r[s, h])
            if s < steps_l:
                if s == 0:
                    src = partial_ref.at[d_l, rows]
                else:
                    got_l[s - 1, h].wait_recv()
                    acc_l[s - 1, rows] = recv_l[s - 1, rows] + partial_ref[d_l, rows]
                    src = acc_l.at[s - 1, rows]
                got_l[s, h] = send(src, recv_l.at[s, rows], rs_sems, half + s * chunks + h, left)
                sent.append(got_l[s, h])
    whiten(me)
    for h in range(chunks):
        rows = pl.ds(h * size, size)
        got_r[steps_r - 1, h].wait_recv()
        got_l[steps_l - 1, h].wait_recv()
        total = partial_ref[me, rows] + recv_r[steps_r - 1, rows] + recv_l[steps_l - 1, rows]
        out_ref[me, rows] = total.astype(out_ref.dtype)
        own_ref[rows] = total

    ag_r = {}
    ag_l = {}
    for t in range(steps_r):
        for h in range(chunks):
            rows = pl.ds(h * size, size)
            b_r = lax.rem(me + n - t, n)
            if t:
                ag_r[t - 1, h].wait_recv()
            ag_r[t, h] = send(out_ref.at[b_r, rows], out_ref.at[b_r, rows], ag_sems, t * chunks + h, right)
            sent.append(ag_r[t, h])
            if t < steps_l:
                b_l = lax.rem(me + t, n)
                if t:
                    ag_l[t - 1, h].wait_recv()
                ag_l[t, h] = send(out_ref.at[b_l, rows], out_ref.at[b_l, rows], ag_sems, half + t * chunks + h, left)
                sent.append(ag_l[t, h])
        intersect(lax.rem(me + n - t, n))
        if t and t < steps_l:
            intersect(lax.rem(me + t, n))
    for h in range(chunks):
        ag_r[steps_r - 1, h].wait_recv()
        ag_l[steps_l - 1, h].wait_recv()
    intersect(lax.rem(me + n - steps_r, n))
    intersect(lax.rem(me + steps_l, n))
    for c in sent:
        c.wait_send()


def row_ring(keys, weights, stored, n, collective_id, chunks=2):
    rows = keys.shape[0] // n
    width = weights.shape[1]
    slots = stored.shape[0]
    steps_r = n // 2
    steps_l = n - 1 - steps_r
    return pl.pallas_call(
        functools.partial(_ring_kernel, n, chunks),
        out_shape=(jax.ShapeDtypeStruct((n, rows, slots), jnp.float32),
                   jax.ShapeDtypeStruct((rows, width), jnp.float32)),
        in_specs=[pl.BlockSpec(memory_space=pltpu.VMEM)] * 3,
        out_specs=(pl.BlockSpec(memory_space=pltpu.VMEM), pl.BlockSpec(memory_space=pltpu.VMEM)),
        scratch_shapes=[
            pltpu.VMEM((n, rows, width), jnp.bfloat16),
            pltpu.VMEM((n, rows, width), jnp.float32),
            pltpu.VMEM((steps_r, rows, width), jnp.float32),
            pltpu.VMEM((steps_l, rows, width), jnp.float32),
            pltpu.VMEM((steps_r - 1, rows, width), jnp.float32),
            pltpu.VMEM((steps_l - 1, rows, width), jnp.float32),
            pltpu.SemaphoreType.DMA((4 * n * chunks,)),
            pltpu.SemaphoreType.DMA((4 * n * chunks,)),
        ],
        compiler_params=pltpu.CompilerParams(collective_id=collective_id, has_side_effects=True),
    )(keys, weights, stored)


def shards(new_keys, precision, stored_keys, pair_batch, pair_count, batch_length, batch_slot):
    row_count = lax.axis_size("row")
    col_count = lax.axis_size("col")
    row_index = lax.axis_index("row")
    total_keys = new_keys.shape[0] * col_count
    block_keys = total_keys // row_count
    part_keys = block_keys // col_count
    local_batches, batch_keys, width = stored_keys.shape
    gathered = torus_gather(new_keys, col_count, 4, 0)
    terms, whitened = row_ring(gathered.reshape(total_keys, new_keys.shape[1]), precision,
                               stored_keys.reshape(local_batches * batch_keys, width), row_count, 3)
    whitened = whitened.astype(jnp.bfloat16)
    terms = terms.reshape(col_count, block_keys // 2, local_batches * batch_keys)
    routed = scatter_route(terms, col_count, row_count, 1)
    table = routed.reshape(row_count, part_keys, local_batches, batch_keys).transpose(0, 2, 1, 3)
    table = table.reshape(row_count * local_batches, part_keys, batch_keys)
    listed = lax.dynamic_index_in_dim(pair_batch, row_index, 0, keepdims=False)
    count = lax.dynamic_index_in_dim(pair_count, row_index, 0, keepdims=False)
    places = jnp.arange(listed.shape[0], dtype=jnp.int32)
    batches = jnp.arange(batch_slot.shape[0], dtype=jnp.int32)
    hit = (listed[:, None] == batches[None, :]) & (places < count)[:, None]
    lengths = jnp.sum(jnp.where(hit, batch_length[None, :], 0), axis=1)
    choose = jnp.where(hit[:, :, None] & (batch_slot[None, :, None] == batches[None, None, :]), 1.0, 0.0)
    choose = jnp.sum(choose, axis=1)
    picked = jnp.einsum("ps,sik->pik", choose, table,
                        precision=lax.Precision.HIGHEST, preferred_element_type=jnp.float32)
    columns = jnp.arange(batch_keys, dtype=jnp.int32)
    shares = jnp.where(columns[None, None, :] < lengths[:, None, None], picked, 0.0)
    return (whitened, shares[None])


def solution(mesh):
    placed = (P("col", "row"), P("row", "col"), P("row", None, "col"), P(), P(), P(), P())
    return jax.shard_map(
        shards,
        mesh=mesh,
        in_specs=placed,
        out_specs=(P("row", "col"), P("row", None, "col", None)),
        check_vma=False,
    )
```

```python
import functools

import jax
import jax.numpy as jnp
from jax import lax
from jax.experimental import pallas as pl
from jax.experimental.pallas import tpu as pltpu
from jax.sharding import PartitionSpec as P


def _exchange_kernel(axis, other, n, gather, x_ref, out_ref, send_sems, recv_sems):
    me = lax.axis_index(axis)
    mine = lax.axis_index(other)

    def at(peer):
        return (peer, mine) if axis == "row" else (mine, peer)

    barrier = pltpu.get_barrier_semaphore()
    for d in range(1, n):
        peer = lax.rem(me + d, n)
        pl.semaphore_signal(barrier, inc=1, device_id=at(peer), device_id_type=pl.DeviceIdType.MESH)
    pl.semaphore_wait(barrier, n - 1)
    copies = []
    for d in range(1, n):
        peer = lax.rem(me + d, n)
        src = x_ref if gather else x_ref.at[peer]
        copy = pltpu.make_async_remote_copy(
            src_ref=src, dst_ref=out_ref.at[me], send_sem=send_sems.at[d], recv_sem=recv_sems.at[d],
            device_id=at(peer), device_id_type=pl.DeviceIdType.MESH)
        copy.start()
        copies.append(copy)
    if gather:
        out_ref[me] = x_ref[...]
    else:
        out_ref[me] = x_ref[me]
    for d in range(1, n):
        copies[d - 1].wait_send()
        source = lax.rem(me + n - d, n)
        src = x_ref if gather else x_ref.at[source]
        incoming = pltpu.make_async_remote_copy(
            src_ref=src, dst_ref=out_ref.at[source], send_sem=send_sems.at[d], recv_sem=recv_sems.at[d],
            device_id=at(source), device_id_type=pl.DeviceIdType.MESH)
        incoming.wait_recv()


def exchange(x, axis, other, n, gather, collective_id):
    block = x.shape if gather else x.shape[1:]
    return pl.pallas_call(
        functools.partial(_exchange_kernel, axis, other, n, gather),
        out_shape=jax.ShapeDtypeStruct((n,) + tuple(block), x.dtype),
        in_specs=[pl.BlockSpec(memory_space=pltpu.VMEM)],
        out_specs=pl.BlockSpec(memory_space=pltpu.VMEM),
        scratch_shapes=[pltpu.SemaphoreType.DMA((n,)), pltpu.SemaphoreType.DMA((n,))],
        compiler_params=pltpu.CompilerParams(collective_id=collective_id, has_side_effects=True),
    )(x)


def _gather_kernel(n, x_ref, out_ref, send_sems, forward_sems, recv_sems):
    me = lax.axis_index("col")
    mine = lax.axis_index("row")
    core = lax.rem(me, 2)
    chip = me // 2
    chips = n // 2
    sibling = chip * 2 + 1 - core
    peers = [lax.rem(chip + d, chips) * 2 + core for d in range(1, chips)]
    barrier = pltpu.get_barrier_semaphore()
    for peer in peers + [sibling]:
        pl.semaphore_signal(barrier, inc=1, device_id=(mine, peer), device_id_type=pl.DeviceIdType.MESH)
    pl.semaphore_wait(barrier, chips)

    def copy(src, slot, sem, peer):
        return pltpu.make_async_remote_copy(
            src_ref=src, dst_ref=out_ref.at[slot], send_sem=sem, recv_sem=recv_sems.at[slot],
            device_id=(mine, peer), device_id_type=pl.DeviceIdType.MESH)

    sent = []
    for d, peer in enumerate(peers + [sibling]):
        c = copy(x_ref, me, send_sems.at[d], peer)
        c.start()
        sent.append(c)
    out_ref[me] = x_ref[...]
    for d, peer in enumerate(peers):
        copy(x_ref, peer, send_sems.at[d], peer).wait_recv()
        c = copy(out_ref.at[peer], peer, forward_sems.at[d], sibling)
        c.start()
        sent.append(c)
    copy(x_ref, sibling, send_sems.at[0], sibling).wait_recv()
    for d in range(1, chips):
        far = lax.rem(chip + d, chips) * 2 + 1 - core
        copy(x_ref, far, send_sems.at[0], sibling).wait_recv()
    for c in sent:
        c.wait_send()


def col_gather(x, n, collective_id):
    return pl.pallas_call(
        functools.partial(_gather_kernel, n),
        out_shape=jax.ShapeDtypeStruct((n,) + x.shape, x.dtype),
        in_specs=[pl.BlockSpec(memory_space=pltpu.VMEM)],
        out_specs=pl.BlockSpec(memory_space=pltpu.VMEM),
        scratch_shapes=[
            pltpu.SemaphoreType.DMA((n,)),
            pltpu.SemaphoreType.DMA((n,)),
            pltpu.SemaphoreType.DMA((n,)),
        ],
        compiler_params=pltpu.CompilerParams(collective_id=collective_id, has_side_effects=True),
    )(x)


def _scatter_kernel(n, x_ref, out_ref, half, recv, acc, send_sems, recv_sems):
    me = lax.axis_index("col")
    mine = lax.axis_index("row")
    core = lax.rem(me, 2)
    chip = me // 2
    chips = n // 2
    sibling = chip * 2 + 1 - core
    peers = [lax.rem(chip + d, chips) * 2 + core for d in range(1, chips)]
    barrier = pltpu.get_barrier_semaphore()
    for peer in peers + [sibling]:
        pl.semaphore_signal(barrier, inc=1, device_id=(mine, peer), device_id_type=pl.DeviceIdType.MESH)
    pl.semaphore_wait(barrier, chips)

    swap = pltpu.make_async_remote_copy(
        src_ref=x_ref.at[:, 1 - core], dst_ref=half, send_sem=send_sems.at[0], recv_sem=recv_sems.at[0],
        device_id=(mine, sibling), device_id_type=pl.DeviceIdType.MESH)
    swap.start()
    swap.wait_recv()
    acc[...] = x_ref[:, core] + half[...]
    sent = [swap]
    for d in range(1, chips):
        target = lax.rem(chip + d, chips)
        c = pltpu.make_async_remote_copy(
            src_ref=acc.at[target], dst_ref=recv.at[chip], send_sem=send_sems.at[d], recv_sem=recv_sems.at[d],
            device_id=(mine, target * 2 + core), device_id_type=pl.DeviceIdType.MESH)
        c.start()
        sent.append(c)
    swap(chip).wait_recv()
    total = x_ref[chip, core] + half_ref[chip]
    for d in range(1, chips):
        source = lax.rem(chip + chips - d, chips)
        pltpu.make_async_remote_copy(
            src_ref=acc.at[source], dst_ref=recv.at[source], send_sem=send_sems.at[d], recv_sem=recv_sems.at[d],
            device_id=(mine, source * 2 + core), device_id_type=pl.DeviceIdType.MESH).wait_recv()
        total = total + recv[source]
    out_ref[...] = total
    for c in sent:
        c.wait_send()


def col_scatter(x, n, collective_id):
    chips = n // 2
    block = x.shape[1:]
    return pl.pallas_call(
        functools.partial(_scatter_kernel, n),
        out_shape=jax.ShapeDtypeStruct(block, x.dtype),
        in_specs=[pl.BlockSpec(memory_space=pltpu.VMEM)],
        out_specs=pl.BlockSpec(memory_space=pltpu.VMEM),
        scratch_shapes=[
            pltpu.VMEM((chips,) + block, x.dtype),
            pltpu.VMEM((chips,) + block, x.dtype),
            pltpu.VMEM((chips,) + block, x.dtype),
            pltpu.SemaphoreType.DMA((chips,)),
            pltpu.SemaphoreType.DMA((chips,)),
        ],
        compiler_params=pltpu.CompilerParams(collective_id=collective_id, has_side_effects=True),
    )(x.reshape((chips, 2) + block))


def _route_kernel(x_ref, out_ref, send_buf, send_sems, recv_sems):
    row = lax.axis_index("row")
    col = lax.axis_index("col")
    pairs = x_ref.shape[0] // 2
    rows = lax.axis_size("row")
    block = col // 2
    half = lax.rem(col, 2)
    base = pairs * half
    source_col = 2 * row + col // pairs
    mirrored = (row == block) & (col // pairs == half)

    barrier = pltpu.get_barrier_semaphore()
    for k in range(pairs):
        target = base + k

        @pl.when((block != row) | (target != col))
        def _():
            pl.semaphore_signal(barrier, inc=1, device_id=(block, target), device_id_type=pl.DeviceIdType.MESH)
    for r in range(rows):

        @pl.when((r != row) | (source_col != col))
        def _():
            pl.semaphore_signal(barrier, inc=1, device_id=(r, source_col), device_id_type=pl.DeviceIdType.MESH)

    @pl.when(mirrored)
    def _():
        pl.semaphore_wait(barrier, pairs + rows - 2)

    @pl.when(jnp.logical_not(mirrored))
    def _():
        pl.semaphore_wait(barrier, pairs + rows)

    for k in range(pairs):
        send_buf[k] = x_ref[2 * k:2 * k + 2, :]

    def copy(k, r, device):
        return pltpu.make_async_remote_copy(
            src_ref=send_buf.at[k], dst_ref=out_ref.at[r], send_sem=send_sems.at[k], recv_sem=recv_sems.at[r],
            device_id=device, device_id_type=pl.DeviceIdType.MESH)

    for k in range(pairs):
        target = base + k

        @pl.when((block != row) | (target != col))
        def _():
            copy(k, row, (block, target)).start()

        @pl.when((block == row) & (target == col))
        def _():
            out_ref[row] = send_buf[k]
    for r in range(rows):

        @pl.when((r != row) | (source_col != col))
        def _():
            copy(0, r, (r, source_col)).wait_recv()
    for k in range(pairs):
        target = base + k

        @pl.when((block != row) | (target != col))
        def _():
            copy(k, row, (block, target)).wait_send()


def route(x, rows, collective_id):
    pairs = x.shape[0] // 2
    return pl.pallas_call(
        _route_kernel,
        out_shape=jax.ShapeDtypeStruct((rows, 2, x.shape[1]), x.dtype),
        in_specs=[pl.BlockSpec(memory_space=pltpu.VMEM)],
        out_specs=pl.BlockSpec(memory_space=pltpu.VMEM),
        scratch_shapes=[
            pltpu.VMEM((pairs, 2, x.shape[1]), x.dtype),
            pltpu.SemaphoreType.DMA((pairs,)),
            pltpu.SemaphoreType.DMA((rows,)),
        ],
        compiler_params=pltpu.CompilerParams(collective_id=collective_id, has_side_effects=True),
    )(x)


def _scatter_route_kernel(n, x_ref, out_ref, half_ref, recv, acc, summed, send_buf, send_sems, recv_sems,
                          route_send, route_recv, swap_send, swap_recv):
    me = lax.axis_index("col")
    row = lax.axis_index("row")
    rows = lax.axis_size("row")
    core = lax.rem(me, 2)
    chip = me // 2
    chips = n // 2
    pairs = summed.shape[0] // 2
    sibling = chip * 2 + 1 - core
    peers = [lax.rem(chip + d, chips) * 2 + core for d in range(1, chips)]
    block = me // 2
    base = pairs * core
    source_col = 2 * row + me // pairs
    mirrored = (row == block) & (me // pairs == core)

    barrier = pltpu.get_barrier_semaphore()
    for peer in peers + [sibling]:
        pl.semaphore_signal(barrier, inc=1, device_id=(row, peer), device_id_type=pl.DeviceIdType.MESH)
    for k in range(pairs):
        target = base + k

        @pl.when((block != row) | (target != me))
        def _():
            pl.semaphore_signal(barrier, inc=1, device_id=(block, target), device_id_type=pl.DeviceIdType.MESH)
    for r in range(rows):

        @pl.when((r != row) | (source_col != me))
        def _():
            pl.semaphore_signal(barrier, inc=1, device_id=(r, source_col), device_id_type=pl.DeviceIdType.MESH)

    @pl.when(mirrored)
    def _():
        pl.semaphore_wait(barrier, chips + pairs + rows - 2)

    @pl.when(jnp.logical_not(mirrored))
    def _():
        pl.semaphore_wait(barrier, chips + pairs + rows)

    def swap(k):
        return pltpu.make_async_remote_copy(
            src_ref=x_ref.at[k, 1 - core], dst_ref=half_ref.at[k], send_sem=swap_send.at[k], recv_sem=swap_recv.at[k],
            device_id=(row, sibling), device_id_type=pl.DeviceIdType.MESH)

    sent = []
    for d in list(range(1, chips)) + [0]:
        c = swap(lax.rem(chip + d, chips))
        c.start()
        sent.append(c)
    for d in range(1, chips):
        target = lax.rem(chip + d, chips)
        swap(target).wait_recv()
        acc[target] = x_ref[target, core] + half_ref[target]
        c = pltpu.make_async_remote_copy(
            src_ref=acc.at[target], dst_ref=recv.at[chip], send_sem=send_sems.at[d], recv_sem=recv_sems.at[d],
            device_id=(row, target * 2 + core), device_id_type=pl.DeviceIdType.MESH)
        c.start()
        sent.append(c)
    swap(chip).wait_recv()
    total = x_ref[chip, core] + half_ref[chip]
    for d in range(1, chips):
        source = lax.rem(chip + chips - d, chips)
        pltpu.make_async_remote_copy(
            src_ref=acc.at[source], dst_ref=recv.at[source], send_sem=send_sems.at[d], recv_sem=recv_sems.at[d],
            device_id=(row, source * 2 + core), device_id_type=pl.DeviceIdType.MESH).wait_recv()
        total = total + recv[source]
    summed[...] = total
    for k in range(pairs):
        send_buf[k] = summed[2 * k:2 * k + 2, :]

    def copy(k, r, device):
        return pltpu.make_async_remote_copy(
            src_ref=send_buf.at[k], dst_ref=out_ref.at[r], send_sem=route_send.at[k], recv_sem=route_recv.at[r],
            device_id=device, device_id_type=pl.DeviceIdType.MESH)

    for k in range(pairs):
        target = base + k

        @pl.when((block != row) | (target != me))
        def _():
            copy(k, row, (block, target)).start()

        @pl.when((block == row) & (target == me))
        def _():
            out_ref[row] = send_buf[k]
    for r in range(rows):

        @pl.when((r != row) | (source_col != me))
        def _():
            copy(0, r, (r, source_col)).wait_recv()
    for k in range(pairs):
        target = base + k

        @pl.when((block != row) | (target != me))
        def _():
            copy(k, row, (block, target)).wait_send()
    for c in sent:
        c.wait_send()


def scatter_route(x, n, rows, collective_id):
    chips = n // 2
    block = x.shape[1:]
    pairs = block[0] // 2
    return pl.pallas_call(
        functools.partial(_scatter_route_kernel, n),
        out_shape=jax.ShapeDtypeStruct((rows, 2, block[1]), x.dtype),
        in_specs=[pl.BlockSpec(memory_space=pltpu.VMEM)],
        out_specs=pl.BlockSpec(memory_space=pltpu.VMEM),
        scratch_shapes=[
            pltpu.VMEM((chips,) + block, x.dtype),
            pltpu.VMEM((chips,) + block, x.dtype),
            pltpu.VMEM((chips,) + block, x.dtype),
            pltpu.VMEM(block, x.dtype),
            pltpu.VMEM((pairs, 2, block[1]), x.dtype),
            pltpu.SemaphoreType.DMA((chips,)),
            pltpu.SemaphoreType.DMA((chips,)),
            pltpu.SemaphoreType.DMA((pairs,)),
            pltpu.SemaphoreType.DMA((rows,)),
            pltpu.SemaphoreType.DMA((chips,)),
            pltpu.SemaphoreType.DMA((chips,)),
        ],
        compiler_params=pltpu.CompilerParams(collective_id=collective_id, has_side_effects=True),
    )(x.reshape((chips, 2) + block))


def _torus_gather_kernel(n, side, x_ref, out_ref, send_sems, recv_sems):
    me = lax.axis_index("col")
    mine = lax.axis_index("row")
    core = lax.rem(me, 2)
    chip = me // 2
    chips = n // 2
    across = lax.rem(chip, side)
    down = chip // side
    sibling = chip * 2 + 1 - core
    width = x_ref.shape[1] // 2
    x_peers = [(down * side + lax.rem(across + d, side)) * 2 + core for d in range(1, side)]
    y_peers = [(lax.rem(down + d, chips // side) * side + across) * 2 + core for d in range(1, chips // side)]
    barrier = pltpu.get_barrier_semaphore()
    for peer in x_peers + y_peers + [sibling]:
        pl.semaphore_signal(barrier, inc=1, device_id=(mine, peer), device_id_type=pl.DeviceIdType.MESH)
    pl.semaphore_wait(barrier, len(x_peers) + len(y_peers) + 1)

    count = [0]
    sent = []

    def push(slot, part, peer, src=None):
        cols = pl.ds(part * width, width)
        copy = pltpu.make_async_remote_copy(
            src_ref=out_ref.at[slot, :, cols] if src is None else src, dst_ref=out_ref.at[slot, :, cols],
            send_sem=send_sems.at[count[0]], recv_sem=recv_sems.at[slot * 2 + part],
            device_id=(mine, peer), device_id_type=pl.DeviceIdType.MESH)
        copy.start()
        count[0] += 1
        sent.append(copy)

    def arrived(slot, part):
        cols = pl.ds(part * width, width)
        pltpu.make_async_remote_copy(
            src_ref=out_ref.at[slot, :, cols], dst_ref=out_ref.at[slot, :, cols],
            send_sem=send_sems.at[0], recv_sem=recv_sems.at[slot * 2 + part],
            device_id=(mine, sibling), device_id_type=pl.DeviceIdType.MESH).wait_recv()

    out_ref[me] = x_ref[...]
    for part, first, second in ((0, x_peers, y_peers), (1, y_peers, x_peers)):
        for peer in first + second + [sibling]:
            push(me, part, peer, x_ref.at[:, pl.ds(part * width, width)])
    for part, first, second in ((0, x_peers, y_peers), (1, y_peers, x_peers)):
        for peer in first:
            arrived(peer, part)
            for other in second + [sibling]:
                push(peer, part, other)
    for part, first, second in ((0, x_peers, y_peers), (1, y_peers, x_peers)):
        for peer in second:
            for line in [peer] + [lax.rem(p + 2 * chips + peer - me, 2 * chips) for p in first]:
                arrived(line, part)
                push(line, part, sibling)
    for slot_chip in range(chips):
        for part in range(2):
            arrived(slot_chip * 2 + 1 - core, part)
    for c in sent:
        c.wait_send()


def torus_gather(x, n, side, collective_id):
    sends = 4 * n
    return pl.pallas_call(
        functools.partial(_torus_gather_kernel, n, side),
        out_shape=jax.ShapeDtypeStruct((n,) + x.shape, x.dtype),
        in_specs=[pl.BlockSpec(memory_space=pltpu.VMEM)],
        out_specs=pl.BlockSpec(memory_space=pltpu.VMEM),
        scratch_shapes=[
            pltpu.SemaphoreType.DMA((sends,)),
            pltpu.SemaphoreType.DMA((2 * n,)),
        ],
        compiler_params=pltpu.CompilerParams(collective_id=collective_id, has_side_effects=True),
    )(x)


def _ring_kernel(n, chunks, keys_ref, weights_ref, stored_ref, terms_ref, own_ref, out_ref, partial_ref, recv_r, recv_l, acc_r, acc_l,
                 rs_sems, ag_sems):
    me = lax.axis_index("row")
    mine = lax.axis_index("col")
    right = lax.rem(me + 1, n)
    left = lax.rem(me + n - 1, n)
    steps_r = n // 2
    steps_l = n - 1 - steps_r
    block = partial_ref.shape[1]
    size = block // chunks
    half = n * chunks
    barrier = pltpu.get_barrier_semaphore()
    for peer in (left, right):
        pl.semaphore_signal(barrier, inc=1, device_id=(peer, mine), device_id_type=pl.DeviceIdType.MESH)
    pl.semaphore_wait(barrier, 2)

    def whiten(d):
        start = pl.multiple_of(d * block, block)
        partial_ref[d] = jnp.dot(keys_ref[pl.ds(start, block), :], weights_ref[...],
                                 preferred_element_type=jnp.float32)

    def intersect(b):
        terms_ref[b] = lax.dot_general(out_ref[b], stored_ref[...], (((1,), (1,)), ((), ())),
                                       preferred_element_type=jnp.float32)

    def send(src, dst, sems, k, peer):
        copy = pltpu.make_async_remote_copy(
            src_ref=src, dst_ref=dst, send_sem=sems.at[k], recv_sem=sems.at[k + 2 * half],
            device_id=(peer, mine), device_id_type=pl.DeviceIdType.MESH)
        copy.start()
        return copy

    sent = []
    got_r = {}
    got_l = {}
    for s in range(steps_r):
        d_r = lax.rem(me + steps_r - s, n)
        d_l = lax.rem(me + n - steps_l + s, n)
        whiten(d_r)
        if s < steps_l:
            whiten(d_l)
        for h in range(chunks):
            rows = pl.ds(h * size, size)
            if s == 0:
                src = partial_ref.at[d_r, rows]
            else:
                got_r[s - 1, h].wait_recv()
                acc_r[s - 1, rows] = recv_r[s - 1, rows] + partial_ref[d_r, rows]
                src = acc_r.at[s - 1, rows]
            got_r[s, h] = send(src, recv_r.at[s, rows], rs_sems, s * chunks + h, right)
            sent.append(got_r[s, h])
            if s < steps_l:
                if s == 0:
                    src = partial_ref.at[d_l, rows]
                else:
                    got_l[s - 1, h].wait_recv()
                    acc_l[s - 1, rows] = recv_l[s - 1, rows] + partial_ref[d_l, rows]
                    src = acc_l.at[s - 1, rows]
                got_l[s, h] = send(src, recv_l.at[s, rows], rs_sems, half + s * chunks + h, left)
                sent.append(got_l[s, h])
    whiten(me)
    for h in range(chunks):
        rows = pl.ds(h * size, size)
        got_r[steps_r - 1, h].wait_recv()
        got_l[steps_l - 1, h].wait_recv()
        total = partial_ref[me, rows] + recv_r[steps_r - 1, rows] + recv_l[steps_l - 1, rows]
        rounded = total.astype(out_ref.dtype)
        out_ref[me, rows] = rounded
        own_ref[rows] = rounded

    ag_r = {}
    ag_l = {}
    for t in range(steps_r):
        for h in range(chunks):
            rows = pl.ds(h * size, size)
            b_r = lax.rem(me + n - t, n)
            if t:
                ag_r[t - 1, h].wait_recv()
            ag_r[t, h] = send(out_ref.at[b_r, rows], out_ref.at[b_r, rows], ag_sems, t * chunks + h, right)
            sent.append(ag_r[t, h])
            if t < steps_l:
                b_l = lax.rem(me + t, n)
                if t:
                    ag_l[t - 1, h].wait_recv()
                ag_l[t, h] = send(out_ref.at[b_l, rows], out_ref.at[b_l, rows], ag_sems, half + t * chunks + h, left)
                sent.append(ag_l[t, h])
        intersect(lax.rem(me + n - t, n))
        if t and t < steps_l:
            intersect(lax.rem(me + t, n))
    for h in range(chunks):
        ag_r[steps_r - 1, h].wait_recv()
        ag_l[steps_l - 1, h].wait_recv()
    intersect(lax.rem(me + n - steps_r, n))
    intersect(lax.rem(me + steps_l, n))
    for c in sent:
        c.wait_send()


def row_ring(keys, weights, stored, n, collective_id, chunks=2):
    rows = keys.shape[0] // n
    width = weights.shape[1]
    slots = stored.shape[0]
    steps_r = n // 2
    steps_l = n - 1 - steps_r
    return pl.pallas_call(
        functools.partial(_ring_kernel, n, chunks),
        out_shape=(jax.ShapeDtypeStruct((n, rows, slots), jnp.float32),
                   jax.ShapeDtypeStruct((rows, width), jnp.bfloat16)),
        in_specs=[pl.BlockSpec(memory_space=pltpu.VMEM)] * 3,
        out_specs=(pl.BlockSpec(memory_space=pltpu.VMEM), pl.BlockSpec(memory_space=pltpu.VMEM)),
        scratch_shapes=[
            pltpu.VMEM((n, rows, width), jnp.bfloat16),
            pltpu.VMEM((n, rows, width), jnp.float32),
            pltpu.VMEM((steps_r, rows, width), jnp.float32),
            pltpu.VMEM((steps_l, rows, width), jnp.float32),
            pltpu.VMEM((steps_r - 1, rows, width), jnp.float32),
            pltpu.VMEM((steps_l - 1, rows, width), jnp.float32),
            pltpu.SemaphoreType.DMA((4 * n * chunks,)),
            pltpu.SemaphoreType.DMA((4 * n * chunks,)),
        ],
        compiler_params=pltpu.CompilerParams(collective_id=collective_id, has_side_effects=True),
    )(keys, weights, stored)


def shards(new_keys, precision, stored_keys, pair_batch, pair_count, batch_length, batch_slot):
    row_count = lax.axis_size("row")
    col_count = lax.axis_size("col")
    row_index = lax.axis_index("row")
    total_keys = new_keys.shape[0] * col_count
    block_keys = total_keys // row_count
    part_keys = block_keys // col_count
    local_batches, batch_keys, width = stored_keys.shape
    gathered = torus_gather(new_keys, col_count, 4, 0)
    terms, whitened = row_ring(gathered.reshape(total_keys, new_keys.shape[1]), precision,
                               stored_keys.reshape(local_batches * batch_keys, width), row_count, 3)
    terms = terms.reshape(col_count, block_keys // 2, local_batches * batch_keys)
    routed = scatter_route(terms, col_count, row_count, 1)
    table = routed.reshape(row_count, part_keys, local_batches, batch_keys).transpose(0, 2, 1, 3)
    table = table.reshape(row_count * local_batches, part_keys, batch_keys)
    listed = lax.dynamic_index_in_dim(pair_batch, row_index, 0, keepdims=False)
    count = lax.dynamic_index_in_dim(pair_count, row_index, 0, keepdims=False)
    places = jnp.arange(listed.shape[0], dtype=jnp.int32)
    batches = jnp.arange(batch_slot.shape[0], dtype=jnp.int32)
    hit = (listed[:, None] == batches[None, :]) & (places < count)[:, None]
    lengths = jnp.sum(jnp.where(hit, batch_length[None, :], 0), axis=1)
    choose = jnp.where(hit[:, :, None] & (batch_slot[None, :, None] == batches[None, None, :]), 1.0, 0.0)
    choose = jnp.sum(choose, axis=1)
    picked = jnp.einsum("ps,sk->pk", choose, table.reshape(table.shape[0], -1),
                        precision=lax.Precision.HIGHEST, preferred_element_type=jnp.float32)
    picked = picked.reshape(listed.shape[0], part_keys, batch_keys)
    columns = jnp.arange(batch_keys, dtype=jnp.int32)
    shares = jnp.where(columns[None, None, :] < lengths[:, None, None], picked, 0.0)
    return (whitened, shares[None])


def solution(mesh):
    placed = (P("col", "row"), P("row", "col"), P("row", None, "col"), P(), P(), P(), P())
    return jax.shard_map(
        shards,
        mesh=mesh,
        in_specs=placed,
        out_specs=(P("row", "col"), P("row", None, "col", None)),
        check_vma=False,
    )
```
